32 devices in a mesh: win: 8 (over y, x, core), seq: 4 (over z).
Axes of the slice: x: 2, y: 2, z: 4, core: 2. Of those that a mesh axis runs over, the one named last changes fastest.
Arguments:
- tokens: bfloat16 [16, 512, 768], P('win', 'seq'), may hold values from -50 to 50, as said below
- cotangent: bfloat16 [16, 512, 768], P('win', 'seq'), may hold values from -6 to 6
- noise_times: float32 [16], P('win'), may hold values from 0 to 1
- cath_ids: int32 [16], P('win'), may hold values from 0 to 3
- chain_start: int32 [16], P('win'), may hold values from 128 to 512
- distance_bins: int32 [16, 512, 512], P('win', 'seq'), may hold values from 0 to 63
- class_table: bfloat16 [4, 768], replicated, may hold values from -6 to 6
- ada_weight: bfloat16 [768, 4608], replicated, may hold values from -0.21875 to 0.21875
- qkv_weight: bfloat16 [768, 2304], replicated, may hold values from -0.21875 to 0.21875
- out_weight: bfloat16 [768, 768], replicated, may hold values from -0.875 to 0.875
- pair_table: bfloat16 [128, 256], replicated, may hold values from -6 to 6
- pair_weight: bfloat16 [256, 12], replicated, may hold values from -0.375 to 0.375
- gate_weight: bfloat16 [768, 3072], replicated, may hold values from -0.21875 to 0.21875
- up_weight: bfloat16 [768, 3072], replicated, may hold values from -0.21875 to 0.21875
- down_weight: bfloat16 [3072, 768], replicated, may hold values from -0.21875 to 0.21875
Outputs:
- layer_out: bfloat16 [16, 512, 768], P('win', 'seq')
- grad_tokens: bfloat16 [16, 512, 768], P('win', 'seq')
- grad_class: float32 [3072], P(('win', 'seq'))
- grad_ada: float32 [3538944], P(('win', 'seq'))
- grad_qkv: float32 [1769472], P(('win', 'seq'))
- grad_out: float32 [589824], P(('win', 'seq'))
- grad_pair_table: float32 [32768], P(('win', 'seq'))
- grad_pair_weight: float32 [3072], P(('win', 'seq'))
- grad_gate: float32 [2359296], P(('win', 'seq'))
- grad_up: float32 [2359296], P(('win', 'seq'))
- grad_down: float32 [2359296], P(('win', 'seq'))
The draws below stay inside these ranges and needn't reach their ends.
Inputs may be any that keep to these rules, and one draw needn't show every extreme that they name: tokens: activations with row and feature scales. `chain_start`: the value 512 means the window holds a single chain.
All inputs are finite; a program needn't handle non-finite values.
Results may differ from the reference program's by a relative error of at most 0.019.
Values may be sent and summed in bfloat16 or wider, within the bound.
A program may use at most 384 MiB of HBM per device.

```python
import math
import jax
import jax.numpy as jnp
from jax import lax

D = 768
HEADS = 12
HEAD = 64
FF = 3072
PAIR = 256
BINS = 64
CLASSES = 4
LENGTH = 512
WINDOWS = 16


def draw_tokens(key, part):
    key_base, key_rows, key_cols = jax.random.split(key, 3)
    base = jax.random.normal(key_base, (WINDOWS, LENGTH, D), jnp.float32)
    row_scale = jnp.exp(jax.random.uniform(key_rows, (WINDOWS, LENGTH, 1), jnp.float32, math.log(0.4), math.log(4.0)))
    col_scale = jnp.exp(jax.random.uniform(key_cols, (D,), jnp.float32, math.log(0.5), math.log(2.0)))
    return jnp.clip(base * row_scale * col_scale, -50.0, 50.0).astype(jnp.bfloat16)


def plant(array, own_key, smallest, high):
    longest = array.shape.index(max(array.shape))
    spots = []
    for shift in (0, 1):
        where = [jax.random.randint(jax.random.fold_in(own_key, axis), (), 0, length) for axis, length in enumerate(array.shape)]
        where[longest] = (where[longest] + shift) % array.shape[longest]
        spots.append(tuple(where))
    return array.at[spots[0]].set(smallest).at[spots[1]].set(high)


def spiked(result, own_key, source, target, blocks, factor):
    def block_of(axis_at):
        return (jnp.arange(result.shape[axis_at]) // (result.shape[axis_at] // blocks)).reshape((-1,) + (1,) * (result.ndim - 1 - axis_at))

    one_side = jax.random.permutation(own_key, blocks)[block_of(target)]
    second = (block_of(target) + blocks // 2) % blocks
    return jnp.where((block_of(source) == one_side) | (block_of(source) == second), factor * result, result)


def steps_of(key, shape, pieces, low, high):
    def one(axis_at, blocks):
        heights = jax.random.uniform(jax.random.fold_in(jax.random.fold_in(key, 6), axis_at), (blocks,), jnp.float32, low / len(pieces), high / len(pieces))
        return jnp.repeat(jnp.exp(heights), shape[axis_at] // blocks).reshape((-1,) + (1,) * (len(shape) - axis_at - 1))

    gain = one(*pieces[0])
    for cut in pieces[1:]:
        gain = gain * one(*cut)
    return gain


def centred(stream_key, dims, scale, reach, pieces=(), kind=jnp.bfloat16):
    values = scale * jax.random.normal(stream_key, dims, jnp.float32)
    if pieces:
        values = values * steps_of(stream_key, dims, pieces, -0.22, 0.18)
    return jnp.clip(values, -reach, reach).astype(kind)


def bell_draw_with(stream_key, dims, deviation, most, cuts, heavy, held_as=jnp.bfloat16):
    array = deviation * jax.random.normal(stream_key, dims, jnp.float32)
    if cuts:
        array = array * steps_of(stream_key, dims, cuts, -0.22, 0.18)
    return jnp.clip(spiked(array, jax.random.fold_in(stream_key, 3), *heavy), -most, most).astype(held_as)


def setup_inputs(seed: int = 0) -> dict:
    keys = jax.random.split(jax.random.key(seed), 16)
    tokens = draw_tokens(jax.random.fold_in(keys[15], 71), 0)
    cotangent = bell_draw_with(keys[1], (WINDOWS, LENGTH, D), 1.0, 6.0, ((0, 8), (1, 4)), (0, 2, 8, 2.0))
    noise_times = jnp.clip(1.0 * jax.random.uniform(keys[2], (WINDOWS,), jnp.float32) ** steps_of(keys[2], (WINDOWS,), ((0, 8),), -0.2, 0.2), 0.0, 1.0)
    cath_ids = plant(jax.random.randint(keys[3], (WINDOWS,), 0, CLASSES), jax.random.fold_in(keys[3], 1), 0, CLASSES - 1).astype(jnp.int32)
    chain_start = plant(jax.random.randint(keys[4], (WINDOWS,), LENGTH // 4, LENGTH + 1), jax.random.fold_in(keys[4], 1), LENGTH // 4, LENGTH).astype(jnp.int32)
    distance_bins = plant(jax.random.randint(keys[5], (WINDOWS, LENGTH, LENGTH), 0, BINS), jax.random.fold_in(keys[5], 1), 0, BINS - 1).astype(jnp.int32)
    class_table = centred(keys[6], (CLASSES, D), 1.0, 6.0)
    ada_weight = centred(keys[7], (D, 6 * D), D ** -0.5, 0.21875)
    qkv_weight = centred(keys[8], (D, 3 * D), D ** -0.5, 0.21875)
    out_weight = centred(keys[9], (D, D), (D // 16) ** -0.5, 0.875)
    pair_table = centred(keys[10], (2 * BINS, PAIR), 1.0, 6.0)
    pair_weight = centred(keys[11], (PAIR, HEADS), PAIR ** -0.5, 0.375)
    gate_weight = centred(keys[12], (D, FF), D ** -0.5, 0.21875)
    up_weight = centred(keys[13], (D, FF), D ** -0.5, 0.21875)
    down_weight = centred(keys[14], (FF, D), (FF // 4) ** -0.5, 0.21875)
    return {"tokens": tokens, "cotangent": cotangent, "noise_times": noise_times, "cath_ids": cath_ids, "chain_start": chain_start, "distance_bins": distance_bins, "class_table": class_table, "ada_weight": ada_weight, "qkv_weight": qkv_weight, "out_weight": out_weight, "pair_table": pair_table, "pair_weight": pair_weight, "gate_weight": gate_weight, "up_weight": up_weight, "down_weight": down_weight}


highest = lax.Precision.HIGHEST
norm_eps = 1e-06

@jax.custom_vjp
def low(v):
    return lax.optimization_barrier(v.astype(jnp.bfloat16)).astype(jnp.float32)

@jax.custom_vjp
def low_back(v):
    return v

def low_keep(v):
    return (low(v), None)

def low_pass(kept, grad):
    return (grad,)

def back_keep(v):
    return (v, None)

def back_low(kept, grad):
    return (low(grad),)
low.defvjp(low_keep, low_pass)
low_back.defvjp(back_keep, back_low)

def layer_norm(values):
    centered = values - lax.optimization_barrier(jnp.mean(values, axis=-1, keepdims=True))
    variance = lax.optimization_barrier(jnp.mean(centered * centered, axis=-1, keepdims=True))
    return centered * lax.rsqrt(variance + norm_eps)

def time_embed(noise_times, model_width):
    half_width = model_width // 2
    frequency = jnp.exp(-math.log(10000.0) * jnp.arange(half_width).astype(jnp.float32) / half_width)
    angles = 1000.0 * noise_times[:, None] * frequency[None, :]
    return jnp.concatenate([jnp.sin(angles), jnp.cos(angles)], axis=-1)

def block_step(params, table_bias, block_tokens, block_mods, block_index):
    group_size = block_tokens.shape[0]
    head_scale = 1.0 / math.sqrt(HEAD)
    shift_attn = block_mods[:, 0][:, None, :]
    scale_attn = block_mods[:, 1][:, None, :]
    gate_attn = block_mods[:, 2][:, None, :]
    shift_ffn = block_mods[:, 3][:, None, :]
    scale_ffn = block_mods[:, 4][:, None, :]
    gate_ffn = block_mods[:, 5][:, None, :]
    attn_in = low(layer_norm(block_tokens) * (1.0 + scale_attn) + shift_attn)
    qkv_values = low(low_back(jnp.einsum('gld,de->gle', attn_in, params['qkv_weight'], precision=highest)))
    queries = qkv_values[..., :D].reshape(group_size, LENGTH, HEADS, HEAD)
    keys_all = qkv_values[..., D:2 * D].reshape(group_size, LENGTH, HEADS, HEAD)
    values_all = qkv_values[..., 2 * D:].reshape(group_size, LENGTH, HEADS, HEAD)
    raw_scores = jnp.einsum('gqhe,gkhe->ghqk', queries, keys_all, precision=highest)
    pair_bias = jnp.moveaxis(table_bias[block_index], -1, 1)
    scores = low_back(raw_scores * head_scale + pair_bias)
    soft_probs = jax.nn.softmax(scores, axis=-1)
    attn_mixed = jnp.einsum('ghqk,gkhe->gqhe', low(soft_probs), values_all, precision=highest)
    attn_mixed = low(low_back(attn_mixed)).reshape(group_size, LENGTH, D)
    attn_out = low_back(jnp.einsum('gld,de->gle', attn_mixed, params['out_weight'], precision=highest))
    hidden_state = block_tokens + jax.nn.sigmoid(gate_attn) * attn_out
    ffn_in = low(layer_norm(hidden_state) * (1.0 + scale_ffn) + shift_ffn)
    gate_val = low_back(jnp.einsum('gld,df->glf', ffn_in, params['gate_weight'], precision=highest))
    up_val = low_back(jnp.einsum('gld,df->glf', ffn_in, params['up_weight'], precision=highest))
    ffn_hidden = low(jax.nn.silu(gate_val) * up_val)
    ffn_out = low_back(jnp.einsum('glf,fd->gld', ffn_hidden, params['down_weight'], precision=highest))
    return hidden_state + jax.nn.sigmoid(gate_ffn) * ffn_out

def reference(tokens, cotangent, noise_times, cath_ids, chain_start, distance_bins, class_table, ada_weight, qkv_weight, out_weight, pair_table, pair_weight, gate_weight, up_weight, down_weight):
    params = {'class_table': class_table.astype(jnp.float32), 'ada_weight': ada_weight.astype(jnp.float32), 'qkv_weight': qkv_weight.astype(jnp.float32), 'out_weight': out_weight.astype(jnp.float32), 'pair_table': pair_table.astype(jnp.float32), 'pair_weight': pair_weight.astype(jnp.float32), 'gate_weight': gate_weight.astype(jnp.float32), 'up_weight': up_weight.astype(jnp.float32), 'down_weight': down_weight.astype(jnp.float32)}
    positions = jnp.arange(LENGTH).astype(jnp.int32)
    first_chain = positions[None, :] < chain_start[:, None]
    same_chain = (first_chain[:, :, None] == first_chain[:, None, :]).astype(jnp.int32)
    pair_index = (distance_bins + BINS * same_chain).astype(jnp.int32)
    group_size = math.gcd(WINDOWS, max(1, 4096 // LENGTH))

    def layer_forward(weights, tokens_in):
        pre_cond = weights['class_table'][cath_ids] + time_embed(noise_times, D)
        condition = jax.nn.silu(pre_cond)
        modulation = jnp.dot(condition, weights['ada_weight'], precision=highest).reshape(WINDOWS, 6, D)
        table_bias = low(jnp.dot(weights['pair_table'], weights['pair_weight'], precision=highest))
        stepper = jax.checkpoint(block_step)

        def one_group(block_items):
            block_tokens, block_mods, block_index = block_items
            return stepper(weights, table_bias, block_tokens, block_mods, block_index)
        outputs = lax.map(one_group, (tokens_in.reshape(-1, group_size, LENGTH, D), modulation.reshape(-1, group_size, 6, D), pair_index.reshape(-1, group_size, LENGTH, LENGTH)))
        return outputs.reshape(WINDOWS, LENGTH, D)
    outputs, pullback = jax.vjp(layer_forward, params, tokens.astype(jnp.float32))
    weight_grads, grad_in = pullback(cotangent.astype(jnp.float32))
    return (outputs.astype(jnp.bfloat16), grad_in.astype(jnp.bfloat16), weight_grads['class_table'].reshape(-1), weight_grads['ada_weight'].reshape(-1), weight_grads['qkv_weight'].reshape(-1), weight_grads['out_weight'].reshape(-1), weight_grads['pair_table'].reshape(-1), weight_grads['pair_weight'].reshape(-1), weight_grads['gate_weight'].reshape(-1), weight_grads['up_weight'].reshape(-1), weight_grads['down_weight'].reshape(-1))
```

```python
import math

import jax
import jax.numpy as jnp
from jax import lax
from jax.sharding import PartitionSpec as P

highest = lax.Precision.HIGHEST
norm_eps = 1e-06
f32 = jnp.float32
bf16 = jnp.bfloat16


def layer_norm_parts(values):
    centered = values - jnp.mean(values, axis=-1, keepdims=True)
    variance = jnp.mean(centered * centered, axis=-1, keepdims=True)
    inv_std = lax.rsqrt(variance + norm_eps)
    return (centered * inv_std, inv_std)


def norm_back(grad_normed, normed, inv_std):
    first_mean = jnp.mean(grad_normed, axis=-1, keepdims=True)
    second_mean = jnp.mean(grad_normed * normed, axis=-1, keepdims=True)
    return (grad_normed - first_mean - normed * second_mean) * inv_std


def time_embed(noise_times, model_width):
    half_width = model_width // 2
    frequency = jnp.exp(
        -math.log(10000.0) * jnp.arange(half_width).astype(f32) / half_width
    )
    angles = 1000.0 * noise_times[:, None] * frequency[None, :]
    return jnp.concatenate([jnp.sin(angles), jnp.cos(angles)], axis=-1)


def dot(a, b):
    return jnp.dot(a, b, preferred_element_type=f32)


def dot_nt(a, b):
    return lax.dot_general(a, b, (((1,), (1,)), ((), ())), preferred_element_type=f32)


def dot_tn(a, b):
    return lax.dot_general(a, b, (((0,), (0,)), ((), ())), preferred_element_type=f32)


def halving_steps(flip):
    win_bits = int(math.log2(lax.axis_size("win")))
    seq_bits = int(math.log2(lax.axis_size("seq")))
    far = list(range(1, win_bits))
    if flip:
        far = far[::-1]
    return [("win", bit) for bit in [0] + far] + [("seq", bit) for bit in range(seq_bits)]


def exchange(values, axis, bit):
    size = lax.axis_size(axis)
    return lax.ppermute(values, axis, [(i, i ^ (1 << bit)) for i in range(size)])


def reduce_owned(grad, flip):
    win_bits = int(math.log2(lax.axis_size("win")))
    seq_bits = int(math.log2(lax.axis_size("seq")))
    columns = grad.shape[1]
    names = [("win", bit) for bit in range(win_bits)[::-1]] + [("seq", bit) for bit in range(seq_bits)[::-1]]
    current = grad
    for step in halving_steps(flip):
        at = names.index(step)
        before = 2**at
        rows = current.shape[0]
        view = current.reshape(before, 2, rows // (2 * before), columns)
        mine = (lax.axis_index(step[0]) >> step[1]) & 1
        send = lax.dynamic_index_in_dim(view, 1 - mine, 1, keepdims=False).astype(bf16)
        got = exchange(send.reshape(rows // 2, columns), *step)
        keep = lax.dynamic_index_in_dim(view, mine, 1, keepdims=False).reshape(rows // 2, columns)
        current = keep.astype(f32) + got.astype(f32)
        names.remove(step)
        if names:
            current = current.astype(bf16)
    return current


def per_device(
    tokens,
    cotangent,
    noise_times,
    cath_ids,
    chain_start,
    distance_bins,
    class_table,
    ada_weight,
    qkv_weight,
    out_weight,
    pair_table,
    pair_weight,
    gate_weight,
    up_weight,
    down_weight,
):
    windows, row_count, width = tokens.shape
    length = distance_bins.shape[2]
    head_count = pair_weight.shape[1]
    head_size = width // head_count
    head_scale = 1.0 / math.sqrt(head_size)
    table_rows = pair_table.shape[0]
    bin_count = table_rows // 2
    classes = class_table.shape[0]
    total_rows = windows * row_count
    win_count = lax.axis_size("win")
    seq_count = lax.axis_size("seq")
    devices = win_count * seq_count
    owner = lax.axis_index("win") * seq_count + lax.axis_index("seq")
    tokens_all = lax.all_gather(tokens, "seq", axis=1, tiled=True)
    class_onehot = (cath_ids[:, None] == jnp.arange(classes, dtype=jnp.int32)[None, :]).astype(f32)
    pre_cond = jnp.dot(
        class_onehot, class_table.astype(f32), precision=highest
    ) + time_embed(noise_times, width)
    cond_sig = jax.nn.sigmoid(pre_cond)
    condition = pre_cond * cond_sig
    window_facts = lax.all_gather(
        jnp.concatenate([pre_cond, class_onehot], axis=-1), "win", axis=0, tiled=True
    )
    ada_float = ada_weight.astype(f32)
    modulation = jnp.dot(condition, ada_float, precision=highest).reshape(windows, 6, width)
    shift_attn = modulation[:, 0][:, None, :]
    scale_attn = modulation[:, 1][:, None, :]
    gate_attn = modulation[:, 2][:, None, :]
    shift_ffn = modulation[:, 3][:, None, :]
    scale_ffn = modulation[:, 4][:, None, :]
    gate_ffn = modulation[:, 5][:, None, :]
    table_bias = dot(pair_table, pair_weight).astype(bf16)
    row_pos = lax.axis_index("seq") * row_count + jnp.arange(row_count, dtype=jnp.int32)
    key_pos = jnp.arange(length, dtype=jnp.int32)
    row_first = row_pos[None, :] < chain_start[:, None]
    key_first = key_pos[None, :] < chain_start[:, None]
    pair_index = distance_bins + bin_count * (
        row_first[:, :, None] == key_first[:, None, :]
    ).astype(jnp.int32)
    tokens_float = tokens.astype(f32)
    normed_x, inv_x = layer_norm_parts(tokens_float)
    attn_in = (normed_x * (1.0 + scale_attn) + shift_attn).astype(bf16).reshape(total_rows, width)
    normed_all, _ = layer_norm_parts(tokens_all.astype(f32))
    attn_in_all = (
        (normed_all * (1.0 + scale_attn) + shift_attn).astype(bf16).reshape(windows * length, width)
    )
    queries = dot(attn_in, qkv_weight[:, :width]).astype(bf16)
    keys_values = dot(attn_in_all, qkv_weight[:, width:]).astype(bf16)
    keys_all = keys_values[:, :width]
    values_all = keys_values[:, width:]

    def head_split(array, rows):
        return array.reshape(windows, rows, head_count, head_size)

    query_heads = head_split(queries, row_count)
    key_heads = head_split(keys_all, length)
    value_heads = head_split(values_all, length)
    pair_onehot = (
        pair_index[:, None, :, :] == jnp.arange(table_rows, dtype=jnp.int32)[None, :, None, None]
    ).astype(bf16)
    raw_scores = jnp.einsum("grhe,glhe->ghrl", query_heads, key_heads, preferred_element_type=f32)
    pair_bias = jnp.einsum("kh,gkrl->ghrl", table_bias, pair_onehot, preferred_element_type=f32)
    scores = raw_scores * head_scale + pair_bias
    row_max = jnp.max(scores, axis=-1, keepdims=True)
    exp_scores = jnp.exp(scores - row_max)
    exp_total = jnp.sum(exp_scores, axis=-1, keepdims=True)
    soft_probs = exp_scores / exp_total
    probs_low = soft_probs.astype(bf16)
    attn_mixed = jnp.einsum("ghrl,glhe->grhe", probs_low, value_heads, preferred_element_type=f32)
    attn_mixed = attn_mixed.astype(bf16).reshape(total_rows, width)

    attn_out = dot(attn_mixed, out_weight).reshape(windows, row_count, width)
    gate_attn_sig = jax.nn.sigmoid(gate_attn)
    hidden_state = tokens_float + gate_attn_sig * attn_out
    normed_h, inv_h = layer_norm_parts(hidden_state)
    ffn_in = (normed_h * (1.0 + scale_ffn) + shift_ffn).astype(bf16).reshape(total_rows, width)
    gate_val = dot(ffn_in, gate_weight)
    up_val = dot(ffn_in, up_weight)
    gate_sig = jax.nn.sigmoid(gate_val)
    silu_gate = gate_val * gate_sig
    ffn_hidden = (silu_gate * up_val).astype(bf16)
    gate_ffn_sig = jax.nn.sigmoid(gate_ffn)
    grad_layer = cotangent.astype(f32)
    grad_ffn = (gate_ffn_sig * grad_layer).astype(bf16).reshape(total_rows, width)
    owned_down = reduce_owned(dot_tn(ffn_hidden, grad_ffn).astype(bf16), False)
    ffn_out = dot(ffn_hidden, down_weight).reshape(windows, row_count, width)
    layer_out = (hidden_state + gate_ffn_sig * ffn_out).astype(bf16)
    grad_gate_ffn = jnp.sum(grad_layer * ffn_out * gate_ffn_sig * (1.0 - gate_ffn_sig), axis=1)
    grad_hidden_ffn = dot_nt(grad_ffn, down_weight)
    grad_up_val = (grad_hidden_ffn * silu_gate).astype(bf16)
    grad_gate_val = (
        grad_hidden_ffn * up_val * gate_sig * (1.0 + gate_val * (1.0 - gate_sig))
    ).astype(bf16)
    owned_gate = reduce_owned(dot_tn(ffn_in, grad_gate_val).astype(bf16), True)
    owned_up = reduce_owned(dot_tn(ffn_in, grad_up_val).astype(bf16), False)
    grad_ffn_in = dot_nt(grad_gate_val, gate_weight) + dot_nt(grad_up_val, up_weight)
    grad_ffn_in = grad_ffn_in.reshape(windows, row_count, width)
    grad_scale_ffn = jnp.sum(grad_ffn_in * normed_h, axis=1)
    grad_shift_ffn = jnp.sum(grad_ffn_in, axis=1)
    grad_hidden = grad_layer + norm_back(grad_ffn_in * (1.0 + scale_ffn), normed_h, inv_h)
    grad_attn_out = (gate_attn_sig * grad_hidden).astype(bf16).reshape(total_rows, width)
    grad_gate_attn = jnp.sum(grad_hidden * attn_out * gate_attn_sig * (1.0 - gate_attn_sig), axis=1)
    grad_out = dot_tn(attn_mixed, grad_attn_out).astype(bf16)
    grad_mixed = dot_nt(grad_attn_out, out_weight).astype(bf16)

    grad_heads = head_split(grad_mixed, row_count)
    grad_probs = jnp.einsum("grhe,glhe->ghrl", grad_heads, value_heads, preferred_element_type=f32)
    grad_scores = (
        soft_probs * (grad_probs - jnp.sum(soft_probs * grad_probs, axis=-1, keepdims=True))
    ).astype(bf16)
    grad_query = (
        jnp.einsum("ghrl,glhe->grhe", grad_scores, key_heads, preferred_element_type=f32) * head_scale
    )
    grad_key = (
        jnp.einsum("ghrl,grhe->glhe", grad_scores, query_heads, preferred_element_type=f32)
        * head_scale
    )
    grad_value = jnp.einsum("ghrl,grhe->glhe", probs_low, grad_heads, preferred_element_type=f32)
    grad_table = jnp.einsum("ghrl,gkrl->kh", grad_scores, pair_onehot, preferred_element_type=f32)
    grad_query = grad_query.astype(bf16).reshape(total_rows, width)
    grad_kv = jnp.concatenate(
        [
            grad_key.astype(bf16).reshape(windows * length, width),
            grad_value.astype(bf16).reshape(windows * length, width),
        ],
        axis=-1,
    )
    grad_in_part = dot_nt(grad_kv, qkv_weight[:, width:]).astype(bf16)
    grad_in_far = lax.psum_scatter(
        grad_in_part.reshape(windows, length, width), "seq", scatter_dimension=1, tiled=True
    )
    grad_qkv = jnp.concatenate(
        [
            dot_tn(attn_in, grad_query).astype(bf16),
            dot_tn(attn_in_all, grad_kv).astype(bf16),
            grad_out,
        ],
        axis=-1,
    )
    owned_qkv_out = reduce_owned(grad_qkv, True)
    grad_attn_in = dot_nt(grad_query, qkv_weight[:, :width]).reshape(
        windows, row_count, width
    ) + grad_in_far.astype(f32)
    grad_scale_attn = jnp.sum(grad_attn_in * normed_x, axis=1)
    grad_shift_attn = jnp.sum(grad_attn_in, axis=1)
    grad_tokens = (
        grad_hidden + norm_back(grad_attn_in * (1.0 + scale_attn), normed_x, inv_x)
    ).astype(bf16)
    grad_mod = jnp.concatenate(
        [
            grad_shift_attn,
            grad_scale_attn,
            grad_gate_attn,
            grad_shift_ffn,
            grad_scale_ffn,
            grad_gate_ffn,
        ],
        axis=1,
    )
    parts = jnp.concatenate([grad_mod.reshape(-1), grad_table.reshape(-1)])
    parts_all = lax.all_gather(parts, ("win", "seq"), axis=0)
    mod_size = windows * 6 * width
    mod_all = jnp.sum(
        parts_all[:, :mod_size].reshape(win_count, seq_count, windows, 6 * width), axis=1
    ).reshape(win_count * windows, 6 * width)
    table_all = jnp.sum(parts_all[:, mod_size:], axis=0).reshape(table_rows, head_count)
    pre_all = window_facts[:, :width]
    onehot_all = window_facts[:, width:]
    ada_rows = width // devices
    sig_all = jax.nn.sigmoid(pre_all)
    condition_rows = lax.dynamic_slice_in_dim(pre_all * sig_all, owner * ada_rows, ada_rows, 1)
    owned_ada = lax.dot_general(
        condition_rows, mod_all, (((0,), (0,)), ((), ())), precision=highest
    )
    class_share = classes * width // devices
    per_class = width // class_share
    column_at = (owner % per_class) * class_share
    pre_cols = lax.dynamic_slice_in_dim(pre_all, column_at, class_share, 1)
    sig_cols = lax.dynamic_slice_in_dim(sig_all, column_at, class_share, 1)
    ada_cols = lax.dynamic_slice_in_dim(ada_weight, column_at, class_share, 0).astype(f32)
    grad_cond = lax.dot_general(mod_all, ada_cols, (((1,), (1,)), ((), ())), precision=highest)
    grad_pre = grad_cond * sig_cols * (1.0 + pre_cols * (1.0 - sig_cols))
    onehot_mine = lax.dynamic_slice_in_dim(onehot_all, owner // per_class, 1, 1)
    owned_class = jnp.sum(grad_pre * onehot_mine, axis=0)
    grad_pair_table = jnp.dot(table_all, pair_weight.astype(f32).T, precision=highest).reshape(-1)
    grad_pair_weight = jnp.dot(pair_table.astype(f32).T, table_all, precision=highest).reshape(-1)
    table_size = grad_pair_table.shape[0] // devices
    weight_size = grad_pair_weight.shape[0] // devices
    owned_pair_table = lax.dynamic_slice_in_dim(grad_pair_table, owner * table_size, table_size)
    owned_pair_weight = lax.dynamic_slice_in_dim(grad_pair_weight, owner * weight_size, weight_size)
    return (
        layer_out,
        grad_tokens,
        owned_class,
        owned_ada.reshape(-1),
        owned_qkv_out[:, : 3 * width].reshape(-1),
        owned_qkv_out[:, 3 * width :].reshape(-1),
        owned_pair_table,
        owned_pair_weight,
        owned_gate.reshape(-1),
        owned_up.reshape(-1),
        owned_down.reshape(-1),
    )


def solution(mesh):
    rows = P("win", "seq", None)
    flat = P(("win", "seq"))
    placed = (rows, rows, P("win"), P("win"), P("win"), rows) + (P(),) * 9
    return jax.shard_map(
        per_device, mesh=mesh, in_specs=placed, out_specs=(rows, rows) + (flat,) * 9, check_vma=False
    )
```

```python
import functools
import math

import jax
import jax.numpy as jnp
from jax import lax
from jax.experimental import pallas as pl
from jax.experimental.pallas import tpu as pltpu
from jax.sharding import PartitionSpec as P

highest = lax.Precision.HIGHEST
norm_eps = 1e-06
f32 = jnp.float32
bf16 = jnp.bfloat16


def layer_norm_parts(values):
    centered = values - jnp.mean(values, axis=-1, keepdims=True)
    variance = jnp.mean(centered * centered, axis=-1, keepdims=True)
    inv_std = lax.rsqrt(variance + norm_eps)
    return (centered * inv_std, inv_std)


def norm_back(grad_normed, normed, inv_std):
    first_mean = jnp.mean(grad_normed, axis=-1, keepdims=True)
    second_mean = jnp.mean(grad_normed * normed, axis=-1, keepdims=True)
    return (grad_normed - first_mean - normed * second_mean) * inv_std


def time_embed(noise_times, model_width):
    half_width = model_width // 2
    frequency = jnp.exp(
        -math.log(10000.0) * jnp.arange(half_width).astype(f32) / half_width
    )
    angles = 1000.0 * noise_times[:, None] * frequency[None, :]
    return jnp.concatenate([jnp.sin(angles), jnp.cos(angles)], axis=-1)


def dot(a, b):
    return jnp.dot(a, b, preferred_element_type=f32)


def dot_nt(a, b):
    return lax.dot_general(a, b, (((1,), (1,)), ((), ())), preferred_element_type=f32)


def dot_tn(a, b):
    return lax.dot_general(a, b, (((0,), (0,)), ((), ())), preferred_element_type=f32)


def pair_halves(values, head_size):
    lane = lax.broadcasted_iota(jnp.int32, values.shape, 1)
    zero = jnp.zeros_like(values)
    return jnp.concatenate(
        [jnp.where(lane < head_size, values, zero), jnp.where(lane >= head_size, values, zero)], axis=0
    )


def pair_diagonal(values, head_size, rows):
    return jnp.concatenate([values[:head_size, :rows], values[head_size:, rows:]], axis=0).T


def transposed_index(facts_ref, bins_ref, bin_count):
    window = pl.program_id(0)
    start = facts_ref[window]
    offset = facts_ref[pl.num_programs(0)]
    bins = bins_ref[0].T
    key_first = lax.broadcasted_iota(jnp.int32, bins.shape, 0) < start
    row_first = lax.broadcasted_iota(jnp.int32, bins.shape, 1) + offset < start
    return bins + jnp.where(key_first == row_first, bin_count, 0)


def pair_scores(pair, cols, q_ref, k_ref, table_ref, index_ref, head_scale, head_size):
    q_pair = pair_halves(q_ref[:, cols] * head_scale, head_size)
    k_pair = k_ref[:, cols]
    scores = dot_nt(k_pair, q_pair)
    index = index_ref[...]
    biases = []
    for head in range(2):
        entries = jnp.broadcast_to(table_ref[pl.ds(2 * pair + head, 1), :], index.shape)
        biases.append(jnp.take_along_axis(entries, index, axis=1, mode="promise_in_bounds"))
    return (q_pair, k_pair, scores + jnp.concatenate(biases, axis=1))


def attend_kernel(
    head_size, bin_count, facts_ref, q_ref, k_ref, v_ref, bins_ref, table_ref, out_ref, log_ref, index_ref
):
    rows, width = q_ref.shape
    head_scale = 1.0 / math.sqrt(head_size)
    index_ref[...] = transposed_index(facts_ref, bins_ref, bin_count)

    def one_pair(pair, carry):
        cols = pl.ds(pl.multiple_of(pair * 2 * head_size, 2 * head_size), 2 * head_size)
        _, _, scores = pair_scores(
            pair, cols, q_ref, k_ref, table_ref, index_ref, head_scale, head_size
        )
        top = jnp.max(scores, axis=0, keepdims=True)
        raised = jnp.exp(scores - top)
        total = jnp.sum(raised, axis=0, keepdims=True)
        probs = (raised * (1.0 / total)).astype(bf16)
        mixed = dot(v_ref[:, cols].T, probs)
        out_ref[:, cols] = pair_diagonal(mixed, head_size, rows).astype(bf16)
        log_ref[0, pl.ds(pair, 1), :] = top + jnp.log(total)
        return carry

    lax.fori_loop(0, width // (2 * head_size), one_pair, 0)


def attend_back_kernel(
    head_size,
    bin_count,
    facts_ref,
    q_ref,
    k_ref,
    v_ref,
    bins_ref,
    table_ref,
    grad_ref,
    log_ref,
    grad_q_ref,
    grad_kv_ref,
    grad_scores_ref,
    index_ref,
):
    rows, width = q_ref.shape
    head_scale = 1.0 / math.sqrt(head_size)
    index_ref[...] = transposed_index(facts_ref, bins_ref, bin_count)

    def one_pair(pair, carry):
        start = pl.multiple_of(pair * 2 * head_size, 2 * head_size)
        cols = pl.ds(start, 2 * head_size)
        v_cols = pl.ds(width + start, 2 * head_size)
        q_pair, k_pair, scores = pair_scores(
            pair, cols, q_ref, k_ref, table_ref, index_ref, head_scale, head_size
        )
        probs = jnp.exp(scores - log_ref[0, pl.ds(pair, 1), :])
        g_pair = pair_halves(grad_ref[:, cols], head_size)
        grad_kv_ref[:, v_cols] = dot(probs.astype(bf16), g_pair).astype(bf16)
        grad_probs = dot_nt(v_ref[:, cols], g_pair)
        delta = jnp.sum(probs * grad_probs, axis=0, keepdims=True)
        grad_scores = (probs * (grad_probs - delta)).astype(bf16)
        grad_kv_ref[:, cols] = dot(grad_scores, q_pair).astype(bf16)
        grad_q = pair_diagonal(dot(k_pair.T, grad_scores), head_size, rows) * head_scale
        grad_q_ref[:, cols] = grad_q.astype(bf16)
        grad_scores_ref[0, 2 * pair] = grad_scores[:, :rows]
        grad_scores_ref[0, 2 * pair + 1] = grad_scores[:, rows:]
        return carry

    lax.fori_loop(0, width // (2 * head_size), one_pair, 0)


def attention_specs(rows, length, width, table_shape):
    return [
        pl.BlockSpec(memory_space=pltpu.SMEM),
        pl.BlockSpec((rows, width), lambda w: (w, 0)),
        pl.BlockSpec((length, width), lambda w: (w, 0)),
        pl.BlockSpec((length, width), lambda w: (w, 1)),
        pl.BlockSpec((1, rows, length), lambda w: (w, 0, 0)),
        pl.BlockSpec(table_shape, lambda w: (0, 0)),
    ]


def attend(facts, queries, keys_values, bins, table, head_size):
    windows, rows, length = bins.shape
    width = queries.shape[1]
    pairs = width // (2 * head_size)
    return pl.pallas_call(
        functools.partial(attend_kernel, head_size, table.shape[1] // 2),
        grid=(windows,),
        in_specs=attention_specs(rows, length, width, table.shape),
        out_specs=[
            pl.BlockSpec((rows, width), lambda w: (w, 0)),
            pl.BlockSpec((1, pairs, 2 * rows), lambda w: (w, 0, 0)),
        ],
        out_shape=[
            jax.ShapeDtypeStruct((windows * rows, width), bf16),
            jax.ShapeDtypeStruct((windows, pairs, 2 * rows), f32),
        ],
        scratch_shapes=[pltpu.VMEM((length, rows), jnp.int32)],
        cost_estimate=pl.CostEstimate(
            flops=8 * windows * rows * length * width,
            bytes_accessed=4 * windows * rows * length,
            transcendentals=windows * rows * length * 2 * pairs,
        ),
        name="attend",
    )(facts, queries, keys_values, keys_values, bins, table)


def attend_back(facts, queries, keys_values, bins, table, grads, logs, head_size):
    windows, rows, length = bins.shape
    width = queries.shape[1]
    pairs = width // (2 * head_size)
    return pl.pallas_call(
        functools.partial(attend_back_kernel, head_size, table.shape[1] // 2),
        grid=(windows,),
        in_specs=attention_specs(rows, length, width, table.shape)
        + [
            pl.BlockSpec((rows, width), lambda w: (w, 0)),
            pl.BlockSpec((1, pairs, 2 * rows), lambda w: (w, 0, 0)),
        ],
        out_specs=[
            pl.BlockSpec((rows, width), lambda w: (w, 0)),
            pl.BlockSpec((length, 2 * width), lambda w: (w, 0)),
            pl.BlockSpec((1, 2 * pairs, length, rows), lambda w: (w, 0, 0, 0)),
        ],
        out_shape=[
            jax.ShapeDtypeStruct((windows * rows, width), bf16),
            jax.ShapeDtypeStruct((windows * length, 2 * width), bf16),
            jax.ShapeDtypeStruct((windows, 2 * pairs, length, rows), bf16),
        ],
        scratch_shapes=[pltpu.VMEM((length, rows), jnp.int32)],
        cost_estimate=pl.CostEstimate(
            flops=20 * windows * rows * length * width,
            bytes_accessed=8 * windows * rows * length * pairs,
            transcendentals=windows * rows * length * 2 * pairs,
        ),
        name="attend_back",
    )(facts, queries, keys_values, keys_values, bins, table, grads, logs)


def halving_steps(flip):
    win_bits = int(math.log2(lax.axis_size("win")))
    seq_bits = int(math.log2(lax.axis_size("seq")))
    far = list(range(1, win_bits))
    if flip:
        far = far[::-1]
    return [("win", bit) for bit in [0] + far] + [("seq", bit) for bit in range(seq_bits)]


def exchange(values, axis, bit):
    size = lax.axis_size(axis)
    return lax.ppermute(values, axis, [(i, i ^ (1 << bit)) for i in range(size)])


def reduce_owned(grad, flip):
    win_bits = int(math.log2(lax.axis_size("win")))
    seq_bits = int(math.log2(lax.axis_size("seq")))
    columns = grad.shape[1]
    names = [("win", bit) for bit in range(win_bits)[::-1]] + [("seq", bit) for bit in range(seq_bits)[::-1]]
    current = grad
    for step in halving_steps(flip):
        at = names.index(step)
        before = 2**at
        rows = current.shape[0]
        view = current.reshape(before, 2, rows // (2 * before), columns)
        mine = (lax.axis_index(step[0]) >> step[1]) & 1
        send = lax.dynamic_index_in_dim(view, 1 - mine, 1, keepdims=False).astype(bf16)
        got = exchange(send.reshape(rows // 2, columns), *step)
        keep = lax.dynamic_index_in_dim(view, mine, 1, keepdims=False).reshape(rows // 2, columns)
        current = keep.astype(f32) + got.astype(f32)
        names.remove(step)
        if names:
            current = current.astype(bf16)
    return current


def per_device(
    tokens,
    cotangent,
    noise_times,
    cath_ids,
    chain_start,
    distance_bins,
    class_table,
    ada_weight,
    qkv_weight,
    out_weight,
    pair_table,
    pair_weight,
    gate_weight,
    up_weight,
    down_weight,
):
    windows, row_count, width = tokens.shape
    length = distance_bins.shape[2]
    head_count = pair_weight.shape[1]
    head_size = width // head_count
    table_rows = pair_table.shape[0]
    bin_count = table_rows // 2
    classes = class_table.shape[0]
    total_rows = windows * row_count
    win_count = lax.axis_size("win")
    seq_count = lax.axis_size("seq")
    devices = win_count * seq_count
    owner = lax.axis_index("win") * seq_count + lax.axis_index("seq")
    tokens_all = lax.all_gather(tokens, "seq", axis=1, tiled=True)
    class_onehot = (cath_ids[:, None] == jnp.arange(classes, dtype=jnp.int32)[None, :]).astype(f32)
    pre_cond = jnp.dot(
        class_onehot, class_table.astype(f32), precision=highest
    ) + time_embed(noise_times, width)
    cond_sig = jax.nn.sigmoid(pre_cond)
    condition = pre_cond * cond_sig
    window_facts = jnp.concatenate([pre_cond, class_onehot], axis=-1)
    ada_float = ada_weight.astype(f32)
    modulation = jnp.dot(condition, ada_float, precision=highest).reshape(windows, 6, width)
    shift_attn = modulation[:, 0][:, None, :]
    scale_attn = modulation[:, 1][:, None, :]
    gate_attn = modulation[:, 2][:, None, :]
    shift_ffn = modulation[:, 3][:, None, :]
    scale_ffn = modulation[:, 4][:, None, :]
    gate_ffn = modulation[:, 5][:, None, :]
    table_bias = dot(pair_table, pair_weight).astype(bf16)
    facts = jnp.concatenate(
        [chain_start, jnp.full((1,), lax.axis_index("seq") * row_count, jnp.int32)]
    )
    table = table_bias.astype(f32).T
    tokens_float = tokens.astype(f32)
    normed_x, inv_x = layer_norm_parts(tokens_float)
    attn_in = (normed_x * (1.0 + scale_attn) + shift_attn).astype(bf16).reshape(total_rows, width)
    normed_all, _ = layer_norm_parts(tokens_all.astype(f32))
    attn_in_all = (
        (normed_all * (1.0 + scale_attn) + shift_attn).astype(bf16).reshape(windows * length, width)
    )
    queries = dot(attn_in, qkv_weight[:, :width]).astype(bf16)
    keys_values = dot(attn_in_all, qkv_weight[:, width:]).astype(bf16)
    attn_mixed, log_totals = attend(facts, queries, keys_values, distance_bins, table, head_size)
    attn_out = dot(attn_mixed, out_weight).reshape(windows, row_count, width)
    gate_attn_sig = jax.nn.sigmoid(gate_attn)
    hidden_state = tokens_float + gate_attn_sig * attn_out
    normed_h, inv_h = layer_norm_parts(hidden_state)
    ffn_in = (normed_h * (1.0 + scale_ffn) + shift_ffn).astype(bf16).reshape(total_rows, width)
    gate_val = dot(ffn_in, gate_weight)
    up_val = dot(ffn_in, up_weight)
    gate_sig = jax.nn.sigmoid(gate_val)
    silu_gate = gate_val * gate_sig
    ffn_hidden = (silu_gate * up_val).astype(bf16)
    gate_ffn_sig = jax.nn.sigmoid(gate_ffn)
    grad_layer = cotangent.astype(f32)
    grad_ffn = (gate_ffn_sig * grad_layer).astype(bf16).reshape(total_rows, width)
    owned_down = reduce_owned(dot_tn(ffn_hidden, grad_ffn).astype(bf16), False)
    ffn_out = dot(ffn_hidden, down_weight).reshape(windows, row_count, width)
    layer_out = (hidden_state + gate_ffn_sig * ffn_out).astype(bf16)
    grad_gate_ffn = jnp.sum(grad_layer * ffn_out * gate_ffn_sig * (1.0 - gate_ffn_sig), axis=1)
    grad_hidden_ffn = dot_nt(grad_ffn, down_weight)
    grad_up_val = (grad_hidden_ffn * silu_gate).astype(bf16)
    grad_gate_val = (
        grad_hidden_ffn * up_val * gate_sig * (1.0 + gate_val * (1.0 - gate_sig))
    ).astype(bf16)
    owned_gate = reduce_owned(dot_tn(ffn_in, grad_gate_val).astype(bf16), True)
    owned_up = reduce_owned(dot_tn(ffn_in, grad_up_val).astype(bf16), False)
    grad_ffn_in = dot_nt(grad_gate_val, gate_weight) + dot_nt(grad_up_val, up_weight)
    grad_ffn_in = grad_ffn_in.reshape(windows, row_count, width)
    grad_scale_ffn = jnp.sum(grad_ffn_in * normed_h, axis=1)
    grad_shift_ffn = jnp.sum(grad_ffn_in, axis=1)
    grad_hidden = grad_layer + norm_back(grad_ffn_in * (1.0 + scale_ffn), normed_h, inv_h)
    grad_attn_out = (gate_attn_sig * grad_hidden).astype(bf16).reshape(total_rows, width)
    grad_gate_attn = jnp.sum(grad_hidden * attn_out * gate_attn_sig * (1.0 - gate_attn_sig), axis=1)
    grad_out = dot_tn(attn_mixed, grad_attn_out).astype(bf16)
    grad_mixed = dot_nt(grad_attn_out, out_weight).astype(bf16)

    grad_query, grad_kv, grad_scores = attend_back(
        facts, queries, keys_values, distance_bins, table, grad_mixed, log_totals, head_size
    )
    row_first = lax.axis_index("seq") * row_count + jnp.arange(row_count)[None, None, :] < chain_start[:, None, None]
    key_first = jnp.arange(length)[None, :, None] < chain_start[:, None, None]
    index_back = jnp.swapaxes(distance_bins, 1, 2) + bin_count * (row_first == key_first).astype(jnp.int32)
    pair_onehot = (
        index_back[:, None, :, :] == jnp.arange(table_rows, dtype=jnp.int32)[None, :, None, None]
    ).astype(bf16)
    grad_table = jnp.einsum("whji,wkji->kh", grad_scores, pair_onehot, preferred_element_type=f32)
    grad_in_part = dot_nt(grad_kv, qkv_weight[:, width:]).astype(bf16)
    grad_in_far = lax.psum_scatter(
        grad_in_part.reshape(windows, length, width), "seq", scatter_dimension=1, tiled=True
    )
    grad_qkv = jnp.concatenate(
        [
            dot_tn(attn_in, grad_query).astype(bf16),
            dot_tn(attn_in_all, grad_kv).astype(bf16),
            grad_out,
        ],
        axis=-1,
    )
    owned_qkv_out = reduce_owned(grad_qkv, True)
    grad_attn_in = dot_nt(grad_query, qkv_weight[:, :width]).reshape(
        windows, row_count, width
    ) + grad_in_far.astype(f32)
    grad_scale_attn = jnp.sum(grad_attn_in * normed_x, axis=1)
    grad_shift_attn = jnp.sum(grad_attn_in, axis=1)
    grad_tokens = (
        grad_hidden + norm_back(grad_attn_in * (1.0 + scale_attn), normed_x, inv_x)
    ).astype(bf16)
    grad_mod = jnp.concatenate(
        [
            grad_shift_attn,
            grad_scale_attn,
            grad_gate_attn,
            grad_shift_ffn,
            grad_scale_ffn,
            grad_gate_ffn,
        ],
        axis=1,
    )
    parts = jnp.concatenate([grad_mod.reshape(-1), grad_table.reshape(-1), window_facts.reshape(-1)])
    parts = jnp.pad(parts, (0, -parts.shape[0] % 1024))
    parts_all = lax.all_gather(parts, ("win", "seq"), axis=0)
    mod_size = windows * 6 * width
    mod_all = jnp.sum(
        parts_all[:, :mod_size].reshape(win_count, seq_count, windows, 6 * width), axis=1
    ).reshape(win_count * windows, 6 * width)
    table_end = mod_size + table_rows * head_count
    table_all = jnp.sum(parts_all[:, mod_size:table_end], axis=0).reshape(table_rows, head_count)
    window_facts = parts_all[::seq_count, table_end : table_end + windows * (width + classes)].reshape(win_count * windows, width + classes)
    pre_all = window_facts[:, :width]
    onehot_all = window_facts[:, width:]
    ada_rows = width // devices
    sig_all = jax.nn.sigmoid(pre_all)
    condition_rows = lax.dynamic_slice_in_dim(pre_all * sig_all, owner * ada_rows, ada_rows, 1)
    owned_ada = lax.dot_general(
        condition_rows, mod_all, (((0,), (0,)), ((), ())), precision=highest
    )
    class_share = classes * width // devices
    per_class = width // class_share
    column_at = (owner % per_class) * class_share
    pre_cols = lax.dynamic_slice_in_dim(pre_all, column_at, class_share, 1)
    sig_cols = lax.dynamic_slice_in_dim(sig_all, column_at, class_share, 1)
    ada_cols = lax.dynamic_slice_in_dim(ada_weight, column_at, class_share, 0).astype(f32)
    grad_cond = lax.dot_general(mod_all, ada_cols, (((1,), (1,)), ((), ())), precision=highest)
    grad_pre = grad_cond * sig_cols * (1.0 + pre_cols * (1.0 - sig_cols))
    onehot_mine = lax.dynamic_slice_in_dim(onehot_all, owner // per_class, 1, 1)
    owned_class = jnp.sum(grad_pre * onehot_mine, axis=0)
    grad_pair_table = jnp.dot(table_all, pair_weight.astype(f32).T, precision=highest).reshape(-1)
    grad_pair_weight = jnp.dot(pair_table.astype(f32).T, table_all, precision=highest).reshape(-1)
    table_size = grad_pair_table.shape[0] // devices
    weight_size = grad_pair_weight.shape[0] // devices
    owned_pair_table = lax.dynamic_slice_in_dim(grad_pair_table, owner * table_size, table_size)
    owned_pair_weight = lax.dynamic_slice_in_dim(grad_pair_weight, owner * weight_size, weight_size)
    return (
        layer_out,
        grad_tokens,
        owned_class,
        owned_ada.reshape(-1),
        owned_qkv_out[:, : 3 * width].reshape(-1),
        owned_qkv_out[:, 3 * width :].reshape(-1),
        owned_pair_table,
        owned_pair_weight,
        owned_gate.reshape(-1),
        owned_up.reshape(-1),
        owned_down.reshape(-1),
    )


def solution(mesh):
    rows = P("win", "seq", None)
    flat = P(("win", "seq"))
    placed = (rows, rows, P("win"), P("win"), P("win"), rows) + (P(),) * 9
    return jax.shard_map(
        per_device, mesh=mesh, in_specs=placed, out_specs=(rows, rows) + (flat,) * 9, check_vma=False
    )
```

```python
import functools
import math

import jax
import jax.numpy as jnp
from jax import lax
from jax.experimental import pallas as pl
from jax.experimental.pallas import tpu as pltpu
from jax.sharding import PartitionSpec as P

highest = lax.Precision.HIGHEST
norm_eps = 1e-06
f32 = jnp.float32
bf16 = jnp.bfloat16


def layer_norm_parts(values):
    centered = values - jnp.mean(values, axis=-1, keepdims=True)
    variance = jnp.mean(centered * centered, axis=-1, keepdims=True)
    inv_std = lax.rsqrt(variance + norm_eps)
    return (centered * inv_std, inv_std)


def norm_back(grad_normed, normed, inv_std):
    first_mean = jnp.mean(grad_normed, axis=-1, keepdims=True)
    second_mean = jnp.mean(grad_normed * normed, axis=-1, keepdims=True)
    return (grad_normed - first_mean - normed * second_mean) * inv_std


def time_embed(noise_times, model_width):
    half_width = model_width // 2
    frequency = jnp.exp(
        -math.log(10000.0) * jnp.arange(half_width).astype(f32) / half_width
    )
    angles = 1000.0 * noise_times[:, None] * frequency[None, :]
    return jnp.concatenate([jnp.sin(angles), jnp.cos(angles)], axis=-1)


def dot(a, b):
    return jnp.dot(a, b, preferred_element_type=f32)


def dot_nt(a, b):
    return lax.dot_general(a, b, (((1,), (1,)), ((), ())), preferred_element_type=f32)


def dot_tn(a, b):
    return lax.dot_general(a, b, (((0,), (0,)), ((), ())), preferred_element_type=f32)


def pair_halves(values, head_size):
    lane = lax.broadcasted_iota(jnp.int32, values.shape, 1)
    zero = jnp.zeros_like(values)
    return jnp.concatenate(
        [jnp.where(lane < head_size, values, zero), jnp.where(lane >= head_size, values, zero)], axis=0
    )


def pair_diagonal(values, head_size, rows):
    return jnp.concatenate([values[:head_size, :rows], values[head_size:, rows:]], axis=0).T


def transposed_index(facts_ref, bins_ref, bin_count):
    window = pl.program_id(0)
    start = facts_ref[window]
    offset = facts_ref[pl.num_programs(0)]
    bins = bins_ref[0].T
    key_first = lax.broadcasted_iota(jnp.int32, bins.shape, 0) < start
    row_first = lax.broadcasted_iota(jnp.int32, bins.shape, 1) + offset < start
    return bins + jnp.where(key_first == row_first, bin_count, 0)


def pair_scores(pair, cols, q_ref, k_ref, table_ref, index_ref, head_scale, head_size):
    q_pair = pair_halves(q_ref[:, cols] * head_scale, head_size)
    k_pair = k_ref[:, cols]
    scores = dot_nt(k_pair, q_pair)
    index = index_ref[...]
    biases = []
    for head in range(2):
        entries = jnp.broadcast_to(table_ref[pl.ds(2 * pair + head, 1), :], index.shape)
        biases.append(jnp.take_along_axis(entries, index, axis=1, mode="promise_in_bounds"))
    return (q_pair, k_pair, scores + jnp.concatenate(biases, axis=1))


def attend_kernel(
    head_size, bin_count, facts_ref, q_ref, k_ref, v_ref, bins_ref, table_ref, out_ref, log_ref, index_ref
):
    rows, width = q_ref.shape
    head_scale = 1.0 / math.sqrt(head_size)
    index_ref[...] = transposed_index(facts_ref, bins_ref, bin_count)

    def one_pair(pair, carry):
        cols = pl.ds(pl.multiple_of(pair * 2 * head_size, 2 * head_size), 2 * head_size)
        _, _, scores = pair_scores(
            pair, cols, q_ref, k_ref, table_ref, index_ref, head_scale, head_size
        )
        top = jnp.max(scores, axis=0, keepdims=True)
        raised = jnp.exp(scores - top)
        total = jnp.sum(raised, axis=0, keepdims=True)
        probs = (raised * (1.0 / total)).astype(bf16)
        mixed = dot(v_ref[:, cols].T, probs)
        out_ref[:, cols] = pair_diagonal(mixed, head_size, rows).astype(bf16)
        log_ref[0, pl.ds(pair, 1), :] = top + jnp.log(total)
        return carry

    lax.fori_loop(0, width // (2 * head_size), one_pair, 0)


def attend_back_kernel(
    head_size,
    bin_count,
    facts_ref,
    q_ref,
    k_ref,
    v_ref,
    bins_ref,
    table_ref,
    grad_ref,
    log_ref,
    grad_q_ref,
    grad_kv_ref,
    grad_scores_ref,
    index_ref,
):
    rows, width = q_ref.shape
    head_scale = 1.0 / math.sqrt(head_size)
    index_ref[...] = transposed_index(facts_ref, bins_ref, bin_count)

    def one_pair(pair, carry):
        start = pl.multiple_of(pair * 2 * head_size, 2 * head_size)
        cols = pl.ds(start, 2 * head_size)
        v_cols = pl.ds(width + start, 2 * head_size)
        q_pair, k_pair, scores = pair_scores(
            pair, cols, q_ref, k_ref, table_ref, index_ref, head_scale, head_size
        )
        probs = jnp.exp(scores - log_ref[0, pl.ds(pair, 1), :])
        g_pair = pair_halves(grad_ref[:, cols], head_size)
        grad_kv_ref[:, v_cols] = dot(probs.astype(bf16), g_pair).astype(bf16)
        grad_probs = dot_nt(v_ref[:, cols], g_pair)
        delta = jnp.sum(probs * grad_probs, axis=0, keepdims=True)
        grad_scores = (probs * (grad_probs - delta)).astype(bf16)
        grad_kv_ref[:, cols] = dot(grad_scores, q_pair).astype(bf16)
        grad_q = pair_diagonal(dot(k_pair.T, grad_scores), head_size, rows) * head_scale
        grad_q_ref[:, cols] = grad_q.astype(bf16)
        grad_scores_ref[0, 2 * pair] = grad_scores[:, :rows]
        grad_scores_ref[0, 2 * pair + 1] = grad_scores[:, rows:]
        return carry

    lax.fori_loop(0, width // (2 * head_size), one_pair, 0)


def attention_specs(rows, length, width, table_shape):
    return [
        pl.BlockSpec(memory_space=pltpu.SMEM),
        pl.BlockSpec((rows, width), lambda w: (w, 0)),
        pl.BlockSpec((length, width), lambda w: (w, 0)),
        pl.BlockSpec((length, width), lambda w: (w, 1)),
        pl.BlockSpec((1, rows, length), lambda w: (w, 0, 0)),
        pl.BlockSpec(table_shape, lambda w: (0, 0)),
    ]


def attend(facts, queries, keys_values, bins, table, head_size):
    windows, rows, length = bins.shape
    width = queries.shape[1]
    pairs = width // (2 * head_size)
    return pl.pallas_call(
        functools.partial(attend_kernel, head_size, table.shape[1] // 2),
        grid=(windows,),
        in_specs=attention_specs(rows, length, width, table.shape),
        out_specs=[
            pl.BlockSpec((rows, width), lambda w: (w, 0)),
            pl.BlockSpec((1, pairs, 2 * rows), lambda w: (w, 0, 0)),
        ],
        out_shape=[
            jax.ShapeDtypeStruct((windows * rows, width), bf16),
            jax.ShapeDtypeStruct((windows, pairs, 2 * rows), f32),
        ],
        scratch_shapes=[pltpu.VMEM((length, rows), jnp.int32)],
        cost_estimate=pl.CostEstimate(
            flops=8 * windows * rows * length * width,
            bytes_accessed=4 * windows * rows * length,
            transcendentals=windows * rows * length * 2 * pairs,
        ),
        name="attend",
    )(facts, queries, keys_values, keys_values, bins, table)


def attend_back(facts, queries, keys_values, bins, table, grads, logs, head_size):
    windows, rows, length = bins.shape
    width = queries.shape[1]
    pairs = width // (2 * head_size)
    return pl.pallas_call(
        functools.partial(attend_back_kernel, head_size, table.shape[1] // 2),
        grid=(windows,),
        in_specs=attention_specs(rows, length, width, table.shape)
        + [
            pl.BlockSpec((rows, width), lambda w: (w, 0)),
            pl.BlockSpec((1, pairs, 2 * rows), lambda w: (w, 0, 0)),
        ],
        out_specs=[
            pl.BlockSpec((rows, width), lambda w: (w, 0)),
            pl.BlockSpec((length, 2 * width), lambda w: (w, 0)),
            pl.BlockSpec((1, 2 * pairs, length, rows), lambda w: (w, 0, 0, 0)),
        ],
        out_shape=[
            jax.ShapeDtypeStruct((windows * rows, width), bf16),
            jax.ShapeDtypeStruct((windows * length, 2 * width), bf16),
            jax.ShapeDtypeStruct((windows, 2 * pairs, length, rows), bf16),
        ],
        scratch_shapes=[pltpu.VMEM((length, rows), jnp.int32)],
        cost_estimate=pl.CostEstimate(
            flops=20 * windows * rows * length * width,
            bytes_accessed=8 * windows * rows * length * pairs,
            transcendentals=windows * rows * length * 2 * pairs,
        ),
        name="attend_back",
    )(facts, queries, keys_values, keys_values, bins, table, grads, logs)


def bit_steps():
    win_bits = int(math.log2(lax.axis_size("win")))
    seq_bits = int(math.log2(lax.axis_size("seq")))
    return [("win", bit) for bit in range(win_bits)[::-1]] + [
        ("seq", bit) for bit in range(seq_bits)[::-1]
    ]


CORE = ("win", 0)


def my_bit(step):
    return lax.rem(lax.axis_index(step[0]) // (1 << step[1]), 2)


def partner(step):
    return {step[0]: lax.axis_index(step[0]) + (1 - 2 * my_bit(step)) * (1 << step[1])}


def greet():
    barrier = pltpu.get_barrier_semaphore()
    for step in bit_steps():
        pl.semaphore_signal(barrier, inc=1, device_id=partner(step), device_id_type=pl.DeviceIdType.MESH)
    pl.semaphore_wait(barrier, len(bit_steps()))


def remote(source, target, send_sem, recv_sem, step):
    return pltpu.make_async_remote_copy(
        src_ref=source,
        dst_ref=target,
        send_sem=send_sem,
        recv_sem=recv_sem,
        device_id=partner(step),
        device_id_type=pl.DeviceIdType.MESH,
    )


def each_block(shape, body):
    lead = shape[:-2]
    count = math.prod(lead)

    def one(flat, carry):
        index = []
        for size in lead[::-1]:
            index.append(lax.rem(flat, size))
            flat = flat // size
        body(tuple(index[::-1]))
        return carry

    if count == 1:
        body((0,) * len(lead))
    else:
        lax.fori_loop(0, count, one, 0)


class Flow:
    def __init__(self, rows, columns, chunks, flip):
        steps = bit_steps()
        win_steps = [step for step in steps if step[0] == "win" and step != CORE]
        self.seq_steps = [step for step in steps if step[0] == "seq"]
        self.far = win_steps if flip else win_steps[::-1]
        self.names = win_steps
        self.near = self.seq_steps[::-1]
        self.chunks = chunks
        self.width = columns // chunks
        self.share = rows // 2 ** len(steps)
        self.block = self.share * 2 ** len(self.seq_steps)
        self.columns = columns

    def view(self, grad):
        return grad.reshape((2,) * (len(self.far) + 1) + (self.block, self.columns))

    def scratch(self):
        chunks, width = (self.chunks, self.width)
        far, near = (len(self.far), len(self.near))
        shapes = [(2,) * far + (self.block, width)] * 2
        shapes += [(2,) * (far - 1 - i) + (self.block, width) for i in range(far)]
        shapes += [(2,) * near + (self.share, width)]
        shapes += [(2,) * (near - 1 - i) + (self.share, width) for i in range(near)]
        buffers = [pltpu.VMEM((chunks,) + shape, bf16) for shape in shapes]
        count = 1 + far + near
        return buffers + [
            pltpu.SemaphoreType.DMA((chunks,)),
            pltpu.SemaphoreType.DMA((count, chunks)),
            pltpu.SemaphoreType.DMA((count, chunks)),
        ]

    def bind(self, grad, out, scratch):
        self.grad, self.out = grad, out
        far, near = (len(self.far), len(self.near))
        self.mine = scratch[0]
        self.first = scratch[1]
        self.far_bufs = list(scratch[2 : 2 + far])
        self.turn = scratch[2 + far]
        self.near_bufs = list(scratch[3 + far : 3 + far + near])
        self.local_sem, self.send_sem, self.recv_sem = scratch[3 + far + near :]

    def piece(self, bit, chunk):
        index = (slice(None),) * len(self.far) + (bit, slice(None))
        return self.grad.at[index + (pl.ds(pl.multiple_of(chunk * self.width, 128), self.width),)]

    def local_copy(self, chunk):
        return pltpu.make_async_copy(
            self.piece(my_bit(CORE), chunk), self.mine.at[chunk], self.local_sem.at[chunk]
        )

    def copy(self, stage, chunk):
        send, recv = (self.send_sem.at[stage, chunk], self.recv_sem.at[stage, chunk])
        far = len(self.far)
        if stage == 0:
            return remote(
                self.piece(1 - my_bit(CORE), chunk), self.first.at[chunk], send, recv, CORE
            )
        if stage <= far:
            step = self.far[stage - 1]
            source = ([self.first] + self.far_bufs)[stage - 1]
            target = self.far_bufs[stage - 1]
            axis = self.axis_of(step, self.far[: stage - 1], self.names)
        else:
            at = stage - 1 - far
            step = self.near[at]
            source = ([self.turn] + self.near_bufs)[at]
            target = self.near_bufs[at]
            axis = self.axis_of(step, self.near[:at], self.seq_steps)
        index = (chunk,) + (slice(None),) * axis + (1 - my_bit(step),)
        return remote(source.at[index], target.at[chunk], send, recv, step)

    def axis_of(self, step, gone, names):
        return [name for name in names if name not in gone].index(step)

    def stages(self):
        return 2 + len(self.far) + len(self.near)

    def run(self, stage, chunk):
        far, near = (len(self.far), len(self.near))
        if stage == 0:
            self.local_copy(chunk).start()
            self.copy(0, chunk).start()
            return
        self.copy(stage - 1, chunk).wait_recv()
        if stage == 1:
            self.local_copy(chunk).wait()
            shape = self.first.shape[1:]

            def add_first(index):
                at = (chunk,) + index
                self.first[at] = (self.first[at].astype(f32) + self.mine[at].astype(f32)).astype(bf16)

            each_block(shape, add_first)
        elif stage < 1 + far:
            target = self.far_bufs[stage - 2]
            source = ([self.first] + self.far_bufs)[stage - 2]
            self.add_half(target, source, self.far, self.names, stage - 2, chunk)
        elif stage == 1 + far:
            step = self.far[-1]
            source = ([self.first] + self.far_bufs)[far - 1]
            target = self.far_bufs[far - 1]
            total = target[chunk].astype(f32) + source[chunk, my_bit(step)].astype(f32)
            total = total.astype(bf16)
            count = 2**near
            for owner in range(count):
                at, rest = ((), owner)
                for _ in range(near):
                    at = (rest % 2,) + at
                    rest = rest // 2
                self.turn[(chunk,) + at] = total[owner * self.share : (owner + 1) * self.share]
        elif stage < 1 + far + near:
            at = stage - 2 - far
            source = ([self.turn] + self.near_bufs)[at]
            self.add_half(self.near_bufs[at], source, self.near, self.seq_steps, at, chunk)
        else:
            source = ([self.turn] + self.near_bufs)[near - 1]
            kept = source[chunk, my_bit(self.near[-1])]
            total = self.near_bufs[near - 1][chunk].astype(f32) + kept.astype(f32)
            self.out[:, pl.ds(pl.multiple_of(chunk * self.width, 128), self.width)] = total
        if stage < 1 + far + near:
            self.copy(stage, chunk).start()

    def add_half(self, target, source, steps, names, at, chunk):
        step = steps[at]
        axis = self.axis_of(step, steps[:at], names)
        bit = my_bit(step)

        def add(index):
            from_at = (chunk,) + index[:axis] + (bit,) + index[axis:]
            to_at = (chunk,) + index
            target[to_at] = (target[to_at].astype(f32) + source[from_at].astype(f32)).astype(bf16)

        each_block(target.shape[1:], add)

    def drain(self, chunk):
        for stage in range(self.stages() - 1):
            self.copy(stage, chunk).wait_send()


def reduce_kernel(flows, *refs):
    count = len(flows)
    scratch = list(refs[2 * count :])
    for at, flow in enumerate(flows):
        size = len(flow.scratch())
        flow.bind(refs[at], refs[count + at], scratch[:size])
        scratch = scratch[size:]
    chunks = flows[0].chunks
    stages = flows[0].stages()
    greet()
    order = [1, 0] + list(range(2, stages))

    def step(at, carry):
        for stage in order:
            chunk = at - stage

            @pl.when((chunk >= 0) & (chunk < chunks))
            def _(stage=stage, chunk=chunk):
                for flow in flows:
                    flow.run(stage, chunk)

        return carry

    lax.fori_loop(0, chunks + stages - 1, step, 0)

    def finish(chunk, carry):
        for flow in flows:
            flow.drain(chunk)
        return carry

    lax.fori_loop(0, chunks, finish, 0)


def reduce_grads(grads, chunks, flips, name, collective_id):
    flows = [Flow(g.shape[0], g.shape[1], chunks, flip) for g, flip in zip(grads, flips)]
    scratch = []
    for flow in flows:
        scratch += flow.scratch()
    return pl.pallas_call(
        functools.partial(reduce_kernel, flows),
        in_specs=[pl.BlockSpec(memory_space=pl.ANY)] * len(flows),
        out_specs=[pl.BlockSpec(memory_space=pltpu.VMEM)] * len(flows),
        out_shape=[jax.ShapeDtypeStruct((flow.share, flow.columns), f32) for flow in flows],
        scratch_shapes=scratch,
        compiler_params=pltpu.CompilerParams(
            collective_id=collective_id, has_side_effects=True, vmem_limit_bytes=48 * 2**20
        ),
        cost_estimate=pl.CostEstimate(
            flops=0, bytes_accessed=200 * 2**20, transcendentals=0
        ),
        name=name,
    )(*[flow.view(grad) for flow, grad in zip(flows, grads)])


def sum_seq(values):
    for bit in range(int(math.log2(lax.axis_size("seq")))):
        values = values + exchange(values, ("seq", bit))
    return values


def exchange(values, step):
    size = lax.axis_size(step[0])
    return lax.ppermute(values, step[0], [(i, i ^ (1 << step[1])) for i in range(size)])


def gather_win(values):
    out = values[None]
    for bit in range(int(math.log2(lax.axis_size("win")))):
        step = ("win", bit)
        got = exchange(out, step)
        low = my_bit(step) == 0
        out = jnp.concatenate([jnp.where(low, out, got), jnp.where(low, got, out)], axis=0)
    return out


def three_parts(values):
    parts = []
    for _ in range(3):
        part = lax.reduce_precision(values, 8, 7)
        parts.append(part.astype(bf16))
        values = values - part
    return parts


def per_device(
    tokens,
    cotangent,
    noise_times,
    cath_ids,
    chain_start,
    distance_bins,
    class_table,
    ada_weight,
    qkv_weight,
    out_weight,
    pair_table,
    pair_weight,
    gate_weight,
    up_weight,
    down_weight,
):
    windows, row_count, width = tokens.shape
    length = distance_bins.shape[2]
    head_count = pair_weight.shape[1]
    head_size = width // head_count
    table_rows = pair_table.shape[0]
    bin_count = table_rows // 2
    classes = class_table.shape[0]
    total_rows = windows * row_count
    win_count = lax.axis_size("win")
    seq_count = lax.axis_size("seq")
    devices = win_count * seq_count
    owner = lax.axis_index("win") * seq_count + lax.axis_index("seq")
    tokens_all = lax.all_gather(tokens, "seq", axis=1, tiled=True)
    class_onehot = (cath_ids[:, None] == jnp.arange(classes, dtype=jnp.int32)[None, :]).astype(f32)
    pre_cond = jnp.dot(
        class_onehot, class_table.astype(f32), precision=highest
    ) + time_embed(noise_times, width)
    cond_sig = jax.nn.sigmoid(pre_cond)
    condition = pre_cond * cond_sig
    modulation = dot(jnp.concatenate(three_parts(condition), axis=0), ada_weight)
    modulation = jnp.sum(modulation.reshape(3, windows, 6, width), axis=0)
    shift_attn = modulation[:, 0][:, None, :]
    scale_attn = modulation[:, 1][:, None, :]
    gate_attn = modulation[:, 2][:, None, :]
    shift_ffn = modulation[:, 3][:, None, :]
    scale_ffn = modulation[:, 4][:, None, :]
    gate_ffn = modulation[:, 5][:, None, :]
    table_bias = dot(pair_table, pair_weight).astype(bf16)
    facts = jnp.concatenate(
        [chain_start, jnp.full((1,), lax.axis_index("seq") * row_count, jnp.int32)]
    )
    table = table_bias.astype(f32).T
    tokens_float = tokens.astype(f32)
    normed_x, inv_x = layer_norm_parts(tokens_float)
    attn_in = (normed_x * (1.0 + scale_attn) + shift_attn).astype(bf16).reshape(total_rows, width)
    normed_all, _ = layer_norm_parts(tokens_all.astype(f32))
    attn_in_all = (
        (normed_all * (1.0 + scale_attn) + shift_attn).astype(bf16).reshape(windows * length, width)
    )
    queries = dot(attn_in, qkv_weight[:, :width]).astype(bf16)
    keys_values = dot(attn_in_all, qkv_weight[:, width:]).astype(bf16)
    attn_mixed, log_totals = attend(facts, queries, keys_values, distance_bins, table, head_size)
    attn_out = dot(attn_mixed, out_weight).reshape(windows, row_count, width)
    gate_attn_sig = jax.nn.sigmoid(gate_attn)
    hidden_state = tokens_float + gate_attn_sig * attn_out
    normed_h, inv_h = layer_norm_parts(hidden_state)
    ffn_in = (normed_h * (1.0 + scale_ffn) + shift_ffn).astype(bf16).reshape(total_rows, width)
    gate_val = dot(ffn_in, gate_weight)
    up_val = dot(ffn_in, up_weight)
    gate_sig = jax.nn.sigmoid(gate_val)
    silu_gate = gate_val * gate_sig
    ffn_hidden = (silu_gate * up_val).astype(bf16)
    gate_ffn_sig = jax.nn.sigmoid(gate_ffn)
    grad_layer = cotangent.astype(f32)
    grad_ffn = (gate_ffn_sig * grad_layer).astype(bf16).reshape(total_rows, width)
    grad_down = dot_tn(ffn_hidden, grad_ffn).astype(bf16)
    ffn_out = dot(ffn_hidden, down_weight).reshape(windows, row_count, width)
    layer_out = (hidden_state + gate_ffn_sig * ffn_out).astype(bf16)
    grad_gate_ffn = jnp.sum(grad_layer * ffn_out * gate_ffn_sig * (1.0 - gate_ffn_sig), axis=1)
    grad_hidden_ffn = dot_nt(grad_ffn, down_weight)
    grad_up_val = (grad_hidden_ffn * silu_gate).astype(bf16)
    grad_gate_val = (
        grad_hidden_ffn * up_val * gate_sig * (1.0 + gate_val * (1.0 - gate_sig))
    ).astype(bf16)
    grad_gate = dot_tn(ffn_in, grad_gate_val).astype(bf16)
    grad_up = dot_tn(ffn_in, grad_up_val).astype(bf16)
    grad_ffn_in = dot_nt(grad_gate_val, gate_weight) + dot_nt(grad_up_val, up_weight)
    grad_ffn_in = grad_ffn_in.reshape(windows, row_count, width)
    grad_scale_ffn = jnp.sum(grad_ffn_in * normed_h, axis=1)
    grad_shift_ffn = jnp.sum(grad_ffn_in, axis=1)
    grad_hidden = grad_layer + norm_back(grad_ffn_in * (1.0 + scale_ffn), normed_h, inv_h)
    grad_attn_out = (gate_attn_sig * grad_hidden).astype(bf16).reshape(total_rows, width)
    grad_gate_attn = jnp.sum(grad_hidden * attn_out * gate_attn_sig * (1.0 - gate_attn_sig), axis=1)
    grad_out = dot_tn(attn_mixed, grad_attn_out).astype(bf16)
    grad_mixed = dot_nt(grad_attn_out, out_weight).astype(bf16)

    grad_query, grad_kv, grad_scores = attend_back(
        facts, queries, keys_values, distance_bins, table, grad_mixed, log_totals, head_size
    )
    row_first = lax.axis_index("seq") * row_count + jnp.arange(row_count)[None, None, :] < chain_start[:, None, None]
    key_first = jnp.arange(length)[None, :, None] < chain_start[:, None, None]
    index_back = jnp.swapaxes(distance_bins, 1, 2) + bin_count * (row_first == key_first).astype(jnp.int32)
    pair_onehot = (
        index_back[:, None, :, :] == jnp.arange(table_rows, dtype=jnp.int32)[None, :, None, None]
    ).astype(bf16)
    grad_table = jnp.einsum("whji,wkji->kh", grad_scores, pair_onehot, preferred_element_type=f32)
    grad_in_part = dot_nt(grad_kv, qkv_weight[:, width:]).astype(bf16)
    grad_in_far = lax.psum_scatter(
        grad_in_part.reshape(windows, length, width), "seq", scatter_dimension=1, tiled=True
    )
    grad_q_weight = dot_tn(attn_in, grad_query).astype(bf16)
    grad_kv_weight = dot_tn(attn_in_all, grad_kv).astype(bf16)
    owned_gate, owned_up, owned_down, owned_kv, owned_q, owned_out = reduce_grads(
        [grad_gate, grad_up, grad_down, grad_kv_weight, grad_q_weight, grad_out],
        6,
        [False, True, False, True, True, True],
        "reduce_all",
        1,
    )
    grad_attn_in = dot_nt(grad_query, qkv_weight[:, :width]).reshape(
        windows, row_count, width
    ) + grad_in_far.astype(f32)
    grad_scale_attn = jnp.sum(grad_attn_in * normed_x, axis=1)
    grad_shift_attn = jnp.sum(grad_attn_in, axis=1)
    grad_tokens = (
        grad_hidden + norm_back(grad_attn_in * (1.0 + scale_attn), normed_x, inv_x)
    ).astype(bf16)
    early_mod = jnp.stack([grad_gate_attn, grad_shift_ffn, grad_scale_ffn, grad_gate_ffn], axis=0)
    early_mod = sum_seq(early_mod.reshape(4 * windows, width))
    onehot_rows = jnp.pad(class_onehot, ((0, 0), (0, width - classes)))
    early_all = gather_win(jnp.concatenate([early_mod, pre_cond, onehot_rows], axis=0))
    late_mod = jnp.concatenate([grad_shift_attn, grad_scale_attn], axis=0)
    table_size = table_rows * head_count
    late = jnp.concatenate([late_mod, grad_table.reshape(table_size // width, width)], axis=0)
    late_all = gather_win(sum_seq(late))
    mod_all = jnp.concatenate(
        [
            late_all[:, : 2 * windows].reshape(win_count, 2, windows, width),
            early_all[:, : 4 * windows].reshape(win_count, 4, windows, width),
        ],
        axis=1,
    )
    mod_all = jnp.swapaxes(mod_all, 1, 2).reshape(win_count * windows, 6 * width)
    table_all = jnp.sum(late_all[:, 2 * windows :], axis=0).reshape(table_rows, head_count)
    facts_all = early_all[:, 4 * windows :].reshape(win_count, 2, windows, width)
    pre_all = facts_all[:, 0].reshape(win_count * windows, width)
    onehot_all = facts_all[:, 1].reshape(win_count * windows, width)
    ada_rows = width // devices
    sig_all = jax.nn.sigmoid(pre_all)
    condition_rows = lax.dynamic_slice_in_dim(pre_all * sig_all, owner * ada_rows, ada_rows, 1)
    owned_ada = lax.dot_general(
        condition_rows, mod_all, (((0,), (0,)), ((), ())), precision=highest
    )
    class_share = classes * width // devices
    per_class = width // class_share
    column_at = (owner % per_class) * class_share
    pre_cols = lax.dynamic_slice_in_dim(pre_all, column_at, class_share, 1)
    sig_cols = lax.dynamic_slice_in_dim(sig_all, column_at, class_share, 1)
    ada_cols = lax.dynamic_slice_in_dim(ada_weight, column_at, class_share, 0).astype(f32)
    grad_cond = lax.dot_general(mod_all, ada_cols, (((1,), (1,)), ((), ())), precision=highest)
    grad_pre = grad_cond * sig_cols * (1.0 + pre_cols * (1.0 - sig_cols))
    onehot_mine = lax.dynamic_slice_in_dim(onehot_all, owner // per_class, 1, 1)
    owned_class = jnp.sum(grad_pre * onehot_mine, axis=0)
    grad_pair_table = jnp.dot(table_all, pair_weight.astype(f32).T, precision=highest).reshape(-1)
    grad_pair_weight = jnp.dot(pair_table.astype(f32).T, table_all, precision=highest).reshape(-1)
    table_size = grad_pair_table.shape[0] // devices
    weight_size = grad_pair_weight.shape[0] // devices
    owned_pair_table = lax.dynamic_slice_in_dim(grad_pair_table, owner * table_size, table_size)
    owned_pair_weight = lax.dynamic_slice_in_dim(grad_pair_weight, owner * weight_size, weight_size)
    return (
        layer_out,
        grad_tokens,
        owned_class,
        owned_ada.reshape(-1),
        jnp.concatenate([owned_q, owned_kv], axis=-1).reshape(-1),
        owned_out.reshape(-1),
        owned_pair_table,
        owned_pair_weight,
        owned_gate.reshape(-1),
        owned_up.reshape(-1),
        owned_down.reshape(-1),
    )


def solution(mesh):
    rows = P("win", "seq", None)
    flat = P(("win", "seq"))
    placed = (rows, rows, P("win"), P("win"), P("win"), rows) + (P(),) * 9
    return jax.shard_map(
        per_device, mesh=mesh, in_specs=placed, out_specs=(rows, rows) + (flat,) * 9, check_vma=False
    )
```

```python
import functools
import math

import jax
import jax.numpy as jnp
from jax import lax
from jax.experimental import pallas as pl
from jax.experimental.pallas import tpu as pltpu
from jax.sharding import PartitionSpec as P

highest = lax.Precision.HIGHEST
norm_eps = 1e-06
f32 = jnp.float32
bf16 = jnp.bfloat16


def layer_norm_parts(values):
    centered = values - jnp.mean(values, axis=-1, keepdims=True)
    variance = jnp.mean(centered * centered, axis=-1, keepdims=True)
    inv_std = lax.rsqrt(variance + norm_eps)
    return (centered * inv_std, inv_std)


def norm_back(grad_normed, normed, inv_std):
    first_mean = jnp.mean(grad_normed, axis=-1, keepdims=True)
    second_mean = jnp.mean(grad_normed * normed, axis=-1, keepdims=True)
    return (grad_normed - first_mean - normed * second_mean) * inv_std


def time_embed(noise_times, model_width):
    half_width = model_width // 2
    frequency = jnp.exp(
        -math.log(10000.0) * jnp.arange(half_width).astype(f32) / half_width
    )
    angles = 1000.0 * noise_times[:, None] * frequency[None, :]
    return jnp.concatenate([jnp.sin(angles), jnp.cos(angles)], axis=-1)


def dot(a, b):
    return jnp.dot(a, b, preferred_element_type=f32)


def dot_nt(a, b):
    return lax.dot_general(a, b, (((1,), (1,)), ((), ())), preferred_element_type=f32)


def dot_tn(a, b):
    return lax.dot_general(a, b, (((0,), (0,)), ((), ())), preferred_element_type=f32)


def pair_halves(values, head_size):
    lane = lax.broadcasted_iota(jnp.int32, values.shape, 1)
    zero = jnp.zeros_like(values)
    return jnp.concatenate(
        [jnp.where(lane < head_size, values, zero), jnp.where(lane >= head_size, values, zero)], axis=0
    )


def pair_diagonal(values, head_size, rows):
    return jnp.concatenate([values[:head_size, :rows], values[head_size:, rows:]], axis=0).T


def attend_kernel(
    head_size, bin_count, facts_ref, q_ref, k_ref, v_ref, bins_ref, table_ref, out_ref, probs_ref, index_ref
):
    rows, width = q_ref.shape
    head_scale = 1.0 / math.sqrt(head_size)
    start = facts_ref[pl.program_id(0)]
    offset = facts_ref[pl.num_programs(0)]
    bins = bins_ref[0].T
    key_first = lax.broadcasted_iota(jnp.int32, bins.shape, 0) < start
    row_first = lax.broadcasted_iota(jnp.int32, bins.shape, 1) + offset < start
    index_ref[0] = bins + jnp.where(key_first == row_first, bin_count, 0)

    def one_pair(pair, carry):
        cols = pl.ds(pl.multiple_of(pair * 2 * head_size, 2 * head_size), 2 * head_size)
        index = index_ref[0]
        biases = []
        for head in range(2):
            entries = jnp.broadcast_to(table_ref[pl.ds(2 * pair + head, 1), :], index.shape)
            biases.append(jnp.take_along_axis(entries, index, axis=1, mode="promise_in_bounds"))
        q_pair = pair_halves(q_ref[:, cols] * head_scale, head_size)
        scores = dot_nt(k_ref[:, cols], q_pair) + jnp.concatenate(biases, axis=1)
        top = jnp.max(scores, axis=0, keepdims=True)
        raised = jnp.exp(scores - top)
        total = jnp.sum(raised, axis=0, keepdims=True)
        probs = (raised * (1.0 / total)).astype(bf16)
        mixed = dot(v_ref[:, cols].T, probs)
        out_ref[:, cols] = pair_diagonal(mixed, head_size, rows).astype(bf16)
        probs_ref[0, pair] = probs
        return carry

    lax.fori_loop(0, width // (2 * head_size), one_pair, 0)


def attend(facts, queries, keys_values, bins, table, head_size):
    windows, rows, length = bins.shape
    width = queries.shape[1]
    pairs = width // (2 * head_size)
    return pl.pallas_call(
        functools.partial(attend_kernel, head_size, table.shape[1] // 2),
        grid=(windows,),
        in_specs=[
            pl.BlockSpec(memory_space=pltpu.SMEM),
            pl.BlockSpec((rows, width), lambda w: (w, 0)),
            pl.BlockSpec((length, width), lambda w: (w, 0)),
            pl.BlockSpec((length, width), lambda w: (w, 1)),
            pl.BlockSpec((1, rows, length), lambda w: (w, 0, 0)),
            pl.BlockSpec(table.shape, lambda w: (0, 0)),
        ],
        out_specs=[
            pl.BlockSpec((rows, width), lambda w: (w, 0)),
            pl.BlockSpec((1, pairs, length, 2 * rows), lambda w: (w, 0, 0, 0)),
            pl.BlockSpec((1, length, rows), lambda w: (w, 0, 0)),
        ],
        out_shape=[
            jax.ShapeDtypeStruct((windows * rows, width), bf16),
            jax.ShapeDtypeStruct((windows, pairs, length, 2 * rows), bf16),
            jax.ShapeDtypeStruct((windows, length, rows), jnp.int32),
        ],
        cost_estimate=pl.CostEstimate(
            flops=8 * windows * rows * length * width,
            bytes_accessed=4 * windows * rows * length,
            transcendentals=windows * rows * length * 2 * pairs,
        ),
        name="attend",
    )(facts, queries, keys_values, keys_values, bins, table)


def bit_steps():
    win_bits = int(math.log2(lax.axis_size("win")))
    seq_bits = int(math.log2(lax.axis_size("seq")))
    return [("win", bit) for bit in range(win_bits)[::-1]] + [
        ("seq", bit) for bit in range(seq_bits)[::-1]
    ]


CORE = ("win", 0)


def my_bit(step):
    return lax.rem(lax.axis_index(step[0]) // (1 << step[1]), 2)


def partner(step):
    return {step[0]: lax.axis_index(step[0]) + (1 - 2 * my_bit(step)) * (1 << step[1])}


def greet():
    barrier = pltpu.get_barrier_semaphore()
    for step in bit_steps():
        pl.semaphore_signal(barrier, inc=1, device_id=partner(step), device_id_type=pl.DeviceIdType.MESH)
    pl.semaphore_wait(barrier, len(bit_steps()))


def remote(source, target, send_sem, recv_sem, step):
    return pltpu.make_async_remote_copy(
        src_ref=source,
        dst_ref=target,
        send_sem=send_sem,
        recv_sem=recv_sem,
        device_id=partner(step),
        device_id_type=pl.DeviceIdType.MESH,
    )


def each_block(shape, body):
    lead = shape[:-2]
    count = math.prod(lead)

    def one(flat, carry):
        index = []
        for size in lead[::-1]:
            index.append(lax.rem(flat, size))
            flat = flat // size
        body(tuple(index[::-1]))
        return carry

    if count == 1:
        body((0,) * len(lead))
    else:
        lax.fori_loop(0, count, one, 0)


class Flow:
    def __init__(self, rows, columns, chunks, flip, offset):
        steps = bit_steps()
        win_steps = [step for step in steps if step[0] == "win" and step != CORE]
        self.seq_steps = [step for step in steps if step[0] == "seq"]
        self.far = win_steps if flip else win_steps[::-1]
        self.names = win_steps
        self.near = self.seq_steps[::-1]
        self.chunks = chunks
        self.offset = offset
        self.width = columns // chunks
        self.share = rows // 2 ** len(steps)
        self.block = self.share * 2 ** len(self.seq_steps)
        self.columns = columns

    def view(self, grad):
        return grad.reshape((2,) * (len(self.far) + 1) + (self.block, self.columns))

    def scratch(self):
        chunks, width = (self.chunks, self.width)
        far, near = (len(self.far), len(self.near))
        shapes = [(2,) * far + (self.block, width)] * 2
        shapes += [(2,) * (far - 1 - i) + (self.block, width) for i in range(far)]
        shapes += [(2,) * near + (self.share, width)]
        shapes += [(2,) * (near - 1 - i) + (self.share, width) for i in range(near)]
        buffers = [pltpu.VMEM((chunks if at else 2,) + shape, bf16) for at, shape in enumerate(shapes)]
        count = 1 + far + near
        return buffers + [
            pltpu.SemaphoreType.DMA((chunks,)),
            pltpu.SemaphoreType.DMA((count, chunks)),
            pltpu.SemaphoreType.DMA((count, chunks)),
        ]

    def bind(self, grad, out, scratch):
        self.grad, self.out = grad, out
        far, near = (len(self.far), len(self.near))
        self.mine = scratch[0]
        self.first = scratch[1]
        self.far_bufs = list(scratch[2 : 2 + far])
        self.turn = scratch[2 + far]
        self.near_bufs = list(scratch[3 + far : 3 + far + near])
        self.local_sem, self.send_sem, self.recv_sem = scratch[3 + far + near :]

    def piece(self, bit, chunk):
        index = (slice(None),) * len(self.far) + (bit, slice(None))
        return self.grad.at[index + (pl.ds(pl.multiple_of(chunk * self.width, 128), self.width),)]

    def local_copy(self, chunk):
        return pltpu.make_async_copy(
            self.piece(my_bit(CORE), chunk), self.mine.at[lax.rem(chunk, 2)], self.local_sem.at[chunk]
        )

    def copy(self, stage, chunk):
        send, recv = (self.send_sem.at[stage, chunk], self.recv_sem.at[stage, chunk])
        far = len(self.far)
        if stage == 0:
            return remote(
                self.piece(1 - my_bit(CORE), chunk), self.first.at[chunk], send, recv, CORE
            )
        if stage <= far:
            step = self.far[stage - 1]
            source = ([self.first] + self.far_bufs)[stage - 1]
            target = self.far_bufs[stage - 1]
            axis = self.axis_of(step, self.far[: stage - 1], self.names)
        else:
            at = stage - 1 - far
            step = self.near[at]
            source = ([self.turn] + self.near_bufs)[at]
            target = self.near_bufs[at]
            axis = self.axis_of(step, self.near[:at], self.seq_steps)
        index = (chunk,) + (slice(None),) * axis + (1 - my_bit(step),)
        return remote(source.at[index], target.at[chunk], send, recv, step)

    def axis_of(self, step, gone, names):
        return [name for name in names if name not in gone].index(step)

    def stages(self):
        return 2 + len(self.far) + len(self.near)

    def run(self, stage, chunk):
        far, near = (len(self.far), len(self.near))
        if stage == 0:
            self.local_copy(chunk).start()
            self.copy(0, chunk).start()
            return
        self.copy(stage - 1, chunk).wait_recv()
        if stage == 1:
            self.local_copy(chunk).wait()
            shape = self.first.shape[1:]

            def add_first(index):
                at = (chunk,) + index
                kept = self.mine[(lax.rem(chunk, 2),) + index].astype(f32)
                self.first[at] = (self.first[at].astype(f32) + kept).astype(bf16)

            each_block(shape, add_first)
        elif stage < 1 + far:
            target = self.far_bufs[stage - 2]
            source = ([self.first] + self.far_bufs)[stage - 2]
            self.add_half(target, source, self.far, self.names, stage - 2, chunk)
        elif stage == 1 + far:
            step = self.far[-1]
            source = ([self.first] + self.far_bufs)[far - 1]
            target = self.far_bufs[far - 1]
            total = target[chunk].astype(f32) + source[chunk, my_bit(step)].astype(f32)
            total = total.astype(bf16)
            count = 2**near
            for owner in range(count):
                at, rest = ((), owner)
                for _ in range(near):
                    at = (rest % 2,) + at
                    rest = rest // 2
                self.turn[(chunk,) + at] = total[owner * self.share : (owner + 1) * self.share]
        elif stage < 1 + far + near:
            at = stage - 2 - far
            source = ([self.turn] + self.near_bufs)[at]
            self.add_half(self.near_bufs[at], source, self.near, self.seq_steps, at, chunk)
        else:
            source = ([self.turn] + self.near_bufs)[near - 1]
            kept = source[chunk, my_bit(self.near[-1])]
            total = self.near_bufs[near - 1][chunk].astype(f32) + kept.astype(f32)
            self.out[:, pl.ds(pl.multiple_of(chunk * self.width, 128), self.width)] = total
        if stage < 1 + far + near:
            self.copy(stage, chunk).start()

    def add_half(self, target, source, steps, names, at, chunk):
        step = steps[at]
        axis = self.axis_of(step, steps[:at], names)
        bit = my_bit(step)

        def add(index):
            from_at = (chunk,) + index[:axis] + (bit,) + index[axis:]
            to_at = (chunk,) + index
            target[to_at] = (target[to_at].astype(f32) + source[from_at].astype(f32)).astype(bf16)

        each_block(target.shape[1:], add)

    def drain(self, chunk):
        for stage in range(self.stages() - 1):
            self.copy(stage, chunk).wait_send()


class Load:
    def __init__(self, source, target, sem):
        self.target = target
        self.copy = pltpu.make_async_copy(source, target, sem)


class SmallGather:
    def __init__(self, mine, halves, gathered, send_sem, recv_sem):
        self.mine, self.halves, self.gathered = mine, halves, gathered
        self.send_sem, self.recv_sem = send_sem, recv_sem
        self.steps = bit_steps()[::-1]
        self.seq_count = len([step for step in self.steps if step[0] == "seq"])

    def copy(self, at):
        step = self.steps[at]
        if at < self.seq_count:
            source, target = self.mine.at[at], self.halves.at[at]
        else:
            size = 1 << step[1]
            here = lax.axis_index("win")
            block = pl.ds(here - lax.rem(here, size), size)
            source = target = self.gathered.at[block]
        return remote(source, target, self.send_sem.at[at], self.recv_sem.at[at], step)

    def run(self, at):
        if at > 0:
            self.copy(at - 1).wait_recv()
            if at <= self.seq_count:
                total = self.mine[at - 1] + self.halves[at - 1]
                if at < self.seq_count:
                    self.mine[at] = total
                else:
                    self.gathered[lax.axis_index("win")] = total
        if at < len(self.steps):
            self.copy(at).start()

    def drain(self):
        for at in range(len(self.steps)):
            self.copy(at).wait_send()


def norm_rows(values):
    centered = values - jnp.mean(values, axis=-1, keepdims=True)
    inv_std = lax.rsqrt(jnp.mean(centered * centered, axis=-1, keepdims=True) + norm_eps)
    return (centered * inv_std, inv_std)


def backward_kernel(flows, sizes, *refs):
    windows, rows, length, head_size = sizes
    refs = list(refs)

    def take(count):
        taken = refs[:count]
        del refs[:count]
        return taken

    grads = take(4)
    sources = take(9)
    scale_ref, early_ref = take(2)
    shares = take(6)
    tokens_out, small_out = take(2)
    targets = take(9)
    (load_sem,) = take(1)
    grad_q, grad_kv, grad_scores, q_weight, kv_weight, own_in = take(6)
    far_in, far_half, far_own, far_send, far_recv = take(5)
    (table_sum,) = take(1)
    small = SmallGather(*take(5))
    (small_sem,) = take(1)
    for flow, grad, share in zip(flows, grads + [q_weight, kv_weight], shares):
        flow.bind(grad, share, take(len(flow.scratch())))
    loads = [Load(s, t, load_sem.at[at]) for at, (s, t) in enumerate(zip(sources, targets))]
    q_ref, kv_ref, probs_ref, grad_ref, in_ref, weight_ref, index_ref, tokens_ref, hidden_ref = targets
    width = q_ref.shape[1]
    head_scale = 1.0 / math.sqrt(head_size)
    heads = width // head_size
    seq_steps = bit_steps()[::-1][: small.seq_count]
    for load in loads:
        load.copy.start()
    greet()

    def attend_back(window):
        rows_at = pl.ds(pl.multiple_of(window * rows, rows), rows)
        keys_at = pl.ds(pl.multiple_of(window * length, length), length)

        def one_pair(pair, carry):
            start = pl.multiple_of(pair * 2 * head_size, 2 * head_size)
            cols = pl.ds(start, 2 * head_size)
            v_cols = pl.ds(width + start, 2 * head_size)
            q_pair = pair_halves(q_ref[rows_at, cols] * head_scale, head_size)
            g_pair = pair_halves(grad_ref[rows_at, cols], head_size)
            probs = probs_ref[window, pair]
            grad_kv[keys_at, v_cols] = dot(probs, g_pair).astype(bf16)
            grad_probs = dot_nt(kv_ref[keys_at, v_cols], g_pair)
            probs = probs.astype(f32)
            delta = jnp.sum(probs * grad_probs, axis=0, keepdims=True)
            scores = (probs * (grad_probs - delta)).astype(bf16)
            grad_kv[keys_at, cols] = dot(scores, q_pair).astype(bf16)
            back = dot(kv_ref[keys_at, cols].T, scores)
            grad_q[rows_at, cols] = (pair_diagonal(back, head_size, rows) * head_scale).astype(bf16)
            grad_scores[window, 2 * pair] = scores[:, :rows]
            grad_scores[window, 2 * pair + 1] = scores[:, rows:]
            return carry

        lax.fori_loop(0, heads // 2, one_pair, 0)

    def split_rows(target, values, cols):
        lead = target.shape[:-2]
        block = target.shape[-2]
        for at in range(math.prod(lead)):
            index, rest = ((), at)
            for size in lead[::-1]:
                index = (rest % size,) + index
                rest = rest // size
            target[index + (slice(None), cols)] = values[at * block : (at + 1) * block].astype(bf16)

    def project_back():
        def one_window(window, carry):
            keys_at = pl.ds(pl.multiple_of(window * length, length), length)
            far = dot_nt(grad_kv[keys_at, :], weight_ref[:, width:]).astype(bf16)
            split_owner(far, window)
            return carry

        def split_owner(far, window):
            rows_at = pl.ds(pl.multiple_of(window * rows, rows), rows)
            for owner in range(length // rows):
                index, rest = ((), owner)
                for _ in seq_steps:
                    index = (rest % 2,) + index
                    rest = rest // 2
                far_in[index + (rows_at,)] = far[owner * rows : (owner + 1) * rows]

        lax.fori_loop(0, windows, one_window, 0)
        far_copy(0).start()
        own_in[...] = dot_nt(grad_q[...], weight_ref[:, :width])

    def weight_grads():
        here = lax.axis_index("seq") * rows
        own = [in_ref[pl.ds(pl.multiple_of(w * length + here, rows), rows), :] for w in range(windows)]
        split_rows(q_weight, dot(jnp.concatenate(own, axis=0).T, grad_q[...]), slice(None))
        turned = in_ref[...].T
        step = 512
        for at in range(2 * width // step):
            cols = slice(at * step, (at + 1) * step)
            split_rows(kv_weight, dot(turned, grad_kv[:, cols]), cols)

    far_bufs = [far_in] + [far_half, far_own][-small.seq_count :]

    def far_copy(at):
        step = seq_steps[at]
        index = (slice(None),) * (small.seq_count - 1 - at) + (1 - my_bit(step),)
        return remote(
            far_bufs[at].at[index], far_bufs[at + 1], far_send.at[at], far_recv.at[at], step
        )

    def far_add(at):
        far_copy(at).wait_recv()
        step = seq_steps[at]
        bit = my_bit(step)
        target, source = far_bufs[at + 1], far_bufs[at]
        lead = target.shape[:-2]
        for flat in range(math.prod(lead)):
            for window in range(windows):
                index = ((flat,) if lead else ()) + (pl.ds(window * rows, rows),)
                kept = source[index[:-1] + (bit,) + index[-1:]].astype(f32)
                target[index] = (target[index].astype(f32) + kept).astype(bf16)
        if at + 1 < small.seq_count:
            far_copy(at + 1).start()

    def table_back(window):
        group = 16
        entries = table_sum.shape[1]

        def one_group(at, carry):
            keys = pl.ds(pl.multiple_of(at * group, group), group)
            scores = grad_scores[window, :, keys, :].astype(f32)
            scores = jnp.concatenate([scores, jnp.zeros((16 - heads, group, rows), f32)], axis=0)
            scores = jnp.swapaxes(scores, 0, 1).astype(bf16)
            index = index_ref[window, keys, :]
            spot = lax.broadcasted_iota(jnp.int32, (entries, rows), 0)
            total = jnp.zeros((16, entries), f32)
            for key in range(0, group, 2):
                terms, hots = [], []
                for which in (key, key + 1):
                    terms.append(scores[which])
                    hot = spot == jnp.broadcast_to(index[which : which + 1], (entries, rows))
                    hots.append(jnp.where(hot, 1.0, 0.0).astype(bf16))
                total = total + dot_nt(
                    jnp.concatenate(terms, axis=1), jnp.concatenate(hots, axis=1)
                )
            table_sum[...] += total
            return carry

        lax.fori_loop(0, length // group, one_group, 0)

    def finish_tokens():
        shift_rows, scale_rows = [], []
        for window in range(windows):
            rows_at = pl.ds(window * rows, rows)
            normed, inv_std = norm_rows(tokens_ref[rows_at, :].astype(f32))
            grad_in = own_in[rows_at, :] + far_own[rows_at, :].astype(f32)
            shift_rows.append(jnp.sum(grad_in, axis=0, keepdims=True))
            scale_rows.append(jnp.sum(grad_in * normed, axis=0, keepdims=True))
            dy = grad_in * scale_ref[pl.ds(window, 1), :]
            first = jnp.mean(dy, axis=-1, keepdims=True)
            second = jnp.mean(dy * normed, axis=-1, keepdims=True)
            back = (dy - first - normed * second) * inv_std
            tokens_out[rows_at, :] = (hidden_ref[rows_at, :] + back).astype(bf16)
        facts = jnp.concatenate(shift_rows + scale_rows + [early_ref[...]], axis=0)
        small.mine[0, :, :width] = facts
        small.mine[0, :, width:] = table_sum[...]

    steps = len(small.steps)
    jobs = {}
    for window in range(windows):
        jobs.setdefault(window, []).append(functools.partial(attend_back, window))
    jobs.setdefault(windows, []).extend([project_back, weight_grads])
    jobs.setdefault(windows + 1, []).append(functools.partial(table_back, 0))
    jobs.setdefault(windows + 2, []).append(functools.partial(far_add, 0))
    for window in range(1, windows):
        jobs.setdefault(windows + 2 + window, []).append(functools.partial(table_back, window))
    last = 2 * windows + 2
    for at in range(1, small.seq_count):
        jobs.setdefault(last + 2 * (at - 1), []).append(functools.partial(far_add, at))
    last = last + 2 * (small.seq_count - 2)
    jobs[last].append(finish_tokens)
    for at in range(steps + 1):
        jobs.setdefault(last + at, []).append(functools.partial(small.run, at))
    chunks = flows[0].chunks
    stages = flows[0].stages()
    order = [1, 0] + list(range(2, stages))
    total = max(max(flow.offset for flow in flows) + chunks + stages - 1, max(jobs) + 1)
    table_sum[...] = jnp.zeros_like(table_sum)

    def step(at, carry):
        for stage in order:
            for offset in sorted({flow.offset for flow in flows}):
                chunk = at - stage - offset

                @pl.when((chunk >= 0) & (chunk < chunks))
                def _(stage=stage, chunk=chunk, offset=offset):
                    for flow in flows:
                        if flow.offset == offset:
                            flow.run(stage, chunk)

            if stage == 0:

                @pl.when(at == 0)
                def _():
                    for load in loads:
                        load.copy.wait()

                for when, work in sorted(jobs.items()):

                    @pl.when(at == when)
                    def _(work=work):
                        for job in work:
                            job()

        return carry

    lax.fori_loop(0, total, step, 0)
    store_small = pltpu.make_async_copy(small.gathered, small_out, small_sem)
    store_small.start()

    def finish(chunk, carry):
        for flow in flows:
            flow.drain(chunk)
        return carry

    lax.fori_loop(0, chunks, finish, 0)
    for at in range(small.seq_count):
        far_copy(at).wait_send()
    small.drain()
    store_small.wait()


def backward(grads, loads, scales, early, sizes, chunks, flips):
    windows, rows, length, head_size = sizes
    width = loads[0].shape[1]
    shapes = [g.shape for g in grads] + [(width, width), (width, 2 * width)]
    offsets = [0] * len(grads) + [windows + 1] * 2
    flows = [Flow(s[0], s[1], chunks, flip, offset) for s, flip, offset in zip(shapes, flips, offsets)]
    win_bits = int(math.log2(lax.axis_size("win")))
    seq_bits = int(math.log2(lax.axis_size("seq")))
    total_rows = windows * rows
    small_shape = (16, width + 128)
    heads = width // head_size
    near = (2,) * seq_bits
    scratch = [pltpu.VMEM(load.shape, load.dtype) for load in loads]
    scratch += [
        pltpu.SemaphoreType.DMA((len(loads),)),
        pltpu.VMEM((total_rows, width), bf16),
        pltpu.VMEM((windows * length, 2 * width), bf16),
        pltpu.VMEM((windows, heads, length, rows), bf16),
        pltpu.VMEM((2,) * win_bits + (flows[-2].block, width), bf16),
        pltpu.VMEM((2,) * win_bits + (flows[-1].block, 2 * width), bf16),
        pltpu.VMEM((total_rows, width), f32),
        pltpu.VMEM(near + (total_rows, width), bf16),
        pltpu.VMEM(near[1:] + (total_rows, width), bf16),
        pltpu.VMEM((total_rows, width), bf16),
        pltpu.SemaphoreType.DMA((seq_bits,)),
        pltpu.SemaphoreType.DMA((seq_bits,)),
        pltpu.VMEM((16, 128), f32),
        pltpu.VMEM((seq_bits,) + small_shape, f32),
        pltpu.VMEM((seq_bits,) + small_shape, f32),
        pltpu.VMEM((2**win_bits,) + small_shape, f32),
        pltpu.SemaphoreType.DMA((win_bits + seq_bits,)),
        pltpu.SemaphoreType.DMA((win_bits + seq_bits,)),
        pltpu.SemaphoreType.DMA,
    ]
    for flow in flows:
        scratch += flow.scratch()
    vmem = pl.BlockSpec(memory_space=pltpu.VMEM)
    out_shape = [jax.ShapeDtypeStruct((flow.share, flow.columns), f32) for flow in flows]
    out_shape += [
        jax.ShapeDtypeStruct((total_rows, width), bf16),
        jax.ShapeDtypeStruct((2**win_bits,) + small_shape, f32),
    ]
    return pl.pallas_call(
        functools.partial(backward_kernel, flows, sizes),
        in_specs=[pl.BlockSpec(memory_space=pl.ANY)] * (len(grads) + len(loads)) + [vmem] * 2,
        out_specs=[vmem] * (len(out_shape) - 1) + [pl.BlockSpec(memory_space=pl.ANY)],
        out_shape=out_shape,
        scratch_shapes=scratch,
        compiler_params=pltpu.CompilerParams(
            collective_id=1, has_side_effects=True, vmem_limit_bytes=62 * 2**20
        ),
        cost_estimate=pl.CostEstimate(flops=10**10, bytes_accessed=200 * 2**20, transcendentals=0),
        name="backward",
    )(*[flow.view(grad) for flow, grad in zip(flows, grads)], *loads, scales, early)


def three_parts(values):
    parts = []
    for _ in range(3):
        part = lax.reduce_precision(values, 8, 7)
        parts.append(part.astype(bf16))
        values = values - part
    return parts


def per_device(
    tokens,
    cotangent,
    noise_times,
    cath_ids,
    chain_start,
    distance_bins,
    class_table,
    ada_weight,
    qkv_weight,
    out_weight,
    pair_table,
    pair_weight,
    gate_weight,
    up_weight,
    down_weight,
):
    windows, row_count, width = tokens.shape
    length = distance_bins.shape[2]
    head_count = pair_weight.shape[1]
    head_size = width // head_count
    table_rows = pair_table.shape[0]
    bin_count = table_rows // 2
    classes = class_table.shape[0]
    total_rows = windows * row_count
    win_count = lax.axis_size("win")
    seq_count = lax.axis_size("seq")
    devices = win_count * seq_count
    owner = lax.axis_index("win") * seq_count + lax.axis_index("seq")
    tokens_all = lax.all_gather(tokens, "seq", axis=1, tiled=True)
    class_onehot = (cath_ids[:, None] == jnp.arange(classes, dtype=jnp.int32)[None, :]).astype(f32)
    pre_cond = jnp.dot(
        class_onehot, class_table.astype(f32), precision=highest
    ) + time_embed(noise_times, width)
    cond_sig = jax.nn.sigmoid(pre_cond)
    condition = pre_cond * cond_sig
    modulation = dot(jnp.concatenate(three_parts(condition), axis=0), ada_weight)
    modulation = jnp.sum(modulation.reshape(3, windows, 6, width), axis=0)
    shift_attn = modulation[:, 0][:, None, :]
    scale_attn = modulation[:, 1][:, None, :]
    gate_attn = modulation[:, 2][:, None, :]
    shift_ffn = modulation[:, 3][:, None, :]
    scale_ffn = modulation[:, 4][:, None, :]
    gate_ffn = modulation[:, 5][:, None, :]
    table_bias = dot(pair_table, pair_weight).astype(bf16)
    facts = jnp.concatenate(
        [chain_start, jnp.full((1,), lax.axis_index("seq") * row_count, jnp.int32)]
    )
    table = table_bias.astype(f32).T
    tokens_float = tokens.astype(f32)
    normed_x, inv_x = layer_norm_parts(tokens_float)
    attn_in = (normed_x * (1.0 + scale_attn) + shift_attn).astype(bf16).reshape(total_rows, width)
    normed_all, _ = layer_norm_parts(tokens_all.astype(f32))
    attn_in_all = (
        (normed_all * (1.0 + scale_attn) + shift_attn).astype(bf16).reshape(windows * length, width)
    )
    queries = dot(attn_in, qkv_weight[:, :width]).astype(bf16)
    keys_values = dot(attn_in_all, qkv_weight[:, width:]).astype(bf16)
    attn_mixed, probs, pair_index = attend(facts, queries, keys_values, distance_bins, table, head_size)
    attn_out = dot(attn_mixed, out_weight).reshape(windows, row_count, width)
    gate_attn_sig = jax.nn.sigmoid(gate_attn)
    hidden_state = tokens_float + gate_attn_sig * attn_out
    normed_h, inv_h = layer_norm_parts(hidden_state)
    ffn_in = (normed_h * (1.0 + scale_ffn) + shift_ffn).astype(bf16).reshape(total_rows, width)
    gate_val = dot(ffn_in, gate_weight)
    up_val = dot(ffn_in, up_weight)
    gate_sig = jax.nn.sigmoid(gate_val)
    silu_gate = gate_val * gate_sig
    ffn_hidden = (silu_gate * up_val).astype(bf16)
    gate_ffn_sig = jax.nn.sigmoid(gate_ffn)
    grad_layer = cotangent.astype(f32)
    grad_ffn = (gate_ffn_sig * grad_layer).astype(bf16).reshape(total_rows, width)
    grad_down = dot_tn(ffn_hidden, grad_ffn).astype(bf16)
    ffn_out = dot(ffn_hidden, down_weight).reshape(windows, row_count, width)
    layer_out = (hidden_state + gate_ffn_sig * ffn_out).astype(bf16)
    grad_gate_ffn = jnp.sum(grad_layer * ffn_out * gate_ffn_sig * (1.0 - gate_ffn_sig), axis=1)
    grad_hidden_ffn = dot_nt(grad_ffn, down_weight)
    grad_up_val = (grad_hidden_ffn * silu_gate).astype(bf16)
    grad_gate_val = (
        grad_hidden_ffn * up_val * gate_sig * (1.0 + gate_val * (1.0 - gate_sig))
    ).astype(bf16)
    grad_gate = dot_tn(ffn_in, grad_gate_val).astype(bf16)
    grad_up = dot_tn(ffn_in, grad_up_val).astype(bf16)
    grad_ffn_in = dot_nt(grad_gate_val, gate_weight) + dot_nt(grad_up_val, up_weight)
    grad_ffn_in = grad_ffn_in.reshape(windows, row_count, width)
    grad_scale_ffn = jnp.sum(grad_ffn_in * normed_h, axis=1)
    grad_shift_ffn = jnp.sum(grad_ffn_in, axis=1)
    grad_hidden = grad_layer + norm_back(grad_ffn_in * (1.0 + scale_ffn), normed_h, inv_h)
    grad_attn_out = (gate_attn_sig * grad_hidden).astype(bf16).reshape(total_rows, width)
    grad_gate_attn = jnp.sum(grad_hidden * attn_out * gate_attn_sig * (1.0 - gate_attn_sig), axis=1)
    grad_out = dot_tn(attn_mixed, grad_attn_out).astype(bf16)
    grad_mixed = dot_nt(grad_attn_out, out_weight).astype(bf16)

    early = jnp.concatenate(
        [
            grad_gate_attn,
            grad_shift_ffn,
            grad_scale_ffn,
            grad_gate_ffn,
            pre_cond / seq_count,
            jnp.pad(class_onehot, ((0, 0), (0, width - classes))) / seq_count,
        ],
        axis=0,
    )
    owned_gate, owned_up, owned_down, owned_out, owned_q, owned_kv, grad_tokens, small = backward(
        [grad_gate, grad_up, grad_down, grad_out],
        [
            queries,
            keys_values,
            probs,
            grad_mixed,
            attn_in_all,
            qkv_weight,
            pair_index,
            tokens.reshape(total_rows, width),
            grad_hidden.reshape(total_rows, width),
        ],
        1.0 + scale_attn.reshape(windows, width),
        early,
        (windows, row_count, length, head_size),
        6,
        [False, True, False, True, True, True],
    )
    grad_tokens = grad_tokens.reshape(windows, row_count, width)
    rows_all = small[:, :, :width].reshape(win_count, 8, windows, width)
    mod_all = jnp.swapaxes(rows_all[:, :6], 1, 2).reshape(win_count * windows, 6 * width)
    table_all = jnp.sum(small[:, :head_count, width : width + table_rows], axis=0).T
    pre_all = rows_all[:, 6].reshape(win_count * windows, width)
    onehot_all = rows_all[:, 7].reshape(win_count * windows, width)
    ada_rows = width // devices
    sig_all = jax.nn.sigmoid(pre_all)
    condition_rows = lax.dynamic_slice_in_dim(pre_all * sig_all, owner * ada_rows, ada_rows, 1)
    owned_ada = lax.dot_general(
        condition_rows, mod_all, (((0,), (0,)), ((), ())), precision=highest
    )
    class_share = classes * width // devices
    per_class = width // class_share
    column_at = (owner % per_class) * class_share
    pre_cols = lax.dynamic_slice_in_dim(pre_all, column_at, class_share, 1)
    sig_cols = lax.dynamic_slice_in_dim(sig_all, column_at, class_share, 1)
    ada_cols = lax.dynamic_slice_in_dim(ada_weight, column_at, class_share, 0).astype(f32)
    grad_cond = lax.dot_general(mod_all, ada_cols, (((1,), (1,)), ((), ())), precision=highest)
    grad_pre = grad_cond * sig_cols * (1.0 + pre_cols * (1.0 - sig_cols))
    onehot_mine = lax.dynamic_slice_in_dim(onehot_all, owner // per_class, 1, 1)
    owned_class = jnp.sum(grad_pre * onehot_mine, axis=0)
    grad_pair_table = jnp.dot(table_all, pair_weight.astype(f32).T, precision=highest).reshape(-1)
    grad_pair_weight = jnp.dot(pair_table.astype(f32).T, table_all, precision=highest).reshape(-1)
    table_size = grad_pair_table.shape[0] // devices
    weight_size = grad_pair_weight.shape[0] // devices
    owned_pair_table = lax.dynamic_slice_in_dim(grad_pair_table, owner * table_size, table_size)
    owned_pair_weight = lax.dynamic_slice_in_dim(grad_pair_weight, owner * weight_size, weight_size)
    return (
        layer_out,
        grad_tokens,
        owned_class,
        owned_ada.reshape(-1),
        jnp.concatenate([owned_q, owned_kv], axis=-1).reshape(-1),
        owned_out.reshape(-1),
        owned_pair_table,
        owned_pair_weight,
        owned_gate.reshape(-1),
        owned_up.reshape(-1),
        owned_down.reshape(-1),
    )


def solution(mesh):
    rows = P("win", "seq", None)
    flat = P(("win", "seq"))
    placed = (rows, rows, P("win"), P("win"), P("win"), rows) + (P(),) * 9
    return jax.shard_map(
        per_device, mesh=mesh, in_specs=placed, out_specs=(rows, rows) + (flat,) * 9, check_vma=False
    )
```

```python
import functools
import math

import jax
import jax.numpy as jnp
from jax import lax
from jax.experimental import pallas as pl
from jax.experimental.pallas import tpu as pltpu
from jax.sharding import PartitionSpec as P

highest = lax.Precision.HIGHEST
norm_eps = 1e-06
f32 = jnp.float32
bf16 = jnp.bfloat16


def layer_norm_parts(values):
    centered = values - jnp.mean(values, axis=-1, keepdims=True)
    variance = jnp.mean(centered * centered, axis=-1, keepdims=True)
    inv_std = lax.rsqrt(variance + norm_eps)
    return (centered * inv_std, inv_std)


def norm_back(grad_normed, normed, inv_std):
    first_mean = jnp.mean(grad_normed, axis=-1, keepdims=True)
    second_mean = jnp.mean(grad_normed * normed, axis=-1, keepdims=True)
    return (grad_normed - first_mean - normed * second_mean) * inv_std


def time_embed(noise_times, model_width):
    half_width = model_width // 2
    frequency = jnp.exp(
        -math.log(10000.0) * jnp.arange(half_width).astype(f32) / half_width
    )
    angles = 1000.0 * noise_times[:, None] * frequency[None, :]
    return jnp.concatenate([jnp.sin(angles), jnp.cos(angles)], axis=-1)


def dot(a, b):
    return jnp.dot(a, b, preferred_element_type=f32)


def dot_nt(a, b):
    return lax.dot_general(a, b, (((1,), (1,)), ((), ())), preferred_element_type=f32)


def dot_tn(a, b):
    return lax.dot_general(a, b, (((0,), (0,)), ((), ())), preferred_element_type=f32)


def pair_halves(values, head_size):
    lane = lax.broadcasted_iota(jnp.int32, values.shape, 1)
    zero = jnp.zeros_like(values)
    return jnp.concatenate(
        [jnp.where(lane < head_size, values, zero), jnp.where(lane >= head_size, values, zero)], axis=0
    )


def pair_diagonal(values, head_size, rows):
    return jnp.concatenate([values[:head_size, :rows], values[head_size:, rows:]], axis=0).T


def forward_kernel(
    sizes,
    facts_ref,
    tokens_ref,
    cond_ref,
    table_ref,
    ada_hbm,
    weight_hbm,
    bins_hbm,
    mod_ref,
    q_ref,
    kv_ref,
    in_ref,
    mixed_ref,
    probs_ref,
    index_ref,
    ada_ref,
    weight_ref,
    bins_ref,
    load_sem,
    gathered,
    send_sem,
    recv_sem,
):
    windows, rows, length, head_size = sizes
    width = q_ref.shape[1]
    count = gathered.shape[0]
    here = lax.axis_index("seq")
    head_scale = 1.0 / math.sqrt(head_size)
    loads = [
        Load(source, target, load_sem.at[at])
        for at, (source, target) in enumerate(
            [(ada_hbm, ada_ref), (weight_hbm, weight_ref), (bins_hbm, bins_ref)]
        )
    ]
    for load in loads:
        load.copy.start()
    barrier = pltpu.get_barrier_semaphore()
    for sign in (1, -1):

        @pl.when((here + sign >= 0) & (here + sign < count))
        def _(sign=sign):
            pl.semaphore_signal(
                barrier, inc=1, device_id={"seq": here + sign}, device_id_type=pl.DeviceIdType.MESH
            )

    pl.semaphore_wait(barrier, jnp.where((here == 0) | (here == count - 1), 1, 2))

    def copy(way, hop, window, shard, source=None):
        slot = gathered.at[shard, window]
        return pltpu.make_async_remote_copy(
            src_ref=slot if source is None else source,
            dst_ref=slot,
            send_sem=send_sem.at[way, hop, window],
            recv_sem=recv_sem.at[way, hop, window],
            device_id={"seq": here + 1 - 2 * way},
            device_id_type=pl.DeviceIdType.MESH,
        )

    def for_sends(body):
        for window in range(windows):
            for way in range(2):

                @pl.when((here + 1 - 2 * way >= 0) & (here + 1 - 2 * way < count))
                def _(way=way, window=window):
                    body(copy(way, 0, window, here, tokens_ref.at[window]))

    for_sends(lambda each: each.start())
    loads[0].copy.wait()
    for part in range(mod_ref.shape[1] // width):
        cols = slice(part * width, (part + 1) * width)
        mod = dot(cond_ref[...], ada_ref[:, cols])
        mod_ref[:, cols] = mod[:8] + mod[8:16] + mod[16:24]
    loads[1].copy.wait()
    loads[2].copy.wait()

    def project(window, shard, values):
        normed, _ = norm_rows(values.astype(f32))
        scale = 1.0 + mod_ref[pl.ds(window, 1), width : 2 * width]
        block = (normed * scale + mod_ref[pl.ds(window, 1), :width]).astype(bf16)
        at = pl.ds(pl.multiple_of(window * length + shard * rows, rows), rows)
        in_ref[at, :] = block
        kv_ref[at, :] = dot(block, weight_ref[:, width:]).astype(bf16)
        return block

    def own(window, carry):
        block = project(window, here, tokens_ref[window])
        at = pl.ds(pl.multiple_of(window * rows, rows), rows)
        q_ref[at, :] = dot(block, weight_ref[:, :width]).astype(bf16)
        return carry

    lax.fori_loop(0, windows, own, 0)

    def arrive(way, hop, window):
        sign = 1 - 2 * way
        shard = here - sign * (hop + 1)

        @pl.when((shard >= 0) & (shard < count))
        def _():
            copy(way, hop, window, shard).wait_recv()

            @pl.when((here + sign >= 0) & (here + sign < count))
            def _():
                copy(way, hop + 1, window, shard).start()

            project(window, shard, gathered[shard, window])

    def relay(at, carry):
        arrive(lax.rem(at, 2), at // (2 * windows), lax.rem(at // 2, windows))
        return carry

    lax.fori_loop(0, (count - 2) * windows * 2, relay, 0)

    def finish(window, carry):
        def last(way, inner):
            arrive(way, count - 2, window)
            return inner

        lax.fori_loop(0, 2, last, 0)
        rows_at = pl.ds(pl.multiple_of(window * rows, rows), rows)
        keys_at = pl.ds(pl.multiple_of(window * length, length), length)
        start = facts_ref[window]
        bins = bins_ref[window].T
        key_first = lax.broadcasted_iota(jnp.int32, bins.shape, 0) < start
        row_first = lax.broadcasted_iota(jnp.int32, bins.shape, 1) + here * rows < start
        index_ref[window] = bins + jnp.where(key_first == row_first, table_ref.shape[1] // 2, 0)

        def one_pair(pair, inner):
            begin = pl.multiple_of(pair * 2 * head_size, 2 * head_size)
            cols = pl.ds(begin, 2 * head_size)
            v_cols = pl.ds(width + begin, 2 * head_size)
            index = index_ref[window]
            biases = []
            for head in range(2):
                entries = jnp.broadcast_to(table_ref[pl.ds(2 * pair + head, 1), :], index.shape)
                biases.append(jnp.take_along_axis(entries, index, axis=1, mode="promise_in_bounds"))
            q_pair = pair_halves(q_ref[rows_at, cols] * head_scale, head_size)
            scores = dot_nt(kv_ref[keys_at, cols], q_pair) + jnp.concatenate(biases, axis=1)
            top = jnp.max(scores, axis=0, keepdims=True)
            raised = jnp.exp(scores - top)
            total = jnp.sum(raised, axis=0, keepdims=True)
            probs = (raised * (1.0 / total)).astype(bf16)
            mixed = dot(kv_ref[keys_at, v_cols].T, probs)
            mixed_ref[rows_at, cols] = pair_diagonal(mixed, head_size, rows).astype(bf16)
            probs_ref[window, pair] = probs
            return inner

        lax.fori_loop(0, width // (2 * head_size), one_pair, 0)
        return carry

    lax.fori_loop(0, windows, finish, 0)
    for_sends(lambda each: each.wait_send())

    def sent(at, carry):
        way, hop, window = (lax.rem(at, 2), at // (2 * windows), lax.rem(at // 2, windows))
        sign = 1 - 2 * way
        shard = here - sign * (hop + 1)

        @pl.when((shard >= 0) & (shard < count) & (here + sign >= 0) & (here + sign < count))
        def _():
            copy(way, hop + 1, window, shard).wait_send()

        return carry

    lax.fori_loop(0, (count - 2) * windows * 2, sent, 0)


def forward(facts, tokens, cond_parts, table, ada_weight, qkv_weight, bins, head_size):
    windows, rows, length = bins.shape
    width = tokens.shape[-1]
    pairs = width // (2 * head_size)
    count = lax.axis_size("seq")
    vmem = pl.BlockSpec(memory_space=pltpu.VMEM)
    hbm = pl.BlockSpec(memory_space=pl.ANY)
    return pl.pallas_call(
        functools.partial(forward_kernel, (windows, rows, length, head_size)),
        in_specs=[pl.BlockSpec(memory_space=pltpu.SMEM), vmem, vmem, vmem, hbm, hbm, hbm],
        out_specs=[vmem] * 7,
        out_shape=[
            jax.ShapeDtypeStruct((8, ada_weight.shape[1]), f32),
            jax.ShapeDtypeStruct((windows * rows, width), bf16),
            jax.ShapeDtypeStruct((windows * length, 2 * width), bf16),
            jax.ShapeDtypeStruct((windows * length, width), bf16),
            jax.ShapeDtypeStruct((windows * rows, width), bf16),
            jax.ShapeDtypeStruct((windows, pairs, length, 2 * rows), bf16),
            jax.ShapeDtypeStruct((windows, length, rows), jnp.int32),
        ],
        scratch_shapes=[
            pltpu.VMEM(ada_weight.shape, bf16),
            pltpu.VMEM(qkv_weight.shape, bf16),
            pltpu.VMEM(bins.shape, jnp.int32),
            pltpu.SemaphoreType.DMA((3,)),
            pltpu.VMEM((count, windows, rows, width), bf16),
            pltpu.SemaphoreType.DMA((2, count - 1, windows)),
            pltpu.SemaphoreType.DMA((2, count - 1, windows)),
        ],
        compiler_params=pltpu.CompilerParams(
            collective_id=0, has_side_effects=True, vmem_limit_bytes=48 * 2**20
        ),
        cost_estimate=pl.CostEstimate(flops=10**10, bytes_accessed=40 * 2**20, transcendentals=0),
        name="forward",
    )(facts, tokens, cond_parts, table, ada_weight, qkv_weight, bins)


def bit_steps():
    win_bits = int(math.log2(lax.axis_size("win")))
    seq_bits = int(math.log2(lax.axis_size("seq")))
    return [("win", bit) for bit in range(win_bits)[::-1]] + [
        ("seq", bit) for bit in range(seq_bits)[::-1]
    ]


CORE = ("win", 0)


def my_bit(step):
    return lax.rem(lax.axis_index(step[0]) // (1 << step[1]), 2)


def partner(step):
    return {step[0]: lax.axis_index(step[0]) + (1 - 2 * my_bit(step)) * (1 << step[1])}


def greet():
    barrier = pltpu.get_barrier_semaphore()
    for step in bit_steps():
        pl.semaphore_signal(barrier, inc=1, device_id=partner(step), device_id_type=pl.DeviceIdType.MESH)
    pl.semaphore_wait(barrier, len(bit_steps()))


def remote(source, target, send_sem, recv_sem, step):
    return pltpu.make_async_remote_copy(
        src_ref=source,
        dst_ref=target,
        send_sem=send_sem,
        recv_sem=recv_sem,
        device_id=partner(step),
        device_id_type=pl.DeviceIdType.MESH,
    )


def each_block(shape, body):
    lead = shape[:-2]
    count = math.prod(lead)

    def one(flat, carry):
        index = []
        for size in lead[::-1]:
            index.append(lax.rem(flat, size))
            flat = flat // size
        body(tuple(index[::-1]))
        return carry

    if count == 1:
        body((0,) * len(lead))
    else:
        lax.fori_loop(0, count, one, 0)


class Flow:
    def __init__(self, rows, columns, chunks, flip, offset):
        steps = bit_steps()
        win_steps = [step for step in steps if step[0] == "win" and step != CORE]
        self.seq_steps = [step for step in steps if step[0] == "seq"]
        self.far = win_steps if flip else win_steps[::-1]
        self.names = win_steps
        self.near = self.seq_steps[::-1]
        self.chunks = chunks
        self.offset = offset
        self.width = columns // chunks
        self.share = rows // 2 ** len(steps)
        self.block = self.share * 2 ** len(self.seq_steps)
        self.columns = columns

    def view(self, grad):
        return grad.reshape((2,) * (len(self.far) + 1) + (self.block, self.columns))

    def scratch(self):
        chunks, width = (self.chunks, self.width)
        far, near = (len(self.far), len(self.near))
        shapes = [(2,) * far + (self.block, width)] * 2
        shapes += [(2,) * (far - 1 - i) + (self.block, width) for i in range(far)]
        shapes += [(2,) * near + (self.share, width)]
        shapes += [(2,) * (near - 1 - i) + (self.share, width) for i in range(near)]
        buffers = [pltpu.VMEM((chunks if at else 2,) + shape, bf16) for at, shape in enumerate(shapes)]
        count = 1 + far + near
        return buffers + [
            pltpu.SemaphoreType.DMA((chunks,)),
            pltpu.SemaphoreType.DMA((count, chunks)),
            pltpu.SemaphoreType.DMA((count, chunks)),
        ]

    def bind(self, grad, out, scratch):
        self.grad, self.out = grad, out
        far, near = (len(self.far), len(self.near))
        self.mine = scratch[0]
        self.first = scratch[1]
        self.far_bufs = list(scratch[2 : 2 + far])
        self.turn = scratch[2 + far]
        self.near_bufs = list(scratch[3 + far : 3 + far + near])
        self.local_sem, self.send_sem, self.recv_sem = scratch[3 + far + near :]

    def piece(self, bit, chunk):
        index = (slice(None),) * len(self.far) + (bit, slice(None))
        return self.grad.at[index + (pl.ds(pl.multiple_of(chunk * self.width, 128), self.width),)]

    def local_copy(self, chunk):
        return pltpu.make_async_copy(
            self.piece(my_bit(CORE), chunk), self.mine.at[lax.rem(chunk, 2)], self.local_sem.at[chunk]
        )

    def copy(self, stage, chunk):
        send, recv = (self.send_sem.at[stage, chunk], self.recv_sem.at[stage, chunk])
        far = len(self.far)
        if stage == 0:
            return remote(
                self.piece(1 - my_bit(CORE), chunk), self.first.at[chunk], send, recv, CORE
            )
        if stage <= far:
            step = self.far[stage - 1]
            source = ([self.first] + self.far_bufs)[stage - 1]
            target = self.far_bufs[stage - 1]
            axis = self.axis_of(step, self.far[: stage - 1], self.names)
        else:
            at = stage - 1 - far
            step = self.near[at]
            source = ([self.turn] + self.near_bufs)[at]
            target = self.near_bufs[at]
            axis = self.axis_of(step, self.near[:at], self.seq_steps)
        index = (chunk,) + (slice(None),) * axis + (1 - my_bit(step),)
        return remote(source.at[index], target.at[chunk], send, recv, step)

    def axis_of(self, step, gone, names):
        return [name for name in names if name not in gone].index(step)

    def stages(self):
        return 2 + len(self.far) + len(self.near)

    def run(self, stage, chunk):
        far, near = (len(self.far), len(self.near))
        if stage == 0:
            self.local_copy(chunk).start()
            self.copy(0, chunk).start()
            return
        self.copy(stage - 1, chunk).wait_recv()
        if stage == 1:
            self.local_copy(chunk).wait()
            shape = self.first.shape[1:]

            def add_first(index):
                at = (chunk,) + index
                kept = self.mine[(lax.rem(chunk, 2),) + index].astype(f32)
                self.first[at] = (self.first[at].astype(f32) + kept).astype(bf16)

            each_block(shape, add_first)
        elif stage < 1 + far:
            target = self.far_bufs[stage - 2]
            source = ([self.first] + self.far_bufs)[stage - 2]
            self.add_half(target, source, self.far, self.names, stage - 2, chunk)
        elif stage == 1 + far:
            step = self.far[-1]
            source = ([self.first] + self.far_bufs)[far - 1]
            target = self.far_bufs[far - 1]
            total = target[chunk].astype(f32) + source[chunk, my_bit(step)].astype(f32)
            total = total.astype(bf16)
            count = 2**near
            for owner in range(count):
                at, rest = ((), owner)
                for _ in range(near):
                    at = (rest % 2,) + at
                    rest = rest // 2
                self.turn[(chunk,) + at] = total[owner * self.share : (owner + 1) * self.share]
        elif stage < 1 + far + near:
            at = stage - 2 - far
            source = ([self.turn] + self.near_bufs)[at]
            self.add_half(self.near_bufs[at], source, self.near, self.seq_steps, at, chunk)
        else:
            source = ([self.turn] + self.near_bufs)[near - 1]
            kept = source[chunk, my_bit(self.near[-1])]
            total = self.near_bufs[near - 1][chunk].astype(f32) + kept.astype(f32)
            self.out[:, pl.ds(pl.multiple_of(chunk * self.width, 128), self.width)] = total
        if stage < 1 + far + near:
            self.copy(stage, chunk).start()

    def add_half(self, target, source, steps, names, at, chunk):
        step = steps[at]
        axis = self.axis_of(step, steps[:at], names)
        bit = my_bit(step)

        def add(index):
            from_at = (chunk,) + index[:axis] + (bit,) + index[axis:]
            to_at = (chunk,) + index
            target[to_at] = (target[to_at].astype(f32) + source[from_at].astype(f32)).astype(bf16)

        each_block(target.shape[1:], add)

    def drain(self, chunk):
        for stage in range(self.stages() - 1):
            self.copy(stage, chunk).wait_send()


class Load:
    def __init__(self, source, target, sem):
        self.target = target
        self.copy = pltpu.make_async_copy(source, target, sem)


class SmallGather:
    def __init__(self, mine, halves, gathered, send_sem, recv_sem):
        self.mine, self.halves, self.gathered = mine, halves, gathered
        self.send_sem, self.recv_sem = send_sem, recv_sem
        self.steps = bit_steps()[::-1]
        self.seq_count = len([step for step in self.steps if step[0] == "seq"])

    def copy(self, at):
        step = self.steps[at]
        if at < self.seq_count:
            source, target = self.mine.at[at], self.halves.at[at]
        else:
            size = 1 << step[1]
            here = lax.axis_index("win")
            block = pl.ds(here - lax.rem(here, size), size)
            source = target = self.gathered.at[block]
        return remote(source, target, self.send_sem.at[at], self.recv_sem.at[at], step)

    def run(self, at):
        if at > 0:
            self.copy(at - 1).wait_recv()
            if at <= self.seq_count:
                total = self.mine[at - 1] + self.halves[at - 1]
                if at < self.seq_count:
                    self.mine[at] = total
                else:
                    self.gathered[lax.axis_index("win")] = total
        if at < len(self.steps):
            self.copy(at).start()

    def drain(self):
        for at in range(len(self.steps)):
            self.copy(at).wait_send()


def norm_rows(values):
    centered = values - jnp.mean(values, axis=-1, keepdims=True)
    inv_std = lax.rsqrt(jnp.mean(centered * centered, axis=-1, keepdims=True) + norm_eps)
    return (centered * inv_std, inv_std)


def backward_kernel(flows, sizes, *refs):
    windows, rows, length, head_size = sizes
    refs = list(refs)

    def take(count):
        taken = refs[:count]
        del refs[:count]
        return taken

    grads = take(4)
    sources = take(9)
    scale_ref, early_ref = take(2)
    shares = take(6)
    tokens_out, small_out = take(2)
    targets = take(9)
    (load_sem,) = take(1)
    grad_q, grad_kv, grad_scores, q_weight, kv_weight, own_in = take(6)
    far_in, far_half, far_own, far_send, far_recv = take(5)
    (table_sum,) = take(1)
    small = SmallGather(*take(5))
    (small_sem,) = take(1)
    for flow, grad, share in zip(flows, grads + [q_weight, kv_weight], shares):
        flow.bind(grad, share, take(len(flow.scratch())))
    loads = [Load(s, t, load_sem.at[at]) for at, (s, t) in enumerate(zip(sources, targets))]
    q_ref, kv_ref, probs_ref, grad_ref, in_ref, weight_ref, index_ref, tokens_ref, hidden_ref = targets
    width = q_ref.shape[1]
    head_scale = 1.0 / math.sqrt(head_size)
    heads = width // head_size
    seq_steps = bit_steps()[::-1][: small.seq_count]
    for load in loads:
        load.copy.start()
    greet()

    def attend_back(window):
        rows_at = pl.ds(pl.multiple_of(window * rows, rows), rows)
        keys_at = pl.ds(pl.multiple_of(window * length, length), length)

        def one_pair(pair, carry):
            start = pl.multiple_of(pair * 2 * head_size, 2 * head_size)
            cols = pl.ds(start, 2 * head_size)
            v_cols = pl.ds(width + start, 2 * head_size)
            q_pair = pair_halves(q_ref[rows_at, cols] * head_scale, head_size)
            g_pair = pair_halves(grad_ref[rows_at, cols], head_size)
            probs = probs_ref[window, pair]
            grad_kv[keys_at, v_cols] = dot(probs, g_pair).astype(bf16)
            grad_probs = dot_nt(kv_ref[keys_at, v_cols], g_pair)
            probs = probs.astype(f32)
            delta = jnp.sum(probs * grad_probs, axis=0, keepdims=True)
            scores = (probs * (grad_probs - delta)).astype(bf16)
            grad_kv[keys_at, cols] = dot(scores, q_pair).astype(bf16)
            back = dot(kv_ref[keys_at, cols].T, scores)
            grad_q[rows_at, cols] = (pair_diagonal(back, head_size, rows) * head_scale).astype(bf16)
            grad_scores[window, 2 * pair] = scores[:, :rows]
            grad_scores[window, 2 * pair + 1] = scores[:, rows:]
            return carry

        lax.fori_loop(0, heads // 2, one_pair, 0)

    def split_rows(target, values, cols):
        lead = target.shape[:-2]
        block = target.shape[-2]
        for at in range(math.prod(lead)):
            index, rest = ((), at)
            for size in lead[::-1]:
                index = (rest % size,) + index
                rest = rest // size
            target[index + (slice(None), cols)] = values[at * block : (at + 1) * block].astype(bf16)

    def project_back():
        def one_window(window, carry):
            keys_at = pl.ds(pl.multiple_of(window * length, length), length)
            far = dot_nt(grad_kv[keys_at, :], weight_ref[:, width:]).astype(bf16)
            split_owner(far, window)
            return carry

        def split_owner(far, window):
            rows_at = pl.ds(pl.multiple_of(window * rows, rows), rows)
            for owner in range(length // rows):
                index, rest = ((), owner)
                for _ in seq_steps:
                    index = (rest % 2,) + index
                    rest = rest // 2
                far_in[index + (rows_at,)] = far[owner * rows : (owner + 1) * rows]

        lax.fori_loop(0, windows, one_window, 0)
        far_copy(0).start()
        own_in[...] = dot_nt(grad_q[...], weight_ref[:, :width])

    def weight_grads():
        here = lax.axis_index("seq") * rows
        own = [in_ref[pl.ds(pl.multiple_of(w * length + here, rows), rows), :] for w in range(windows)]
        split_rows(q_weight, dot(jnp.concatenate(own, axis=0).T, grad_q[...]), slice(None))
        turned = in_ref[...].T
        step = 512
        for at in range(2 * width // step):
            cols = slice(at * step, (at + 1) * step)
            split_rows(kv_weight, dot(turned, grad_kv[:, cols]), cols)

    far_bufs = [far_in] + [far_half, far_own][-small.seq_count :]

    def far_copy(at):
        step = seq_steps[at]
        index = (slice(None),) * (small.seq_count - 1 - at) + (1 - my_bit(step),)
        return remote(
            far_bufs[at].at[index], far_bufs[at + 1], far_send.at[at], far_recv.at[at], step
        )

    def far_add(at):
        far_copy(at).wait_recv()
        step = seq_steps[at]
        bit = my_bit(step)
        target, source = far_bufs[at + 1], far_bufs[at]
        lead = target.shape[:-2]
        for flat in range(math.prod(lead)):
            for window in range(windows):
                index = ((flat,) if lead else ()) + (pl.ds(window * rows, rows),)
                kept = source[index[:-1] + (bit,) + index[-1:]].astype(f32)
                target[index] = (target[index].astype(f32) + kept).astype(bf16)
        if at + 1 < small.seq_count:
            far_copy(at + 1).start()

    def table_back(window):
        group = 16
        entries = table_sum.shape[1]

        def one_group(at, carry):
            keys = pl.ds(pl.multiple_of(at * group, group), group)
            scores = grad_scores[window, :, keys, :].astype(f32)
            scores = jnp.concatenate([scores, jnp.zeros((16 - heads, group, rows), f32)], axis=0)
            scores = jnp.swapaxes(scores, 0, 1).astype(bf16)
            index = index_ref[window, keys, :]
            spot = lax.broadcasted_iota(jnp.int32, (entries, rows), 0)
            total = jnp.zeros((16, entries), f32)
            for key in range(0, group, 2):
                terms, hots = [], []
                for which in (key, key + 1):
                    terms.append(scores[which])
                    hot = spot == jnp.broadcast_to(index[which : which + 1], (entries, rows))
                    hots.append(jnp.where(hot, 1.0, 0.0).astype(bf16))
                total = total + dot_nt(
                    jnp.concatenate(terms, axis=1), jnp.concatenate(hots, axis=1)
                )
            table_sum[...] += total
            return carry

        lax.fori_loop(0, length // group, one_group, 0)

    def finish_tokens():
        shift_rows, scale_rows = [], []
        for window in range(windows):
            rows_at = pl.ds(window * rows, rows)
            normed, inv_std = norm_rows(tokens_ref[rows_at, :].astype(f32))
            grad_in = own_in[rows_at, :] + far_own[rows_at, :].astype(f32)
            shift_rows.append(jnp.sum(grad_in, axis=0, keepdims=True))
            scale_rows.append(jnp.sum(grad_in * normed, axis=0, keepdims=True))
            dy = grad_in * scale_ref[pl.ds(window, 1), :]
            first = jnp.mean(dy, axis=-1, keepdims=True)
            second = jnp.mean(dy * normed, axis=-1, keepdims=True)
            back = (dy - first - normed * second) * inv_std
            tokens_out[rows_at, :] = (hidden_ref[rows_at, :] + back).astype(bf16)
        facts = jnp.concatenate(shift_rows + scale_rows + [early_ref[...]], axis=0)
        small.mine[0, :, :width] = facts
        small.mine[0, :, width:] = table_sum[...]

    steps = len(small.steps)
    jobs = {}
    for window in range(windows):
        jobs.setdefault(window, []).append(functools.partial(attend_back, window))
    jobs.setdefault(windows, []).extend([project_back, weight_grads])
    jobs.setdefault(windows + 1, []).append(functools.partial(table_back, 0))
    jobs.setdefault(windows + 2, []).append(functools.partial(far_add, 0))
    for window in range(1, windows):
        jobs.setdefault(windows + 2 + window, []).append(functools.partial(table_back, window))
    last = 2 * windows + 2
    for at in range(1, small.seq_count):
        jobs.setdefault(last + 2 * (at - 1), []).append(functools.partial(far_add, at))
    last = last + 2 * (small.seq_count - 2)
    jobs[last].append(finish_tokens)
    for at in range(steps + 1):
        jobs.setdefault(last + at, []).append(functools.partial(small.run, at))
    chunks = flows[0].chunks
    stages = flows[0].stages()
    order = [1, 0] + list(range(2, stages))
    total = max(max(flow.offset for flow in flows) + chunks + stages - 1, max(jobs) + 1)
    table_sum[...] = jnp.zeros_like(table_sum)

    def step(at, carry):
        for stage in order:
            for offset in sorted({flow.offset for flow in flows}):
                chunk = at - stage - offset

                @pl.when((chunk >= 0) & (chunk < chunks))
                def _(stage=stage, chunk=chunk, offset=offset):
                    for flow in flows:
                        if flow.offset == offset:
                            flow.run(stage, chunk)

            if stage == 0:

                @pl.when(at == 0)
                def _():
                    for load in loads:
                        load.copy.wait()

                for when, work in sorted(jobs.items()):

                    @pl.when(at == when)
                    def _(work=work):
                        for job in work:
                            job()

        return carry

    lax.fori_loop(0, total, step, 0)
    store_small = pltpu.make_async_copy(small.gathered, small_out, small_sem)
    store_small.start()

    def finish(chunk, carry):
        for flow in flows:
            flow.drain(chunk)
        return carry

    lax.fori_loop(0, chunks, finish, 0)
    for at in range(small.seq_count):
        far_copy(at).wait_send()
    small.drain()
    store_small.wait()


def backward(grads, loads, scales, early, sizes, chunks, flips):
    windows, rows, length, head_size = sizes
    width = loads[0].shape[1]
    shapes = [g.shape for g in grads] + [(width, width), (width, 2 * width)]
    offsets = [0] * len(grads) + [windows + 1] * 2
    flows = [Flow(s[0], s[1], chunks, flip, offset) for s, flip, offset in zip(shapes, flips, offsets)]
    win_bits = int(math.log2(lax.axis_size("win")))
    seq_bits = int(math.log2(lax.axis_size("seq")))
    total_rows = windows * rows
    small_shape = (16, width + 128)
    heads = width // head_size
    near = (2,) * seq_bits
    scratch = [pltpu.VMEM(load.shape, load.dtype) for load in loads]
    scratch += [
        pltpu.SemaphoreType.DMA((len(loads),)),
        pltpu.VMEM((total_rows, width), bf16),
        pltpu.VMEM((windows * length, 2 * width), bf16),
        pltpu.VMEM((windows, heads, length, rows), bf16),
        pltpu.VMEM((2,) * win_bits + (flows[-2].block, width), bf16),
        pltpu.VMEM((2,) * win_bits + (flows[-1].block, 2 * width), bf16),
        pltpu.VMEM((total_rows, width), f32),
        pltpu.VMEM(near + (total_rows, width), bf16),
        pltpu.VMEM(near[1:] + (total_rows, width), bf16),
        pltpu.VMEM((total_rows, width), bf16),
        pltpu.SemaphoreType.DMA((seq_bits,)),
        pltpu.SemaphoreType.DMA((seq_bits,)),
        pltpu.VMEM((16, 128), f32),
        pltpu.VMEM((seq_bits,) + small_shape, f32),
        pltpu.VMEM((seq_bits,) + small_shape, f32),
        pltpu.VMEM((2**win_bits,) + small_shape, f32),
        pltpu.SemaphoreType.DMA((win_bits + seq_bits,)),
        pltpu.SemaphoreType.DMA((win_bits + seq_bits,)),
        pltpu.SemaphoreType.DMA,
    ]
    for flow in flows:
        scratch += flow.scratch()
    vmem = pl.BlockSpec(memory_space=pltpu.VMEM)
    out_shape = [jax.ShapeDtypeStruct((flow.share, flow.columns), f32) for flow in flows]
    out_shape += [
        jax.ShapeDtypeStruct((total_rows, width), bf16),
        jax.ShapeDtypeStruct((2**win_bits,) + small_shape, f32),
    ]
    return pl.pallas_call(
        functools.partial(backward_kernel, flows, sizes),
        in_specs=[pl.BlockSpec(memory_space=pl.ANY)] * (len(grads) + len(loads)) + [vmem] * 2,
        out_specs=[vmem] * (len(out_shape) - 1) + [pl.BlockSpec(memory_space=pl.ANY)],
        out_shape=out_shape,
        scratch_shapes=scratch,
        compiler_params=pltpu.CompilerParams(
            collective_id=1, has_side_effects=True, vmem_limit_bytes=62 * 2**20
        ),
        cost_estimate=pl.CostEstimate(flops=10**10, bytes_accessed=200 * 2**20, transcendentals=0),
        name="backward",
    )(*[flow.view(grad) for flow, grad in zip(flows, grads)], *loads, scales, early)


def three_parts(values):
    parts = []
    for _ in range(3):
        part = lax.reduce_precision(values, 8, 7)
        parts.append(part.astype(bf16))
        values = values - part
    return parts


def per_device(
    tokens,
    cotangent,
    noise_times,
    cath_ids,
    chain_start,
    distance_bins,
    class_table,
    ada_weight,
    qkv_weight,
    out_weight,
    pair_table,
    pair_weight,
    gate_weight,
    up_weight,
    down_weight,
):
    windows, row_count, width = tokens.shape
    length = distance_bins.shape[2]
    head_count = pair_weight.shape[1]
    head_size = width // head_count
    table_rows = pair_table.shape[0]
    bin_count = table_rows // 2
    classes = class_table.shape[0]
    total_rows = windows * row_count
    win_count = lax.axis_size("win")
    seq_count = lax.axis_size("seq")
    devices = win_count * seq_count
    owner = lax.axis_index("win") * seq_count + lax.axis_index("seq")
    class_onehot = (cath_ids[:, None] == jnp.arange(classes, dtype=jnp.int32)[None, :]).astype(f32)
    pre_cond = jnp.dot(
        class_onehot, class_table.astype(f32), precision=highest
    ) + time_embed(noise_times, width)
    cond_sig = jax.nn.sigmoid(pre_cond)
    condition = pre_cond * cond_sig
    cond_parts = jnp.concatenate(
        [jnp.pad(part, ((0, 8 - windows), (0, 0))) for part in three_parts(condition)], axis=0
    )
    table_bias = dot(pair_table, pair_weight).astype(bf16)
    modulation, queries, keys_values, attn_in_all, attn_mixed, probs, pair_index = forward(
        chain_start,
        tokens,
        cond_parts,
        table_bias.astype(f32).T,
        ada_weight,
        qkv_weight,
        distance_bins,
        head_size,
    )
    modulation = modulation[:windows].reshape(windows, 6, width)
    shift_attn = modulation[:, 0][:, None, :]
    scale_attn = modulation[:, 1][:, None, :]
    gate_attn = modulation[:, 2][:, None, :]
    shift_ffn = modulation[:, 3][:, None, :]
    scale_ffn = modulation[:, 4][:, None, :]
    gate_ffn = modulation[:, 5][:, None, :]
    tokens_float = tokens.astype(f32)
    attn_out = dot(attn_mixed, out_weight).reshape(windows, row_count, width)
    gate_attn_sig = jax.nn.sigmoid(gate_attn)
    hidden_state = tokens_float + gate_attn_sig * attn_out
    normed_h, inv_h = layer_norm_parts(hidden_state)
    ffn_in = (normed_h * (1.0 + scale_ffn) + shift_ffn).astype(bf16).reshape(total_rows, width)
    gate_val = dot(ffn_in, gate_weight)
    up_val = dot(ffn_in, up_weight)
    gate_sig = jax.nn.sigmoid(gate_val)
    silu_gate = gate_val * gate_sig
    ffn_hidden = (silu_gate * up_val).astype(bf16)
    gate_ffn_sig = jax.nn.sigmoid(gate_ffn)
    grad_layer = cotangent.astype(f32)
    grad_ffn = (gate_ffn_sig * grad_layer).astype(bf16).reshape(total_rows, width)
    grad_down = dot_tn(ffn_hidden, grad_ffn).astype(bf16)
    ffn_out = dot(ffn_hidden, down_weight).reshape(windows, row_count, width)
    layer_out = (hidden_state + gate_ffn_sig * ffn_out).astype(bf16)
    grad_gate_ffn = jnp.sum(grad_layer * ffn_out * gate_ffn_sig * (1.0 - gate_ffn_sig), axis=1)
    grad_hidden_ffn = dot_nt(grad_ffn, down_weight)
    grad_up_val = (grad_hidden_ffn * silu_gate).astype(bf16)
    grad_gate_val = (
        grad_hidden_ffn * up_val * gate_sig * (1.0 + gate_val * (1.0 - gate_sig))
    ).astype(bf16)
    grad_gate = dot_tn(ffn_in, grad_gate_val).astype(bf16)
    grad_up = dot_tn(ffn_in, grad_up_val).astype(bf16)
    grad_ffn_in = dot_nt(grad_gate_val, gate_weight) + dot_nt(grad_up_val, up_weight)
    grad_ffn_in = grad_ffn_in.reshape(windows, row_count, width)
    grad_scale_ffn = jnp.sum(grad_ffn_in * normed_h, axis=1)
    grad_shift_ffn = jnp.sum(grad_ffn_in, axis=1)
    grad_hidden = grad_layer + norm_back(grad_ffn_in * (1.0 + scale_ffn), normed_h, inv_h)
    grad_attn_out = (gate_attn_sig * grad_hidden).astype(bf16).reshape(total_rows, width)
    grad_gate_attn = jnp.sum(grad_hidden * attn_out * gate_attn_sig * (1.0 - gate_attn_sig), axis=1)
    grad_out = dot_tn(attn_mixed, grad_attn_out).astype(bf16)
    grad_mixed = dot_nt(grad_attn_out, out_weight).astype(bf16)

    early = jnp.concatenate(
        [
            grad_gate_attn,
            grad_shift_ffn,
            grad_scale_ffn,
            grad_gate_ffn,
            pre_cond / seq_count,
            jnp.pad(class_onehot, ((0, 0), (0, width - classes))) / seq_count,
        ],
        axis=0,
    )
    owned_gate, owned_up, owned_down, owned_out, owned_q, owned_kv, grad_tokens, small = backward(
        [grad_gate, grad_up, grad_down, grad_out],
        [
            queries,
            keys_values,
            probs,
            grad_mixed,
            attn_in_all,
            qkv_weight,
            pair_index,
            tokens.reshape(total_rows, width),
            grad_hidden.reshape(total_rows, width),
        ],
        1.0 + scale_attn.reshape(windows, width),
        early,
        (windows, row_count, length, head_size),
        6,
        [False, True, False, True, True, True],
    )
    grad_tokens = grad_tokens.reshape(windows, row_count, width)
    rows_all = small[:, :, :width].reshape(win_count, 8, windows, width)
    mod_all = jnp.swapaxes(rows_all[:, :6], 1, 2).reshape(win_count * windows, 6 * width)
    table_all = jnp.sum(small[:, :head_count, width : width + table_rows], axis=0).T
    pre_all = rows_all[:, 6].reshape(win_count * windows, width)
    onehot_all = rows_all[:, 7].reshape(win_count * windows, width)
    ada_rows = width // devices
    sig_all = jax.nn.sigmoid(pre_all)
    condition_rows = lax.dynamic_slice_in_dim(pre_all * sig_all, owner * ada_rows, ada_rows, 1)
    owned_ada = lax.dot_general(
        condition_rows, mod_all, (((0,), (0,)), ((), ())), precision=highest
    )
    class_share = classes * width // devices
    per_class = width // class_share
    column_at = (owner % per_class) * class_share
    pre_cols = lax.dynamic_slice_in_dim(pre_all, column_at, class_share, 1)
    sig_cols = lax.dynamic_slice_in_dim(sig_all, column_at, class_share, 1)
    ada_cols = lax.dynamic_slice_in_dim(ada_weight, column_at, class_share, 0).astype(f32)
    grad_cond = lax.dot_general(mod_all, ada_cols, (((1,), (1,)), ((), ())), precision=highest)
    grad_pre = grad_cond * sig_cols * (1.0 + pre_cols * (1.0 - sig_cols))
    onehot_mine = lax.dynamic_slice_in_dim(onehot_all, owner // per_class, 1, 1)
    owned_class = jnp.sum(grad_pre * onehot_mine, axis=0)
    grad_pair_table = jnp.dot(table_all, pair_weight.astype(f32).T, precision=highest).reshape(-1)
    grad_pair_weight = jnp.dot(pair_table.astype(f32).T, table_all, precision=highest).reshape(-1)
    table_size = grad_pair_table.shape[0] // devices
    weight_size = grad_pair_weight.shape[0] // devices
    owned_pair_table = lax.dynamic_slice_in_dim(grad_pair_table, owner * table_size, table_size)
    owned_pair_weight = lax.dynamic_slice_in_dim(grad_pair_weight, owner * weight_size, weight_size)
    return (
        layer_out,
        grad_tokens,
        owned_class,
        owned_ada.reshape(-1),
        jnp.concatenate([owned_q, owned_kv], axis=-1).reshape(-1),
        owned_out.reshape(-1),
        owned_pair_table,
        owned_pair_weight,
        owned_gate.reshape(-1),
        owned_up.reshape(-1),
        owned_down.reshape(-1),
    )


def solution(mesh):
    rows = P("win", "seq", None)
    flat = P(("win", "seq"))
    placed = (rows, rows, P("win"), P("win"), P("win"), rows) + (P(),) * 9
    return jax.shard_map(
        per_device, mesh=mesh, in_specs=placed, out_specs=(rows, rows) + (flat,) * 9, check_vma=False
    )
```

```python
import functools
import math

import jax
import jax.numpy as jnp
from jax import lax
from jax.experimental import pallas as pl
from jax.experimental.pallas import tpu as pltpu
from jax.sharding import PartitionSpec as P

highest = lax.Precision.HIGHEST
norm_eps = 1e-06
f32 = jnp.float32
bf16 = jnp.bfloat16


def layer_norm_parts(values):
    centered = values - jnp.mean(values, axis=-1, keepdims=True)
    variance = jnp.mean(centered * centered, axis=-1, keepdims=True)
    inv_std = lax.rsqrt(variance + norm_eps)
    return (centered * inv_std, inv_std)


def norm_back(grad_normed, normed, inv_std):
    first_mean = jnp.mean(grad_normed, axis=-1, keepdims=True)
    second_mean = jnp.mean(grad_normed * normed, axis=-1, keepdims=True)
    return (grad_normed - first_mean - normed * second_mean) * inv_std


def time_embed(noise_times, model_width):
    half_width = model_width // 2
    frequency = jnp.exp(
        -math.log(10000.0) * jnp.arange(half_width).astype(f32) / half_width
    )
    angles = 1000.0 * noise_times[:, None] * frequency[None, :]
    return jnp.concatenate([jnp.sin(angles), jnp.cos(angles)], axis=-1)


def dot(a, b):
    return jnp.dot(a, b, preferred_element_type=f32)


def dot_nt(a, b):
    return lax.dot_general(a, b, (((1,), (1,)), ((), ())), preferred_element_type=f32)


def dot_tn(a, b):
    return lax.dot_general(a, b, (((0,), (0,)), ((), ())), preferred_element_type=f32)


def pair_halves(values, head_size):
    lane = lax.broadcasted_iota(jnp.int32, values.shape, 1)
    zero = jnp.zeros_like(values)
    return jnp.concatenate(
        [jnp.where(lane < head_size, values, zero), jnp.where(lane >= head_size, values, zero)], axis=0
    )


def pair_diagonal(values, head_size, rows):
    return jnp.concatenate([values[:head_size, :rows], values[head_size:, rows:]], axis=0).T


def forward_kernel(
    sizes,
    facts_ref,
    tokens_hbm,
    cond_ref,
    table_ref,
    ada_hbm,
    weight_hbm,
    bins_hbm,
    mod_ref,
    q_ref,
    kv_ref,
    in_ref,
    mixed_ref,
    probs_ref,
    index_ref,
    ada_ref,
    weight_ref,
    bins_ref,
    tokens_ref,
    load_sem,
    gathered,
    send_sem,
    recv_sem,
):
    windows, rows, length, head_size = sizes
    width = q_ref.shape[1]
    count = gathered.shape[0]
    here = lax.axis_index("seq")
    head_scale = 1.0 / math.sqrt(head_size)
    loads = [
        Load(source, target, load_sem.at[at])
        for at, (source, target) in enumerate(
            [(ada_hbm, ada_ref), (weight_hbm, weight_ref), (bins_hbm, bins_ref), (tokens_hbm, tokens_ref)]
        )
    ]
    for load in loads:
        load.copy.start()
    barrier = pltpu.get_barrier_semaphore()
    for sign in (1, -1):

        @pl.when((here + sign >= 0) & (here + sign < count))
        def _(sign=sign):
            pl.semaphore_signal(
                barrier, inc=1, device_id={"seq": here + sign}, device_id_type=pl.DeviceIdType.MESH
            )

    pl.semaphore_wait(barrier, jnp.where((here == 0) | (here == count - 1), 1, 2))

    def copy(way, hop, window, shard, source=None):
        slot = gathered.at[shard, window]
        return pltpu.make_async_remote_copy(
            src_ref=slot if source is None else source,
            dst_ref=slot,
            send_sem=send_sem.at[way, hop, window],
            recv_sem=recv_sem.at[way, hop, window],
            device_id={"seq": here + 1 - 2 * way},
            device_id_type=pl.DeviceIdType.MESH,
        )

    def for_sends(body):
        for window in range(windows):
            for way in range(2):

                @pl.when((here + 1 - 2 * way >= 0) & (here + 1 - 2 * way < count))
                def _(way=way, window=window):
                    body(copy(way, 0, window, here, tokens_hbm.at[window]))

    for_sends(lambda each: each.start())
    loads[0].copy.wait()
    for part in range(mod_ref.shape[1] // width):
        cols = slice(part * width, (part + 1) * width)
        mod = dot(cond_ref[...], ada_ref[:, cols])
        mod_ref[:, cols] = mod[:8] + mod[8:16] + mod[16:24]
    loads[1].copy.wait()
    loads[2].copy.wait()
    loads[3].copy.wait()

    def project(window, shard, values):
        normed, _ = norm_rows(values.astype(f32))
        scale = 1.0 + mod_ref[pl.ds(window, 1), width : 2 * width]
        block = (normed * scale + mod_ref[pl.ds(window, 1), :width]).astype(bf16)
        at = pl.ds(pl.multiple_of(window * length + shard * rows, rows), rows)
        in_ref[at, :] = block
        kv_ref[at, :] = dot(block, weight_ref[:, width:]).astype(bf16)
        return block

    def own(window, carry):
        block = project(window, here, tokens_ref[window])
        at = pl.ds(pl.multiple_of(window * rows, rows), rows)
        q_ref[at, :] = dot(block, weight_ref[:, :width]).astype(bf16)
        return carry

    lax.fori_loop(0, windows, own, 0)

    def arrive(way, hop, window):
        sign = 1 - 2 * way
        shard = here - sign * (hop + 1)

        @pl.when((shard >= 0) & (shard < count))
        def _():
            copy(way, hop, window, shard).wait_recv()

            @pl.when((here + sign >= 0) & (here + sign < count))
            def _():
                copy(way, hop + 1, window, shard).start()

            project(window, shard, gathered[shard, window])

    def relay(at, carry):
        arrive(lax.rem(at, 2), at // (2 * windows), lax.rem(at // 2, windows))
        return carry

    lax.fori_loop(0, (count - 2) * windows * 2, relay, 0)

    def finish(window, carry):
        def last(way, inner):
            arrive(way, count - 2, window)
            return inner

        lax.fori_loop(0, 2, last, 0)
        rows_at = pl.ds(pl.multiple_of(window * rows, rows), rows)
        keys_at = pl.ds(pl.multiple_of(window * length, length), length)
        start = facts_ref[window]
        bins = bins_ref[window].T
        key_first = lax.broadcasted_iota(jnp.int32, bins.shape, 0) < start
        row_first = lax.broadcasted_iota(jnp.int32, bins.shape, 1) + here * rows < start
        index_ref[window] = bins + jnp.where(key_first == row_first, table_ref.shape[1] // 2, 0)

        def one_pair(pair, inner):
            begin = pl.multiple_of(pair * 2 * head_size, 2 * head_size)
            cols = pl.ds(begin, 2 * head_size)
            v_cols = pl.ds(width + begin, 2 * head_size)
            index = index_ref[window]
            biases = []
            for head in range(2):
                entries = jnp.broadcast_to(table_ref[pl.ds(2 * pair + head, 1), :], index.shape)
                biases.append(jnp.take_along_axis(entries, index, axis=1, mode="promise_in_bounds"))
            q_pair = pair_halves(q_ref[rows_at, cols] * head_scale, head_size)
            scores = dot_nt(kv_ref[keys_at, cols], q_pair) + jnp.concatenate(biases, axis=1)
            top = jnp.max(scores, axis=0, keepdims=True)
            raised = jnp.exp(scores - top)
            total = jnp.sum(raised, axis=0, keepdims=True)
            probs = (raised * (1.0 / total)).astype(bf16)
            mixed = dot(kv_ref[keys_at, v_cols].T, probs)
            mixed_ref[rows_at, cols] = pair_diagonal(mixed, head_size, rows).astype(bf16)
            probs_ref[window, pair] = probs
            return inner

        lax.fori_loop(0, width // (2 * head_size), one_pair, 0)
        return carry

    lax.fori_loop(0, windows, finish, 0)
    for_sends(lambda each: each.wait_send())

    def sent(at, carry):
        way, hop, window = (lax.rem(at, 2), at // (2 * windows), lax.rem(at // 2, windows))
        sign = 1 - 2 * way
        shard = here - sign * (hop + 1)

        @pl.when((shard >= 0) & (shard < count) & (here + sign >= 0) & (here + sign < count))
        def _():
            copy(way, hop + 1, window, shard).wait_send()

        return carry

    lax.fori_loop(0, (count - 2) * windows * 2, sent, 0)


def forward(facts, tokens, cond_parts, table, ada_weight, qkv_weight, bins, head_size):
    windows, rows, length = bins.shape
    width = tokens.shape[-1]
    pairs = width // (2 * head_size)
    count = lax.axis_size("seq")
    vmem = pl.BlockSpec(memory_space=pltpu.VMEM)
    hbm = pl.BlockSpec(memory_space=pltpu.HBM)
    return pl.pallas_call(
        functools.partial(forward_kernel, (windows, rows, length, head_size)),
        in_specs=[pl.BlockSpec(memory_space=pltpu.SMEM), hbm, vmem, vmem, hbm, hbm, hbm],
        out_specs=[vmem] * 7,
        out_shape=[
            jax.ShapeDtypeStruct((8, ada_weight.shape[1]), f32),
            jax.ShapeDtypeStruct((windows * rows, width), bf16),
            jax.ShapeDtypeStruct((windows * length, 2 * width), bf16),
            jax.ShapeDtypeStruct((windows * length, width), bf16),
            jax.ShapeDtypeStruct((windows * rows, width), bf16),
            jax.ShapeDtypeStruct((windows, pairs, length, 2 * rows), bf16),
            jax.ShapeDtypeStruct((windows, length, rows), jnp.int32),
        ],
        scratch_shapes=[
            pltpu.VMEM(ada_weight.shape, bf16),
            pltpu.VMEM(qkv_weight.shape, bf16),
            pltpu.VMEM(bins.shape, jnp.int32),
            pltpu.VMEM(tokens.shape, bf16),
            pltpu.SemaphoreType.DMA((4,)),
            pltpu.VMEM((count, windows, rows, width), bf16),
            pltpu.SemaphoreType.DMA((2, count - 1, windows)),
            pltpu.SemaphoreType.DMA((2, count - 1, windows)),
        ],
        compiler_params=pltpu.CompilerParams(
            collective_id=0, has_side_effects=True, vmem_limit_bytes=48 * 2**20
        ),
        cost_estimate=pl.CostEstimate(flops=10**10, bytes_accessed=40 * 2**20, transcendentals=0),
        name="forward",
    )(facts, tokens, cond_parts, table, ada_weight, qkv_weight, bins)


def bit_steps():
    win_bits = int(math.log2(lax.axis_size("win")))
    seq_bits = int(math.log2(lax.axis_size("seq")))
    return [("win", bit) for bit in range(win_bits)[::-1]] + [
        ("seq", bit) for bit in range(seq_bits)[::-1]
    ]


CORE = ("win", 0)


def my_bit(step):
    return lax.rem(lax.axis_index(step[0]) // (1 << step[1]), 2)


def partner(step):
    return {step[0]: lax.axis_index(step[0]) + (1 - 2 * my_bit(step)) * (1 << step[1])}


def greet():
    barrier = pltpu.get_barrier_semaphore()
    for step in bit_steps():
        pl.semaphore_signal(barrier, inc=1, device_id=partner(step), device_id_type=pl.DeviceIdType.MESH)
    pl.semaphore_wait(barrier, len(bit_steps()))


def remote(source, target, send_sem, recv_sem, step):
    return pltpu.make_async_remote_copy(
        src_ref=source,
        dst_ref=target,
        send_sem=send_sem,
        recv_sem=recv_sem,
        device_id=partner(step),
        device_id_type=pl.DeviceIdType.MESH,
    )


def each_block(shape, body):
    lead = shape[:-2]
    count = math.prod(lead)

    def one(flat, carry):
        index = []
        for size in lead[::-1]:
            index.append(lax.rem(flat, size))
            flat = flat // size
        body(tuple(index[::-1]))
        return carry

    if count == 1:
        body((0,) * len(lead))
    else:
        lax.fori_loop(0, count, one, 0)


class Flow:
    def __init__(self, rows, columns, chunks, flip, offset):
        steps = bit_steps()
        win_steps = [step for step in steps if step[0] == "win" and step != CORE]
        self.seq_steps = [step for step in steps if step[0] == "seq"]
        self.far = win_steps if flip else win_steps[::-1]
        self.names = win_steps
        self.near = self.seq_steps[::-1]
        self.chunks = chunks
        self.offset = offset
        self.width = columns // chunks
        self.share = rows // 2 ** len(steps)
        self.block = self.share * 2 ** len(self.seq_steps)
        self.columns = columns

    def view(self, grad):
        return grad.reshape((2,) * (len(self.far) + 1) + (self.block, self.columns))

    def scratch(self):
        chunks, width = (self.chunks, self.width)
        far, near = (len(self.far), len(self.near))
        shapes = [(2,) * far + (self.block, width)] * 2
        shapes += [(2,) * (far - 1 - i) + (self.block, width) for i in range(far)]
        shapes += [(2,) * near + (self.share, width)]
        shapes += [(2,) * (near - 1 - i) + (self.share, width) for i in range(near)]
        buffers = [pltpu.VMEM((chunks if at else 2,) + shape, bf16) for at, shape in enumerate(shapes)]
        count = 1 + far + near
        return buffers + [
            pltpu.SemaphoreType.DMA((chunks,)),
            pltpu.SemaphoreType.DMA((count, chunks)),
            pltpu.SemaphoreType.DMA((count, chunks)),
        ]

    def bind(self, grad, out, scratch):
        self.grad, self.out = grad, out
        far, near = (len(self.far), len(self.near))
        self.mine = scratch[0]
        self.first = scratch[1]
        self.far_bufs = list(scratch[2 : 2 + far])
        self.turn = scratch[2 + far]
        self.near_bufs = list(scratch[3 + far : 3 + far + near])
        self.local_sem, self.send_sem, self.recv_sem = scratch[3 + far + near :]

    def piece(self, bit, chunk):
        index = (slice(None),) * len(self.far) + (bit, slice(None))
        return self.grad.at[index + (pl.ds(pl.multiple_of(chunk * self.width, 128), self.width),)]

    def local_copy(self, chunk):
        return pltpu.make_async_copy(
            self.piece(my_bit(CORE), chunk), self.mine.at[lax.rem(chunk, 2)], self.local_sem.at[chunk]
        )

    def copy(self, stage, chunk):
        send, recv = (self.send_sem.at[stage, chunk], self.recv_sem.at[stage, chunk])
        far = len(self.far)
        if stage == 0:
            return remote(
                self.piece(1 - my_bit(CORE), chunk), self.first.at[chunk], send, recv, CORE
            )
        if stage <= far:
            step = self.far[stage - 1]
            source = ([self.first] + self.far_bufs)[stage - 1]
            target = self.far_bufs[stage - 1]
            axis = self.axis_of(step, self.far[: stage - 1], self.names)
        else:
            at = stage - 1 - far
            step = self.near[at]
            source = ([self.turn] + self.near_bufs)[at]
            target = self.near_bufs[at]
            axis = self.axis_of(step, self.near[:at], self.seq_steps)
        index = (chunk,) + (slice(None),) * axis + (1 - my_bit(step),)
        return remote(source.at[index], target.at[chunk], send, recv, step)

    def axis_of(self, step, gone, names):
        return [name for name in names if name not in gone].index(step)

    def stages(self):
        return 2 + len(self.far) + len(self.near)

    def run(self, stage, chunk):
        far, near = (len(self.far), len(self.near))
        if stage == 0:
            self.local_copy(chunk).start()
            self.copy(0, chunk).start()
            return
        self.copy(stage - 1, chunk).wait_recv()
        if stage == 1:
            self.local_copy(chunk).wait()
            shape = self.first.shape[1:]

            def add_first(index):
                at = (chunk,) + index
                kept = self.mine[(lax.rem(chunk, 2),) + index].astype(f32)
                self.first[at] = (self.first[at].astype(f32) + kept).astype(bf16)

            each_block(shape, add_first)
        elif stage < 1 + far:
            target = self.far_bufs[stage - 2]
            source = ([self.first] + self.far_bufs)[stage - 2]
            self.add_half(target, source, self.far, self.names, stage - 2, chunk)
        elif stage == 1 + far:
            step = self.far[-1]
            source = ([self.first] + self.far_bufs)[far - 1]
            target = self.far_bufs[far - 1]
            total = target[chunk].astype(f32) + source[chunk, my_bit(step)].astype(f32)
            total = total.astype(bf16)
            count = 2**near
            for owner in range(count):
                at, rest = ((), owner)
                for _ in range(near):
                    at = (rest % 2,) + at
                    rest = rest // 2
                self.turn[(chunk,) + at] = total[owner * self.share : (owner + 1) * self.share]
        elif stage < 1 + far + near:
            at = stage - 2 - far
            source = ([self.turn] + self.near_bufs)[at]
            self.add_half(self.near_bufs[at], source, self.near, self.seq_steps, at, chunk)
        else:
            source = ([self.turn] + self.near_bufs)[near - 1]
            kept = source[chunk, my_bit(self.near[-1])]
            total = self.near_bufs[near - 1][chunk].astype(f32) + kept.astype(f32)
            self.out[:, pl.ds(pl.multiple_of(chunk * self.width, 128), self.width)] = total
        if stage < 1 + far + near:
            self.copy(stage, chunk).start()

    def add_half(self, target, source, steps, names, at, chunk):
        step = steps[at]
        axis = self.axis_of(step, steps[:at], names)
        bit = my_bit(step)

        def add(index):
            from_at = (chunk,) + index[:axis] + (bit,) + index[axis:]
            to_at = (chunk,) + index
            target[to_at] = (target[to_at].astype(f32) + source[from_at].astype(f32)).astype(bf16)

        each_block(target.shape[1:], add)

    def drain(self, chunk):
        for stage in range(self.stages() - 1):
            self.copy(stage, chunk).wait_send()


class Load:
    def __init__(self, source, target, sem):
        self.target = target
        self.copy = pltpu.make_async_copy(source, target, sem)


class SmallGather:
    def __init__(self, mine, halves, gathered, send_sem, recv_sem):
        self.mine, self.halves, self.gathered = mine, halves, gathered
        self.send_sem, self.recv_sem = send_sem, recv_sem
        self.steps = bit_steps()[::-1]
        self.seq_count = len([step for step in self.steps if step[0] == "seq"])

    def copy(self, at):
        step = self.steps[at]
        if at < self.seq_count:
            source, target = self.mine.at[at], self.halves.at[at]
        else:
            size = 1 << step[1]
            here = lax.axis_index("win")
            block = pl.ds(here - lax.rem(here, size), size)
            source = target = self.gathered.at[block]
        return remote(source, target, self.send_sem.at[at], self.recv_sem.at[at], step)

    def run(self, at):
        if at > 0:
            self.copy(at - 1).wait_recv()
            if at <= self.seq_count:
                total = self.mine[at - 1] + self.halves[at - 1]
                if at < self.seq_count:
                    self.mine[at] = total
                else:
                    self.gathered[lax.axis_index("win")] = total
        if at < len(self.steps):
            self.copy(at).start()

    def drain(self):
        for at in range(len(self.steps)):
            self.copy(at).wait_send()


def norm_rows(values):
    centered = values - jnp.mean(values, axis=-1, keepdims=True)
    inv_std = lax.rsqrt(jnp.mean(centered * centered, axis=-1, keepdims=True) + norm_eps)
    return (centered * inv_std, inv_std)


def backward_kernel(flows, sizes, *refs):
    windows, rows, length, head_size = sizes
    refs = list(refs)

    def take(count):
        taken = refs[:count]
        del refs[:count]
        return taken

    grads = take(4)
    sources = take(9)
    (scale_ref,) = take(1)
    early_refs = take(6)
    shares = take(6)
    tokens_out, small_out = take(2)
    targets = take(9)
    (load_sem,) = take(1)
    grad_q, grad_kv, grad_scores, q_weight, kv_weight, own_in = take(6)
    far_in, far_half, far_own, far_send, far_recv = take(5)
    (table_sum,) = take(1)
    small = SmallGather(*take(5))
    (small_sem,) = take(1)
    for flow, grad, share in zip(flows, grads + [q_weight, kv_weight], shares):
        flow.bind(grad, share, take(len(flow.scratch())))
    loads = [Load(s, t, load_sem.at[at]) for at, (s, t) in enumerate(zip(sources, targets))]
    q_ref, kv_ref, probs_ref, grad_ref, in_ref, weight_ref, index_ref, tokens_ref, hidden_ref = targets
    width = q_ref.shape[1]
    head_scale = 1.0 / math.sqrt(head_size)
    heads = width // head_size
    seq_steps = bit_steps()[::-1][: small.seq_count]
    for load in loads:
        load.copy.start()
    greet()

    def attend_back(window):
        rows_at = pl.ds(pl.multiple_of(window * rows, rows), rows)
        keys_at = pl.ds(pl.multiple_of(window * length, length), length)

        def one_pair(pair, carry):
            start = pl.multiple_of(pair * 2 * head_size, 2 * head_size)
            cols = pl.ds(start, 2 * head_size)
            v_cols = pl.ds(width + start, 2 * head_size)
            q_pair = pair_halves(q_ref[rows_at, cols] * head_scale, head_size)
            g_pair = pair_halves(grad_ref[rows_at, cols], head_size)
            probs = probs_ref[window, pair]
            grad_kv[keys_at, v_cols] = dot(probs, g_pair).astype(bf16)
            grad_probs = dot_nt(kv_ref[keys_at, v_cols], g_pair)
            probs = probs.astype(f32)
            delta = jnp.sum(probs * grad_probs, axis=0, keepdims=True)
            scores = (probs * (grad_probs - delta)).astype(bf16)
            grad_kv[keys_at, cols] = dot(scores, q_pair).astype(bf16)
            back = dot(kv_ref[keys_at, cols].T, scores)
            grad_q[rows_at, cols] = (pair_diagonal(back, head_size, rows) * head_scale).astype(bf16)
            grad_scores[window, 2 * pair] = scores[:, :rows]
            grad_scores[window, 2 * pair + 1] = scores[:, rows:]
            return carry

        lax.fori_loop(0, heads // 2, one_pair, 0)

    def split_rows(target, values, cols):
        lead = target.shape[:-2]
        block = target.shape[-2]
        for at in range(math.prod(lead)):
            index, rest = ((), at)
            for size in lead[::-1]:
                index = (rest % size,) + index
                rest = rest // size
            target[index + (slice(None), cols)] = values[at * block : (at + 1) * block].astype(bf16)

    def project_back():
        def one_window(window, carry):
            keys_at = pl.ds(pl.multiple_of(window * length, length), length)
            far = dot_nt(grad_kv[keys_at, :], weight_ref[:, width:]).astype(bf16)
            split_owner(far, window)
            return carry

        def split_owner(far, window):
            rows_at = pl.ds(pl.multiple_of(window * rows, rows), rows)
            for owner in range(length // rows):
                index, rest = ((), owner)
                for _ in seq_steps:
                    index = (rest % 2,) + index
                    rest = rest // 2
                far_in[index + (rows_at,)] = far[owner * rows : (owner + 1) * rows]

        lax.fori_loop(0, windows, one_window, 0)
        far_copy(0).start()
        own_in[...] = dot_nt(grad_q[...], weight_ref[:, :width])

    def weight_grads():
        here = lax.axis_index("seq") * rows
        own = [in_ref[pl.ds(pl.multiple_of(w * length + here, rows), rows), :] for w in range(windows)]
        split_rows(q_weight, dot(jnp.concatenate(own, axis=0).T, grad_q[...]), slice(None))
        turned = in_ref[...].T
        step = 512
        for at in range(2 * width // step):
            cols = slice(at * step, (at + 1) * step)
            split_rows(kv_weight, dot(turned, grad_kv[:, cols]), cols)

    far_bufs = [far_in] + [far_half, far_own][-small.seq_count :]

    def far_copy(at):
        step = seq_steps[at]
        index = (slice(None),) * (small.seq_count - 1 - at) + (1 - my_bit(step),)
        return remote(
            far_bufs[at].at[index], far_bufs[at + 1], far_send.at[at], far_recv.at[at], step
        )

    def far_add(at):
        far_copy(at).wait_recv()
        step = seq_steps[at]
        bit = my_bit(step)
        target, source = far_bufs[at + 1], far_bufs[at]
        lead = target.shape[:-2]
        for flat in range(math.prod(lead)):
            for window in range(windows):
                index = ((flat,) if lead else ()) + (pl.ds(window * rows, rows),)
                kept = source[index[:-1] + (bit,) + index[-1:]].astype(f32)
                target[index] = (target[index].astype(f32) + kept).astype(bf16)
        if at + 1 < small.seq_count:
            far_copy(at + 1).start()

    def table_back(window):
        group = 16
        entries = table_sum.shape[1]

        def one_group(at, carry):
            keys = pl.ds(pl.multiple_of(at * group, group), group)
            scores = grad_scores[window, :, keys, :].astype(f32)
            scores = jnp.concatenate([scores, jnp.zeros((16 - heads, group, rows), f32)], axis=0)
            scores = jnp.swapaxes(scores, 0, 1).astype(bf16)
            index = index_ref[window, keys, :]
            spot = lax.broadcasted_iota(jnp.int32, (entries, rows), 0)
            total = jnp.zeros((16, entries), f32)
            for key in range(0, group, 2):
                terms, hots = [], []
                for which in (key, key + 1):
                    terms.append(scores[which])
                    hot = spot == jnp.broadcast_to(index[which : which + 1], (entries, rows))
                    hots.append(jnp.where(hot, 1.0, 0.0).astype(bf16))
                total = total + dot_nt(
                    jnp.concatenate(terms, axis=1), jnp.concatenate(hots, axis=1)
                )
            table_sum[...] += total
            return carry

        lax.fori_loop(0, length // group, one_group, 0)

    def finish_tokens():
        shift_rows, scale_rows = [], []
        for window in range(windows):
            rows_at = pl.ds(window * rows, rows)
            normed, inv_std = norm_rows(tokens_ref[rows_at, :].astype(f32))
            grad_in = own_in[rows_at, :] + far_own[rows_at, :].astype(f32)
            shift_rows.append(jnp.sum(grad_in, axis=0, keepdims=True))
            scale_rows.append(jnp.sum(grad_in * normed, axis=0, keepdims=True))
            dy = grad_in * scale_ref[pl.ds(window, 1), :]
            first = jnp.mean(dy, axis=-1, keepdims=True)
            second = jnp.mean(dy * normed, axis=-1, keepdims=True)
            back = (dy - first - normed * second) * inv_std
            tokens_out[rows_at, :] = (hidden_ref[rows_at, :] + back).astype(bf16)
        facts = jnp.concatenate(shift_rows + scale_rows + [early[...] for early in early_refs], axis=0)
        small.mine[0, :, :width] = facts
        small.mine[0, :, width:] = table_sum[...]

    steps = len(small.steps)
    jobs = {}
    for window in range(windows):
        jobs.setdefault(window, []).append(functools.partial(attend_back, window))
    jobs.setdefault(windows, []).extend([project_back, weight_grads])
    jobs.setdefault(windows + 1, []).append(functools.partial(table_back, 0))
    jobs.setdefault(windows + 2, []).append(functools.partial(far_add, 0))
    for window in range(1, windows):
        jobs.setdefault(windows + 2 + window, []).append(functools.partial(table_back, window))
    last = 2 * windows + 2
    for at in range(1, small.seq_count):
        jobs.setdefault(last + 2 * (at - 1), []).append(functools.partial(far_add, at))
    last = last + 2 * (small.seq_count - 2)
    jobs[last].append(finish_tokens)
    for at in range(steps + 1):
        jobs.setdefault(last + at, []).append(functools.partial(small.run, at))
    chunks = flows[0].chunks
    stages = flows[0].stages()
    order = [1, 0] + list(range(2, stages))
    total = max(max(flow.offset for flow in flows) + chunks + stages - 1, max(jobs) + 1)
    table_sum[...] = jnp.zeros_like(table_sum)

    def step(at, carry):
        for stage in order:
            for offset in sorted({flow.offset for flow in flows}):
                chunk = at - stage - offset

                @pl.when((chunk >= 0) & (chunk < chunks))
                def _(stage=stage, chunk=chunk, offset=offset):
                    for flow in flows:
                        if flow.offset == offset:
                            flow.run(stage, chunk)

            if stage == 0:

                @pl.when(at == 0)
                def _():
                    for load in loads:
                        load.copy.wait()

                for when, work in sorted(jobs.items()):

                    @pl.when(at == when)
                    def _(work=work):
                        for job in work:
                            job()

        return carry

    lax.fori_loop(0, total, step, 0)
    store_small = pltpu.make_async_copy(small.gathered, small_out, small_sem)
    store_small.start()

    def finish(chunk, carry):
        for flow in flows:
            flow.drain(chunk)
        return carry

    lax.fori_loop(0, chunks, finish, 0)
    for at in range(small.seq_count):
        far_copy(at).wait_send()
    small.drain()
    store_small.wait()


def backward(grads, loads, scales, early, sizes, chunks, flips):
    windows, rows, length, head_size = sizes
    width = loads[0].shape[1]
    shapes = [g.shape for g in grads] + [(width, width), (width, 2 * width)]
    offsets = [0] * len(grads) + [windows + 1] * 2
    flows = [Flow(s[0], s[1], chunks, flip, offset) for s, flip, offset in zip(shapes, flips, offsets)]
    win_bits = int(math.log2(lax.axis_size("win")))
    seq_bits = int(math.log2(lax.axis_size("seq")))
    total_rows = windows * rows
    small_shape = (16, width + 128)
    heads = width // head_size
    near = (2,) * seq_bits
    scratch = [pltpu.VMEM(load.shape, load.dtype) for load in loads]
    scratch += [
        pltpu.SemaphoreType.DMA((len(loads),)),
        pltpu.VMEM((total_rows, width), bf16),
        pltpu.VMEM((windows * length, 2 * width), bf16),
        pltpu.VMEM((windows, heads, length, rows), bf16),
        pltpu.VMEM((2,) * win_bits + (flows[-2].block, width), bf16),
        pltpu.VMEM((2,) * win_bits + (flows[-1].block, 2 * width), bf16),
        pltpu.VMEM((total_rows, width), f32),
        pltpu.VMEM(near + (total_rows, width), bf16),
        pltpu.VMEM(near[1:] + (total_rows, width), bf16),
        pltpu.VMEM((total_rows, width), bf16),
        pltpu.SemaphoreType.DMA((seq_bits,)),
        pltpu.SemaphoreType.DMA((seq_bits,)),
        pltpu.VMEM((16, 128), f32),
        pltpu.VMEM((seq_bits,) + small_shape, f32),
        pltpu.VMEM((seq_bits,) + small_shape, f32),
        pltpu.VMEM((2**win_bits,) + small_shape, f32),
        pltpu.SemaphoreType.DMA((win_bits + seq_bits,)),
        pltpu.SemaphoreType.DMA((win_bits + seq_bits,)),
        pltpu.SemaphoreType.DMA,
    ]
    for flow in flows:
        scratch += flow.scratch()
    vmem = pl.BlockSpec(memory_space=pltpu.VMEM)
    out_shape = [jax.ShapeDtypeStruct((flow.share, flow.columns), f32) for flow in flows]
    out_shape += [
        jax.ShapeDtypeStruct((total_rows, width), bf16),
        jax.ShapeDtypeStruct((2**win_bits,) + small_shape, f32),
    ]
    return pl.pallas_call(
        functools.partial(backward_kernel, flows, sizes),
        in_specs=[pl.BlockSpec(memory_space=pl.ANY)] * (len(grads) + len(loads)) + [vmem] * (1 + len(early)),
        out_specs=[vmem] * (len(out_shape) - 1) + [pl.BlockSpec(memory_space=pl.ANY)],
        out_shape=out_shape,
        scratch_shapes=scratch,
        compiler_params=pltpu.CompilerParams(
            collective_id=1, has_side_effects=True, vmem_limit_bytes=62 * 2**20
        ),
        cost_estimate=pl.CostEstimate(flops=10**10, bytes_accessed=200 * 2**20, transcendentals=0),
        name="backward",
    )(*[flow.view(grad) for flow, grad in zip(flows, grads)], *loads, scales, *early)


def tail_kernel(windows, *refs):
    gate, up, down, out, q, kv, tokens, small, ada_hbm, pair_table, pair_weight = refs[:11]
    to_gate, to_up, to_down, to_out, to_qkv, to_tokens, to_class, to_ada, to_table, to_weight = refs[11:21]
    by_row, cond_t, pre_t, onehot_t, table_flat, weight_rows, padded, ada_rows, cond_grad, ada_sem = refs[21:]
    width = tokens.shape[1]
    owner = lax.axis_index("win") * lax.axis_size("seq") + lax.axis_index("seq")
    share = to_class.shape[1]
    per_class = width // share
    column_at = lax.rem(owner, per_class) * share
    window_at = pl.multiple_of(jnp.minimum(column_at // 16 * 16, width - ada_rows.shape[0]), 16)
    load_ada = pltpu.make_async_copy(ada_hbm.at[pl.ds(window_at, ada_rows.shape[0]), :], ada_rows, ada_sem)
    load_ada.start()

    def flatten(target, values, columns, first):
        rows = values.shape[0]
        for at in range(values.shape[1] // 128):
            spot = pl.ds(first // 128 + at, rows, stride=columns // 128)
            target[spot, :] = values[:, at * 128 : (at + 1) * 128]

    for target, source in ((to_gate, gate), (to_up, up), (to_down, down), (to_out, out)):
        flatten(target, source, source.shape[1], 0)
    flatten(to_qkv, q, 3 * width, 0)
    flatten(to_qkv, kv, 3 * width, width)
    to_tokens[...] = tokens[...]

    groups = small.shape[0]

    def sort_rows(group, carry):
        for which in range(8):
            for window in range(windows):
                row = small[group, pl.ds(which * windows + window, 1), :width]
                by_row[pl.ds(window * groups + group, 1), which * width : (which + 1) * width] = row
        return carry

    lax.fori_loop(0, groups, sort_rows, 0)

    def rows_of(which):
        return by_row[:, which * width : (which + 1) * width]

    mods = [rows_of(part) for part in range(6)]
    pre = rows_of(6)
    cond_t[...] = (pre * jax.nn.sigmoid(pre)).T
    pre_t[...] = pre.T
    onehot_t[...] = rows_of(7).T
    ada_share = width // (lax.axis_size("win") * lax.axis_size("seq"))
    cond_rows = cond_t[pl.ds(owner * ada_share, ada_share), :]
    grad_cond = jnp.zeros((ada_rows.shape[0], pre.shape[0]), f32)
    load_ada.wait()
    for part, mod in enumerate(mods):
        product = jnp.dot(cond_rows, mod, precision=highest, preferred_element_type=f32)
        flatten(to_ada, product, 6 * width, part * width)
        grad_cond = grad_cond + lax.dot_general(
            ada_rows[:, part * width : (part + 1) * width].astype(f32),
            mod,
            (((1,), (1,)), ((), ())),
            precision=highest,
            preferred_element_type=f32,
        )
    cond_grad[...] = grad_cond
    grad_cond = cond_grad[pl.ds(column_at - window_at, share), :]
    pre_cols = pre_t[pl.ds(column_at, share), :]
    sig_cols = jax.nn.sigmoid(pre_cols)
    grad_pre = grad_cond * sig_cols * (1.0 + pre_cols * (1.0 - sig_cols))
    mine = jnp.broadcast_to(onehot_t[pl.ds(owner // per_class, 1), :], (8, pre.shape[0]))
    of_class = lax.dot_general(
        mine, grad_pre, (((1,), (1,)), ((), ())), precision=highest, preferred_element_type=f32
    )
    to_class[...] = of_class[:1]

    table = jnp.sum(small[:, :, width:], axis=0)
    heads = pair_weight.shape[1]
    padded[...] = jnp.zeros_like(padded)
    padded[:, :heads] = pair_weight[...].astype(f32)
    grad_table = lax.dot_general(
        table.T, padded[...], (((1,), (1,)), ((), ())), precision=highest, preferred_element_type=f32
    )
    flatten(table_flat, grad_table, grad_table.shape[1], 0)
    count = to_table.shape[0]
    to_table[...] = table_flat[pl.ds(owner * count, count), :]
    grad_weight = jnp.dot(
        table, pair_table[...].astype(f32), precision=highest, preferred_element_type=f32
    )
    weight_rows[...] = grad_weight.T
    count = to_weight.shape[1] // heads
    mine = weight_rows[pl.ds(owner * count, count), :]
    head = lax.broadcasted_iota(jnp.int32, (16, 128), 0)
    lane = lax.broadcasted_iota(jnp.int32, (16, 128), 1)
    spread = jnp.dot(
        mine,
        jnp.where(lax.rem(lane, heads) == head, 1.0, 0.0),
        precision=highest,
        preferred_element_type=f32,
    )
    row = lax.broadcasted_iota(jnp.int32, spread.shape, 0)
    lane = lax.broadcasted_iota(jnp.int32, spread.shape, 1)
    spread = jnp.sum(jnp.where(lane // heads == row, spread, 0.0), axis=0, keepdims=True)
    to_weight[...] = spread[:, : to_weight.shape[1]]


def tail(shares, tokens, small, ada_weight, pair_table, pair_weight, windows, class_share):
    width = tokens.shape[1]
    devices = lax.axis_size("win") * lax.axis_size("seq")
    features = pair_table.shape[1]
    span = class_share if class_share % 16 == 0 else -(-(class_share + 15) // 16) * 16
    sizes = [share.size for share in shares[:4]] + [shares[4].size + shares[5].size]
    table_size = pair_table.size // devices
    ada_size = ada_weight.size // devices
    every = windows * small.shape[0]
    vmem = pl.BlockSpec(memory_space=pltpu.VMEM)

    def flat(size):
        return jax.ShapeDtypeStruct((size // 128, 128), f32)

    return pl.pallas_call(
        functools.partial(tail_kernel, windows),
        in_specs=[vmem] * 8 + [pl.BlockSpec(memory_space=pl.ANY)] + [vmem] * 2,
        out_specs=[vmem] * 10,
        out_shape=[flat(size) for size in sizes]
        + [
            jax.ShapeDtypeStruct(tokens.shape, bf16),
            jax.ShapeDtypeStruct((1, class_share), f32),
            flat(ada_size),
            flat(table_size),
            jax.ShapeDtypeStruct((1, pair_weight.size // devices), f32),
        ],
        scratch_shapes=[pltpu.VMEM((every, 8 * width), f32)]
        + [pltpu.VMEM((width, every), f32)] * 3
        + [
            pltpu.VMEM((pair_table.size // 128, 128), f32),
            pltpu.VMEM((features, 16), f32),
            pltpu.VMEM((features, 16), f32),
            pltpu.VMEM((span, ada_weight.shape[1]), bf16),
            pltpu.VMEM((span, every), f32),
            pltpu.SemaphoreType.DMA,
        ],
        name="tail",
    )(*shares, tokens, small, ada_weight, pair_table, pair_weight)


def three_parts(values):
    parts = []
    for _ in range(3):
        part = lax.reduce_precision(values, 8, 7)
        parts.append(part.astype(bf16))
        values = values - part
    return parts


def per_device(
    tokens,
    cotangent,
    noise_times,
    cath_ids,
    chain_start,
    distance_bins,
    class_table,
    ada_weight,
    qkv_weight,
    out_weight,
    pair_table,
    pair_weight,
    gate_weight,
    up_weight,
    down_weight,
):
    windows, row_count, width = tokens.shape
    length = distance_bins.shape[2]
    head_count = pair_weight.shape[1]
    head_size = width // head_count
    table_rows = pair_table.shape[0]
    bin_count = table_rows // 2
    classes = class_table.shape[0]
    total_rows = windows * row_count
    win_count = lax.axis_size("win")
    seq_count = lax.axis_size("seq")
    devices = win_count * seq_count
    class_onehot = (cath_ids[:, None] == jnp.arange(classes, dtype=jnp.int32)[None, :]).astype(f32)
    pre_cond = jnp.dot(
        class_onehot, class_table.astype(f32), precision=highest
    ) + time_embed(noise_times, width)
    cond_sig = jax.nn.sigmoid(pre_cond)
    condition = pre_cond * cond_sig
    cond_parts = jnp.concatenate(
        [jnp.pad(part, ((0, 8 - windows), (0, 0))) for part in three_parts(condition)], axis=0
    )
    table_bias = dot(pair_table, pair_weight).astype(bf16)
    modulation, queries, keys_values, attn_in_all, attn_mixed, probs, pair_index = forward(
        chain_start,
        tokens,
        cond_parts,
        table_bias.astype(f32).T,
        ada_weight,
        qkv_weight,
        distance_bins,
        head_size,
    )
    modulation = modulation[:windows].reshape(windows, 6, width)
    shift_attn = modulation[:, 0][:, None, :]
    scale_attn = modulation[:, 1][:, None, :]
    gate_attn = modulation[:, 2][:, None, :]
    shift_ffn = modulation[:, 3][:, None, :]
    scale_ffn = modulation[:, 4][:, None, :]
    gate_ffn = modulation[:, 5][:, None, :]
    tokens_float = tokens.astype(f32)
    attn_out = dot(attn_mixed, out_weight).reshape(windows, row_count, width)
    gate_attn_sig = jax.nn.sigmoid(gate_attn)
    hidden_state = tokens_float + gate_attn_sig * attn_out
    normed_h, inv_h = layer_norm_parts(hidden_state)
    ffn_in = (normed_h * (1.0 + scale_ffn) + shift_ffn).astype(bf16).reshape(total_rows, width)
    gate_val = dot(ffn_in, gate_weight)
    up_val = dot(ffn_in, up_weight)
    gate_sig = jax.nn.sigmoid(gate_val)
    silu_gate = gate_val * gate_sig
    ffn_hidden = (silu_gate * up_val).astype(bf16)
    gate_ffn_sig = jax.nn.sigmoid(gate_ffn)
    grad_layer = cotangent.astype(f32)
    grad_ffn = (gate_ffn_sig * grad_layer).astype(bf16).reshape(total_rows, width)
    grad_down = dot_tn(ffn_hidden, grad_ffn).astype(bf16)
    ffn_out = dot(ffn_hidden, down_weight).reshape(windows, row_count, width)
    layer_out = (hidden_state + gate_ffn_sig * ffn_out).astype(bf16)
    grad_gate_ffn = jnp.sum(grad_layer * ffn_out * gate_ffn_sig * (1.0 - gate_ffn_sig), axis=1)
    grad_hidden_ffn = dot_nt(grad_ffn, down_weight)
    grad_up_val = (grad_hidden_ffn * silu_gate).astype(bf16)
    grad_gate_val = (
        grad_hidden_ffn * up_val * gate_sig * (1.0 + gate_val * (1.0 - gate_sig))
    ).astype(bf16)
    grad_gate = dot_tn(ffn_in, grad_gate_val).astype(bf16)
    grad_up = dot_tn(ffn_in, grad_up_val).astype(bf16)
    grad_ffn_in = dot_nt(grad_gate_val, gate_weight) + dot_nt(grad_up_val, up_weight)
    grad_ffn_in = grad_ffn_in.reshape(windows, row_count, width)
    grad_scale_ffn = jnp.sum(grad_ffn_in * normed_h, axis=1)
    grad_shift_ffn = jnp.sum(grad_ffn_in, axis=1)
    grad_hidden = grad_layer + norm_back(grad_ffn_in * (1.0 + scale_ffn), normed_h, inv_h)
    grad_attn_out = (gate_attn_sig * grad_hidden).astype(bf16).reshape(total_rows, width)
    grad_gate_attn = jnp.sum(grad_hidden * attn_out * gate_attn_sig * (1.0 - gate_attn_sig), axis=1)
    grad_out = dot_tn(attn_mixed, grad_attn_out).astype(bf16)
    grad_mixed = dot_nt(grad_attn_out, out_weight).astype(bf16)

    early = [
        grad_gate_attn,
        grad_shift_ffn,
        grad_scale_ffn,
        grad_gate_ffn,
        pre_cond / seq_count,
        jnp.pad(class_onehot, ((0, 0), (0, width - classes))) / seq_count,
    ]
    owned_gate, owned_up, owned_down, owned_out, owned_q, owned_kv, grad_tokens, small = backward(
        [grad_gate, grad_up, grad_down, grad_out],
        [
            queries,
            keys_values,
            probs,
            grad_mixed,
            attn_in_all,
            qkv_weight,
            pair_index,
            tokens.reshape(total_rows, width),
            grad_hidden.reshape(total_rows, width),
        ],
        1.0 + scale_attn.reshape(windows, width),
        early,
        (windows, row_count, length, head_size),
        6,
        [False, True, False, True, True, True],
    )
    class_share = classes * width // devices
    flat_gate, flat_up, flat_down, flat_out, flat_qkv, grad_tokens, of_class, flat_ada, of_table, of_weight = tail(
        [owned_gate, owned_up, owned_down, owned_out, owned_q, owned_kv],
        grad_tokens,
        small,
        ada_weight,
        pair_table,
        pair_weight,
        windows,
        class_share,
    )
    return (
        layer_out,
        grad_tokens.reshape(windows, row_count, width),
        of_class.reshape(-1),
        flat_ada.reshape(-1),
        flat_qkv.reshape(-1),
        flat_out.reshape(-1),
        of_table.reshape(-1),
        of_weight.reshape(-1),
        flat_gate.reshape(-1),
        flat_up.reshape(-1),
        flat_down.reshape(-1),
    )


def solution(mesh):
    rows = P("win", "seq", None)
    flat = P(("win", "seq"))
    placed = (rows, rows, P("win"), P("win"), P("win"), rows) + (P(),) * 9
    return jax.shard_map(
        per_device, mesh=mesh, in_specs=placed, out_specs=(rows, rows) + (flat,) * 9, check_vma=False
    )
```

```python
import functools
import math

import jax
import jax.numpy as jnp
from jax import lax
from jax.experimental import pallas as pl
from jax.experimental.pallas import tpu as pltpu
from jax.sharding import PartitionSpec as P

highest = lax.Precision.HIGHEST
norm_eps = 1e-06
f32 = jnp.float32
bf16 = jnp.bfloat16


def norm_back(grad_normed, normed, inv_std):
    first_mean = jnp.mean(grad_normed, axis=-1, keepdims=True)
    second_mean = jnp.mean(grad_normed * normed, axis=-1, keepdims=True)
    return (grad_normed - first_mean - normed * second_mean) * inv_std


def time_embed(noise_times, model_width):
    half_width = model_width // 2
    frequency = jnp.exp(
        -math.log(10000.0) * jnp.arange(half_width).astype(f32) / half_width
    )
    angles = 1000.0 * noise_times[:, None] * frequency[None, :]
    return jnp.concatenate([jnp.sin(angles), jnp.cos(angles)], axis=-1)


def dot(a, b):
    return jnp.dot(a, b, preferred_element_type=f32)


def dot_nt(a, b):
    return lax.dot_general(a, b, (((1,), (1,)), ((), ())), preferred_element_type=f32)


def dot_tn(a, b):
    return lax.dot_general(a, b, (((0,), (0,)), ((), ())), preferred_element_type=f32)


def pair_halves(values, head_size):
    lane = lax.broadcasted_iota(jnp.int32, values.shape, 1)
    zero = jnp.zeros_like(values)
    return jnp.concatenate(
        [jnp.where(lane < head_size, values, zero), jnp.where(lane >= head_size, values, zero)], axis=0
    )


def pair_diagonal(values, head_size, rows):
    return jnp.concatenate([values[:head_size, :rows], values[head_size:, rows:]], axis=0).T


def forward_kernel(
    sizes,
    facts_ref,
    tokens_hbm,
    cond_ref,
    table_ref,
    ada_hbm,
    weight_hbm,
    bins_hbm,
    mod_ref,
    q_ref,
    kv_ref,
    in_ref,
    mixed_ref,
    probs_ref,
    index_ref,
    ada_ref,
    weight_ref,
    bins_ref,
    tokens_ref,
    load_sem,
    gathered,
    send_sem,
    recv_sem,
):
    windows, rows, length, head_size = sizes
    width = q_ref.shape[1]
    count = gathered.shape[0]
    here = lax.axis_index("seq")
    head_scale = 1.0 / math.sqrt(head_size)
    loads = [
        Load(source, target, load_sem.at[at])
        for at, (source, target) in enumerate(
            [(ada_hbm, ada_ref), (weight_hbm, weight_ref), (bins_hbm, bins_ref), (tokens_hbm, tokens_ref)]
        )
    ]
    for load in loads:
        load.copy.start()
    barrier = pltpu.get_barrier_semaphore()
    for sign in (1, -1):

        @pl.when((here + sign >= 0) & (here + sign < count))
        def _(sign=sign):
            pl.semaphore_signal(
                barrier, inc=1, device_id={"seq": here + sign}, device_id_type=pl.DeviceIdType.MESH
            )

    pl.semaphore_wait(barrier, jnp.where((here == 0) | (here == count - 1), 1, 2))

    def copy(way, hop, window, shard, source=None):
        slot = gathered.at[shard, window]
        return pltpu.make_async_remote_copy(
            src_ref=slot if source is None else source,
            dst_ref=slot,
            send_sem=send_sem.at[way, hop, window],
            recv_sem=recv_sem.at[way, hop, window],
            device_id={"seq": here + 1 - 2 * way},
            device_id_type=pl.DeviceIdType.MESH,
        )

    def for_sends(body):
        for window in range(windows):
            for way in range(2):

                @pl.when((here + 1 - 2 * way >= 0) & (here + 1 - 2 * way < count))
                def _(way=way, window=window):
                    body(copy(way, 0, window, here, tokens_hbm.at[window]))

    for_sends(lambda each: each.start())
    loads[0].copy.wait()
    for part in range(mod_ref.shape[1] // width):
        cols = slice(part * width, (part + 1) * width)
        mod = dot(cond_ref[...], ada_ref[:, cols])
        mod_ref[:, cols] = mod[:8] + mod[8:16] + mod[16:24]
    loads[1].copy.wait()
    loads[2].copy.wait()
    loads[3].copy.wait()

    def project(window, shard, values):
        normed, _ = norm_rows(values.astype(f32))
        scale = 1.0 + mod_ref[pl.ds(window, 1), width : 2 * width]
        block = (normed * scale + mod_ref[pl.ds(window, 1), :width]).astype(bf16)
        at = pl.ds(pl.multiple_of(window * length + shard * rows, rows), rows)
        in_ref[at, :] = block
        kv_ref[at, :] = dot(block, weight_ref[:, width:]).astype(bf16)
        return block

    def own(window, carry):
        block = project(window, here, tokens_ref[window])
        at = pl.ds(pl.multiple_of(window * rows, rows), rows)
        q_ref[at, :] = dot(block, weight_ref[:, :width]).astype(bf16)
        return carry

    lax.fori_loop(0, windows, own, 0)

    def arrive(way, hop, window):
        sign = 1 - 2 * way
        shard = here - sign * (hop + 1)

        @pl.when((shard >= 0) & (shard < count))
        def _():
            copy(way, hop, window, shard).wait_recv()

            @pl.when((here + sign >= 0) & (here + sign < count))
            def _():
                copy(way, hop + 1, window, shard).start()

            project(window, shard, gathered[shard, window])

    def relay(at, carry):
        arrive(lax.rem(at, 2), at // (2 * windows), lax.rem(at // 2, windows))
        return carry

    lax.fori_loop(0, (count - 2) * windows * 2, relay, 0)

    def finish(window, carry):
        def last(way, inner):
            arrive(way, count - 2, window)
            return inner

        lax.fori_loop(0, 2, last, 0)
        rows_at = pl.ds(pl.multiple_of(window * rows, rows), rows)
        keys_at = pl.ds(pl.multiple_of(window * length, length), length)
        start = facts_ref[window]
        bins = bins_ref[window].T
        key_first = lax.broadcasted_iota(jnp.int32, bins.shape, 0) < start
        row_first = lax.broadcasted_iota(jnp.int32, bins.shape, 1) + here * rows < start
        index_ref[window] = bins + jnp.where(key_first == row_first, table_ref.shape[1] // 2, 0)

        def one_pair(pair, inner):
            begin = pl.multiple_of(pair * 2 * head_size, 2 * head_size)
            cols = pl.ds(begin, 2 * head_size)
            v_cols = pl.ds(width + begin, 2 * head_size)
            index = index_ref[window]
            biases = []
            for head in range(2):
                entries = jnp.broadcast_to(table_ref[pl.ds(2 * pair + head, 1), :], index.shape)
                biases.append(jnp.take_along_axis(entries, index, axis=1, mode="promise_in_bounds"))
            q_pair = pair_halves(q_ref[rows_at, cols] * head_scale, head_size)
            scores = dot_nt(kv_ref[keys_at, cols], q_pair) + jnp.concatenate(biases, axis=1)
            top = jnp.max(scores, axis=0, keepdims=True)
            raised = jnp.exp(scores - top)
            total = jnp.sum(raised, axis=0, keepdims=True)
            probs = (raised * (1.0 / total)).astype(bf16)
            mixed = dot(kv_ref[keys_at, v_cols].T, probs)
            mixed_ref[rows_at, cols] = pair_diagonal(mixed, head_size, rows).astype(bf16)
            probs_ref[window, pair] = probs
            return inner

        lax.fori_loop(0, width // (2 * head_size), one_pair, 0)
        return carry

    lax.fori_loop(0, windows, finish, 0)
    for_sends(lambda each: each.wait_send())

    def sent(at, carry):
        way, hop, window = (lax.rem(at, 2), at // (2 * windows), lax.rem(at // 2, windows))
        sign = 1 - 2 * way
        shard = here - sign * (hop + 1)

        @pl.when((shard >= 0) & (shard < count) & (here + sign >= 0) & (here + sign < count))
        def _():
            copy(way, hop + 1, window, shard).wait_send()

        return carry

    lax.fori_loop(0, (count - 2) * windows * 2, sent, 0)


def forward(facts, tokens, cond_parts, table, ada_weight, qkv_weight, bins, head_size):
    windows, rows, length = bins.shape
    width = tokens.shape[-1]
    pairs = width // (2 * head_size)
    count = lax.axis_size("seq")
    vmem = pl.BlockSpec(memory_space=pltpu.VMEM)
    hbm = pl.BlockSpec(memory_space=pltpu.HBM)
    return pl.pallas_call(
        functools.partial(forward_kernel, (windows, rows, length, head_size)),
        in_specs=[pl.BlockSpec(memory_space=pltpu.SMEM), hbm, vmem, vmem, hbm, hbm, hbm],
        out_specs=[vmem] * 7,
        out_shape=[
            jax.ShapeDtypeStruct((8, ada_weight.shape[1]), f32),
            jax.ShapeDtypeStruct((windows * rows, width), bf16),
            jax.ShapeDtypeStruct((windows * length, 2 * width), bf16),
            jax.ShapeDtypeStruct((windows * length, width), bf16),
            jax.ShapeDtypeStruct((windows * rows, width), bf16),
            jax.ShapeDtypeStruct((windows, pairs, length, 2 * rows), bf16),
            jax.ShapeDtypeStruct((windows, length, rows), jnp.int32),
        ],
        scratch_shapes=[
            pltpu.VMEM(ada_weight.shape, bf16),
            pltpu.VMEM(qkv_weight.shape, bf16),
            pltpu.VMEM(bins.shape, jnp.int32),
            pltpu.VMEM(tokens.shape, bf16),
            pltpu.SemaphoreType.DMA((4,)),
            pltpu.VMEM((count, windows, rows, width), bf16),
            pltpu.SemaphoreType.DMA((2, count - 1, windows)),
            pltpu.SemaphoreType.DMA((2, count - 1, windows)),
        ],
        compiler_params=pltpu.CompilerParams(
            collective_id=0, has_side_effects=True, vmem_limit_bytes=63 * 2**20
        ),
        cost_estimate=pl.CostEstimate(flops=10**10, bytes_accessed=40 * 2**20, transcendentals=0),
        name="forward",
    )(facts, tokens, cond_parts, table, ada_weight, qkv_weight, bins)


def bit_steps():
    win_bits = int(math.log2(lax.axis_size("win")))
    seq_bits = int(math.log2(lax.axis_size("seq")))
    return [("win", bit) for bit in range(win_bits)[::-1]] + [
        ("seq", bit) for bit in range(seq_bits)[::-1]
    ]


CORE = ("win", 0)


def my_bit(step):
    return lax.rem(lax.axis_index(step[0]) // (1 << step[1]), 2)


def partner(step):
    return {step[0]: lax.axis_index(step[0]) + (1 - 2 * my_bit(step)) * (1 << step[1])}


def greet():
    barrier = pltpu.get_barrier_semaphore()
    for step in bit_steps():
        pl.semaphore_signal(barrier, inc=1, device_id=partner(step), device_id_type=pl.DeviceIdType.MESH)
    pl.semaphore_wait(barrier, len(bit_steps()))


def remote(source, target, send_sem, recv_sem, step):
    return pltpu.make_async_remote_copy(
        src_ref=source,
        dst_ref=target,
        send_sem=send_sem,
        recv_sem=recv_sem,
        device_id=partner(step),
        device_id_type=pl.DeviceIdType.MESH,
    )


def each_block(shape, body):
    lead = shape[:-2]
    count = math.prod(lead)

    def one(flat, carry):
        index = []
        for size in lead[::-1]:
            index.append(lax.rem(flat, size))
            flat = flat // size
        body(tuple(index[::-1]))
        return carry

    if count == 1:
        body((0,) * len(lead))
    else:
        lax.fori_loop(0, count, one, 0)


class Flow:
    def __init__(self, rows, columns, chunks, flip, offset):
        steps = bit_steps()
        win_steps = [step for step in steps if step[0] == "win" and step != CORE]
        self.seq_steps = [step for step in steps if step[0] == "seq"]
        self.far = win_steps if flip else win_steps[::-1]
        self.names = win_steps
        self.near = self.seq_steps[::-1]
        self.chunks = chunks
        self.offset = offset
        self.width = columns // chunks
        self.share = rows // 2 ** len(steps)
        self.block = self.share * 2 ** len(self.seq_steps)
        self.columns = columns

    def view(self, grad):
        return grad.reshape((2,) * (len(self.far) + 1) + (self.block, self.columns))

    def scratch(self):
        chunks, width = (self.chunks, self.width)
        far, near = (len(self.far), len(self.near))
        shapes = [(2,) * far + (self.block, width)] * 2
        shapes += [(2,) * (far - 1 - i) + (self.block, width) for i in range(far)]
        shapes += [(2,) * near + (self.share, width)]
        shapes += [(2,) * (near - 1 - i) + (self.share, width) for i in range(near)]
        buffers = [pltpu.VMEM((chunks if at else 2,) + shape, bf16) for at, shape in enumerate(shapes)]
        count = 1 + far + near
        return buffers + [
            pltpu.SemaphoreType.DMA((chunks,)),
            pltpu.SemaphoreType.DMA((count, chunks)),
            pltpu.SemaphoreType.DMA((count, chunks)),
        ]

    def bind(self, grad, out, scratch):
        self.grad, self.out = grad, out
        far, near = (len(self.far), len(self.near))
        self.mine = scratch[0]
        self.first = scratch[1]
        self.far_bufs = list(scratch[2 : 2 + far])
        self.turn = scratch[2 + far]
        self.near_bufs = list(scratch[3 + far : 3 + far + near])
        self.local_sem, self.send_sem, self.recv_sem = scratch[3 + far + near :]

    def piece(self, bit, chunk):
        index = (slice(None),) * len(self.far) + (bit, slice(None))
        return self.grad.at[index + (pl.ds(pl.multiple_of(chunk * self.width, 128), self.width),)]

    def local_copy(self, chunk):
        return pltpu.make_async_copy(
            self.piece(my_bit(CORE), chunk), self.mine.at[lax.rem(chunk, 2)], self.local_sem.at[chunk]
        )

    def copy(self, stage, chunk):
        send, recv = (self.send_sem.at[stage, chunk], self.recv_sem.at[stage, chunk])
        far = len(self.far)
        if stage == 0:
            return remote(
                self.piece(1 - my_bit(CORE), chunk), self.first.at[chunk], send, recv, CORE
            )
        if stage <= far:
            step = self.far[stage - 1]
            source = ([self.first] + self.far_bufs)[stage - 1]
            target = self.far_bufs[stage - 1]
            axis = self.axis_of(step, self.far[: stage - 1], self.names)
        else:
            at = stage - 1 - far
            step = self.near[at]
            source = ([self.turn] + self.near_bufs)[at]
            target = self.near_bufs[at]
            axis = self.axis_of(step, self.near[:at], self.seq_steps)
        index = (chunk,) + (slice(None),) * axis + (1 - my_bit(step),)
        return remote(source.at[index], target.at[chunk], send, recv, step)

    def axis_of(self, step, gone, names):
        return [name for name in names if name not in gone].index(step)

    def stages(self):
        return 2 + len(self.far) + len(self.near)

    def run(self, stage, chunk):
        far, near = (len(self.far), len(self.near))
        if stage == 0:
            self.local_copy(chunk).start()
            self.copy(0, chunk).start()
            return
        self.copy(stage - 1, chunk).wait_recv()
        if stage == 1:
            self.local_copy(chunk).wait()
            shape = self.first.shape[1:]

            def add_first(index):
                at = (chunk,) + index
                kept = self.mine[(lax.rem(chunk, 2),) + index].astype(f32)
                self.first[at] = (self.first[at].astype(f32) + kept).astype(bf16)

            each_block(shape, add_first)
        elif stage < 1 + far:
            target = self.far_bufs[stage - 2]
            source = ([self.first] + self.far_bufs)[stage - 2]
            self.add_half(target, source, self.far, self.names, stage - 2, chunk)
        elif stage == 1 + far:
            step = self.far[-1]
            source = ([self.first] + self.far_bufs)[far - 1]
            target = self.far_bufs[far - 1]
            total = target[chunk].astype(f32) + source[chunk, my_bit(step)].astype(f32)
            total = total.astype(bf16)
            count = 2**near
            for owner in range(count):
                at, rest = ((), owner)
                for _ in range(near):
                    at = (rest % 2,) + at
                    rest = rest // 2
                self.turn[(chunk,) + at] = total[owner * self.share : (owner + 1) * self.share]
        elif stage < 1 + far + near:
            at = stage - 2 - far
            source = ([self.turn] + self.near_bufs)[at]
            self.add_half(self.near_bufs[at], source, self.near, self.seq_steps, at, chunk)
        else:
            source = ([self.turn] + self.near_bufs)[near - 1]
            kept = source[chunk, my_bit(self.near[-1])]
            total = self.near_bufs[near - 1][chunk].astype(f32) + kept.astype(f32)
            self.out[:, pl.ds(pl.multiple_of(chunk * self.width, 128), self.width)] = total
        if stage < 1 + far + near:
            self.copy(stage, chunk).start()

    def add_half(self, target, source, steps, names, at, chunk):
        step = steps[at]
        axis = self.axis_of(step, steps[:at], names)
        bit = my_bit(step)

        def add(index):
            from_at = (chunk,) + index[:axis] + (bit,) + index[axis:]
            to_at = (chunk,) + index
            target[to_at] = (target[to_at].astype(f32) + source[from_at].astype(f32)).astype(bf16)

        each_block(target.shape[1:], add)

    def drain(self, chunk):
        for stage in range(self.stages() - 1):
            self.copy(stage, chunk).wait_send()


class Load:
    def __init__(self, source, target, sem):
        self.target = target
        self.copy = pltpu.make_async_copy(source, target, sem)


class SmallGather:
    def __init__(self, mine, halves, gathered, send_sem, recv_sem):
        self.mine, self.halves, self.gathered = mine, halves, gathered
        self.send_sem, self.recv_sem = send_sem, recv_sem
        self.steps = bit_steps()[::-1]
        self.seq_count = len([step for step in self.steps if step[0] == "seq"])

    def copy(self, at):
        step = self.steps[at]
        if at < self.seq_count:
            source, target = self.mine.at[at], self.halves.at[at]
        else:
            size = 1 << step[1]
            here = lax.axis_index("win")
            block = pl.ds(here - lax.rem(here, size), size)
            source = target = self.gathered.at[block]
        return remote(source, target, self.send_sem.at[at], self.recv_sem.at[at], step)

    def run(self, at):
        if at > 0:
            self.copy(at - 1).wait_recv()
            if at <= self.seq_count:
                total = self.mine[at - 1] + self.halves[at - 1]
                if at < self.seq_count:
                    self.mine[at] = total
                else:
                    self.gathered[lax.axis_index("win")] = total
        if at < len(self.steps):
            self.copy(at).start()

    def drain(self):
        for at in range(len(self.steps)):
            self.copy(at).wait_send()


def norm_rows(values):
    centered = values - jnp.mean(values, axis=-1, keepdims=True)
    inv_std = lax.rsqrt(jnp.mean(centered * centered, axis=-1, keepdims=True) + norm_eps)
    return (centered * inv_std, inv_std)


def backward_kernel(flows, sizes, *refs):
    windows, rows, length, head_size = sizes
    refs = list(refs)

    def take(count):
        taken = refs[:count]
        del refs[:count]
        return taken

    grads = take(4)
    sources = take(9)
    (scale_ref,) = take(1)
    early_refs = take(3)
    shares = take(6)
    tokens_out, small_out = take(2)
    targets = take(9)
    (load_sem,) = take(1)
    grad_q, grad_kv, grad_scores, q_weight, kv_weight, own_in = take(6)
    far_in, far_half, far_own, far_send, far_recv = take(5)
    (table_sum,) = take(1)
    small = SmallGather(*take(5))
    (small_sem,) = take(1)
    for flow, grad, share in zip(flows, grads + [q_weight, kv_weight], shares):
        flow.bind(grad, share, take(len(flow.scratch())))
    loads = [Load(s, t, load_sem.at[at]) for at, (s, t) in enumerate(zip(sources, targets))]
    q_ref, kv_ref, probs_ref, grad_ref, in_ref, weight_ref, index_ref, tokens_ref, hidden_ref = targets
    width = q_ref.shape[1]
    head_scale = 1.0 / math.sqrt(head_size)
    heads = width // head_size
    seq_steps = bit_steps()[::-1][: small.seq_count]
    for load in loads:
        load.copy.start()
    greet()

    def attend_back(window):
        rows_at = pl.ds(pl.multiple_of(window * rows, rows), rows)
        keys_at = pl.ds(pl.multiple_of(window * length, length), length)

        def one_pair(pair, carry):
            start = pl.multiple_of(pair * 2 * head_size, 2 * head_size)
            cols = pl.ds(start, 2 * head_size)
            v_cols = pl.ds(width + start, 2 * head_size)
            q_pair = pair_halves(q_ref[rows_at, cols] * head_scale, head_size)
            g_pair = pair_halves(grad_ref[rows_at, cols], head_size)
            probs = probs_ref[window, pair]
            grad_kv[keys_at, v_cols] = dot(probs, g_pair).astype(bf16)
            grad_probs = dot_nt(kv_ref[keys_at, v_cols], g_pair)
            probs = probs.astype(f32)
            delta = jnp.sum(probs * grad_probs, axis=0, keepdims=True)
            scores = (probs * (grad_probs - delta)).astype(bf16)
            grad_kv[keys_at, cols] = dot(scores, q_pair).astype(bf16)
            back = dot(kv_ref[keys_at, cols].T, scores)
            grad_q[rows_at, cols] = (pair_diagonal(back, head_size, rows) * head_scale).astype(bf16)
            grad_scores[window, 2 * pair] = scores[:, :rows]
            grad_scores[window, 2 * pair + 1] = scores[:, rows:]
            return carry

        lax.fori_loop(0, heads // 2, one_pair, 0)

    def split_rows(target, values, cols):
        lead = target.shape[:-2]
        block = target.shape[-2]
        for at in range(math.prod(lead)):
            index, rest = ((), at)
            for size in lead[::-1]:
                index = (rest % size,) + index
                rest = rest // size
            target[index + (slice(None), cols)] = values[at * block : (at + 1) * block].astype(bf16)

    def project_back():
        def one_window(window, carry):
            keys_at = pl.ds(pl.multiple_of(window * length, length), length)
            far = dot_nt(grad_kv[keys_at, :], weight_ref[:, width:]).astype(bf16)
            split_owner(far, window)
            return carry

        def split_owner(far, window):
            rows_at = pl.ds(pl.multiple_of(window * rows, rows), rows)
            for owner in range(length // rows):
                index, rest = ((), owner)
                for _ in seq_steps:
                    index = (rest % 2,) + index
                    rest = rest // 2
                far_in[index + (rows_at,)] = far[owner * rows : (owner + 1) * rows]

        lax.fori_loop(0, windows, one_window, 0)
        far_copy(0).start()
        own_in[...] = dot_nt(grad_q[...], weight_ref[:, :width])

    def weight_grads():
        here = lax.axis_index("seq") * rows
        own = [in_ref[pl.ds(pl.multiple_of(w * length + here, rows), rows), :] for w in range(windows)]
        split_rows(q_weight, dot(jnp.concatenate(own, axis=0).T, grad_q[...]), slice(None))
        turned = in_ref[...].T
        step = 512
        for at in range(2 * width // step):
            cols = slice(at * step, (at + 1) * step)
            split_rows(kv_weight, dot(turned, grad_kv[:, cols]), cols)

    far_bufs = [far_in] + [far_half, far_own][-small.seq_count :]

    def far_copy(at):
        step = seq_steps[at]
        index = (slice(None),) * (small.seq_count - 1 - at) + (1 - my_bit(step),)
        return remote(
            far_bufs[at].at[index], far_bufs[at + 1], far_send.at[at], far_recv.at[at], step
        )

    def far_add(at):
        far_copy(at).wait_recv()
        step = seq_steps[at]
        bit = my_bit(step)
        target, source = far_bufs[at + 1], far_bufs[at]
        lead = target.shape[:-2]
        for flat in range(math.prod(lead)):
            for window in range(windows):
                index = ((flat,) if lead else ()) + (pl.ds(window * rows, rows),)
                kept = source[index[:-1] + (bit,) + index[-1:]].astype(f32)
                target[index] = (target[index].astype(f32) + kept).astype(bf16)
        if at + 1 < small.seq_count:
            far_copy(at + 1).start()

    def table_back(window):
        group = 16
        entries = table_sum.shape[1]

        def one_group(at, carry):
            keys = pl.ds(pl.multiple_of(at * group, group), group)
            scores = grad_scores[window, :, keys, :].astype(f32)
            scores = jnp.concatenate([scores, jnp.zeros((16 - heads, group, rows), f32)], axis=0)
            scores = jnp.swapaxes(scores, 0, 1).astype(bf16)
            index = index_ref[window, keys, :]
            spot = lax.broadcasted_iota(jnp.int32, (entries, rows), 0)
            total = jnp.zeros((16, entries), f32)
            for key in range(0, group, 2):
                terms, hots = [], []
                for which in (key, key + 1):
                    terms.append(scores[which])
                    hot = spot == jnp.broadcast_to(index[which : which + 1], (entries, rows))
                    hots.append(jnp.where(hot, 1.0, 0.0).astype(bf16))
                total = total + dot_nt(
                    jnp.concatenate(terms, axis=1), jnp.concatenate(hots, axis=1)
                )
            table_sum[...] += total
            return carry

        lax.fori_loop(0, length // group, one_group, 0)

    def finish_tokens():
        shift_rows, scale_rows = [], []
        for window in range(windows):
            rows_at = pl.ds(window * rows, rows)
            normed, inv_std = norm_rows(tokens_ref[rows_at, :].astype(f32))
            grad_in = own_in[rows_at, :] + far_own[rows_at, :].astype(f32)
            shift_rows.append(jnp.sum(grad_in, axis=0, keepdims=True))
            scale_rows.append(jnp.sum(grad_in * normed, axis=0, keepdims=True))
            dy = grad_in * scale_ref[pl.ds(window, 1), :]
            first = jnp.mean(dy, axis=-1, keepdims=True)
            second = jnp.mean(dy * normed, axis=-1, keepdims=True)
            back = (dy - first - normed * second) * inv_std
            tokens_out[rows_at, :] = (hidden_ref[rows_at, :] + back).astype(bf16)
        facts = jnp.concatenate(shift_rows + scale_rows + [early[...] for early in early_refs], axis=0)
        small.mine[0, :, :width] = facts
        small.mine[0, :, width:] = table_sum[...]

    steps = len(small.steps)
    jobs = {}
    for window in range(windows):
        jobs.setdefault(window, []).append(functools.partial(attend_back, window))
    jobs.setdefault(windows, []).extend([project_back, weight_grads])
    jobs.setdefault(windows + 1, []).append(functools.partial(table_back, 0))
    jobs.setdefault(windows + 2, []).append(functools.partial(far_add, 0))
    for window in range(1, windows):
        jobs.setdefault(windows + 2 + window, []).append(functools.partial(table_back, window))
    last = 2 * windows + 2
    for at in range(1, small.seq_count):
        jobs.setdefault(last + 2 * (at - 1), []).append(functools.partial(far_add, at))
    last = last + 2 * (small.seq_count - 2)
    jobs[last].append(finish_tokens)
    for at in range(steps + 1):
        jobs.setdefault(last + at, []).append(functools.partial(small.run, at))
    chunks = flows[0].chunks
    stages = flows[0].stages()
    order = [1, 0] + list(range(2, stages))
    total = max(max(flow.offset for flow in flows) + chunks + stages - 1, max(jobs) + 1)
    table_sum[...] = jnp.zeros_like(table_sum)

    def step(at, carry):
        for stage in order:
            for offset in sorted({flow.offset for flow in flows}):
                chunk = at - stage - offset

                @pl.when((chunk >= 0) & (chunk < chunks))
                def _(stage=stage, chunk=chunk, offset=offset):
                    for flow in flows:
                        if flow.offset == offset:
                            flow.run(stage, chunk)

            if stage == 0:

                @pl.when(at == 0)
                def _():
                    for load in loads:
                        load.copy.wait()

                for when, work in sorted(jobs.items()):

                    @pl.when(at == when)
                    def _(work=work):
                        for job in work:
                            job()

        return carry

    lax.fori_loop(0, total, step, 0)
    store_small = pltpu.make_async_copy(small.gathered, small_out, small_sem)
    store_small.start()

    def finish(chunk, carry):
        for flow in flows:
            flow.drain(chunk)
        return carry

    lax.fori_loop(0, chunks, finish, 0)
    for at in range(small.seq_count):
        far_copy(at).wait_send()
    small.drain()
    store_small.wait()


def backward(grads, loads, scales, early, sizes, chunks, flips):
    windows, rows, length, head_size = sizes
    width = loads[0].shape[1]
    shapes = [g.shape for g in grads] + [(width, width), (width, 2 * width)]
    offsets = [0] * len(grads) + [windows + 1] * 2
    flows = [Flow(s[0], s[1], chunks, flip, offset) for s, flip, offset in zip(shapes, flips, offsets)]
    win_bits = int(math.log2(lax.axis_size("win")))
    seq_bits = int(math.log2(lax.axis_size("seq")))
    total_rows = windows * rows
    small_shape = (16, width + 128)
    heads = width // head_size
    near = (2,) * seq_bits
    scratch = [pltpu.VMEM(load.shape, load.dtype) for load in loads]
    scratch += [
        pltpu.SemaphoreType.DMA((len(loads),)),
        pltpu.VMEM((total_rows, width), bf16),
        pltpu.VMEM((windows * length, 2 * width), bf16),
        pltpu.VMEM((windows, heads, length, rows), bf16),
        pltpu.VMEM((2,) * win_bits + (flows[-2].block, width), bf16),
        pltpu.VMEM((2,) * win_bits + (flows[-1].block, 2 * width), bf16),
        pltpu.VMEM((total_rows, width), f32),
        pltpu.VMEM(near + (total_rows, width), bf16),
        pltpu.VMEM(near[1:] + (total_rows, width), bf16),
        pltpu.VMEM((total_rows, width), bf16),
        pltpu.SemaphoreType.DMA((seq_bits,)),
        pltpu.SemaphoreType.DMA((seq_bits,)),
        pltpu.VMEM((16, 128), f32),
        pltpu.VMEM((seq_bits,) + small_shape, f32),
        pltpu.VMEM((seq_bits,) + small_shape, f32),
        pltpu.VMEM((2**win_bits,) + small_shape, f32),
        pltpu.SemaphoreType.DMA((win_bits + seq_bits,)),
        pltpu.SemaphoreType.DMA((win_bits + seq_bits,)),
        pltpu.SemaphoreType.DMA,
    ]
    for flow in flows:
        scratch += flow.scratch()
    vmem = pl.BlockSpec(memory_space=pltpu.VMEM)
    out_shape = [jax.ShapeDtypeStruct((flow.share, flow.columns), f32) for flow in flows]
    out_shape += [
        jax.ShapeDtypeStruct((total_rows, width), bf16),
        jax.ShapeDtypeStruct((2**win_bits,) + small_shape, f32),
    ]
    return pl.pallas_call(
        functools.partial(backward_kernel, flows, sizes),
        in_specs=[pl.BlockSpec(memory_space=pl.ANY)] * (len(grads) + len(loads)) + [vmem] * (1 + len(early)),
        out_specs=[vmem] * (len(out_shape) - 1) + [pl.BlockSpec(memory_space=pl.ANY)],
        out_shape=out_shape,
        scratch_shapes=scratch,
        compiler_params=pltpu.CompilerParams(
            collective_id=1, has_side_effects=True, vmem_limit_bytes=62 * 2**20
        ),
        cost_estimate=pl.CostEstimate(flops=10**10, bytes_accessed=200 * 2**20, transcendentals=0),
        name="backward",
    )(*[flow.view(grad) for flow, grad in zip(flows, grads)], *loads, scales, *early)


def tail_kernel(windows, *refs):
    gate, up, down, out, q, kv, tokens, small, ada_hbm, pair_table, pair_weight = refs[:11]
    to_gate, to_up, to_down, to_out, to_qkv, to_tokens, to_class, to_ada, to_table, to_weight = refs[11:21]
    by_row, cond_t, pre_t, onehot_t, table_flat, weight_rows, padded, ada_rows, cond_grad, ada_sem = refs[21:]
    width = tokens.shape[1]
    owner = lax.axis_index("win") * lax.axis_size("seq") + lax.axis_index("seq")
    share = to_class.shape[1]
    per_class = width // share
    column_at = lax.rem(owner, per_class) * share
    window_at = pl.multiple_of(jnp.minimum(column_at // 16 * 16, width - ada_rows.shape[0]), 16)
    load_ada = pltpu.make_async_copy(ada_hbm.at[pl.ds(window_at, ada_rows.shape[0]), :], ada_rows, ada_sem)
    load_ada.start()

    def flatten(target, values, columns, first):
        rows = values.shape[0]
        for at in range(values.shape[1] // 128):
            spot = pl.ds(first // 128 + at, rows, stride=columns // 128)
            target[spot, :] = values[:, at * 128 : (at + 1) * 128]

    for target, source in ((to_gate, gate), (to_up, up), (to_down, down), (to_out, out)):
        flatten(target, source, source.shape[1], 0)
    flatten(to_qkv, q, 3 * width, 0)
    flatten(to_qkv, kv, 3 * width, width)
    to_tokens[...] = tokens[...]

    groups = small.shape[0]

    def sort_rows(group, carry):
        for which in range(8):
            for window in range(windows):
                row = small[group, pl.ds(which * windows + window, 1), :width]
                by_row[pl.ds(window * groups + group, 1), which * width : (which + 1) * width] = row
        return carry

    lax.fori_loop(0, groups, sort_rows, 0)

    def rows_of(which):
        return by_row[:, which * width : (which + 1) * width]

    mods = [rows_of(part) for part in range(6)]
    pre = rows_of(6)
    cond_t[...] = (pre * jax.nn.sigmoid(pre)).T
    pre_t[...] = pre.T
    onehot_t[...] = rows_of(7).T
    ada_share = width // (lax.axis_size("win") * lax.axis_size("seq"))
    cond_rows = cond_t[pl.ds(owner * ada_share, ada_share), :]
    grad_cond = jnp.zeros((ada_rows.shape[0], pre.shape[0]), f32)
    load_ada.wait()
    for part, mod in enumerate(mods):
        product = jnp.dot(cond_rows, mod, precision=highest, preferred_element_type=f32)
        flatten(to_ada, product, 6 * width, part * width)
        grad_cond = grad_cond + lax.dot_general(
            ada_rows[:, part * width : (part + 1) * width].astype(f32),
            mod,
            (((1,), (1,)), ((), ())),
            precision=highest,
            preferred_element_type=f32,
        )
    cond_grad[...] = grad_cond
    grad_cond = cond_grad[pl.ds(column_at - window_at, share), :]
    pre_cols = pre_t[pl.ds(column_at, share), :]
    sig_cols = jax.nn.sigmoid(pre_cols)
    grad_pre = grad_cond * sig_cols * (1.0 + pre_cols * (1.0 - sig_cols))
    mine = jnp.broadcast_to(onehot_t[pl.ds(owner // per_class, 1), :], (8, pre.shape[0]))
    of_class = lax.dot_general(
        mine, grad_pre, (((1,), (1,)), ((), ())), precision=highest, preferred_element_type=f32
    )
    to_class[...] = of_class[:1]

    table = jnp.sum(small[:, :, width:], axis=0)
    heads = pair_weight.shape[1]
    padded[...] = jnp.zeros_like(padded)
    padded[:, :heads] = pair_weight[...].astype(f32)
    grad_table = lax.dot_general(
        table.T, padded[...], (((1,), (1,)), ((), ())), precision=highest, preferred_element_type=f32
    )
    flatten(table_flat, grad_table, grad_table.shape[1], 0)
    count = to_table.shape[0]
    to_table[...] = table_flat[pl.ds(owner * count, count), :]
    grad_weight = jnp.dot(
        table, pair_table[...].astype(f32), precision=highest, preferred_element_type=f32
    )
    weight_rows[...] = grad_weight.T
    count = to_weight.shape[1] // heads
    mine = weight_rows[pl.ds(owner * count, count), :]
    head = lax.broadcasted_iota(jnp.int32, (16, 128), 0)
    lane = lax.broadcasted_iota(jnp.int32, (16, 128), 1)
    spread = jnp.dot(
        mine,
        jnp.where(lax.rem(lane, heads) == head, 1.0, 0.0),
        precision=highest,
        preferred_element_type=f32,
    )
    row = lax.broadcasted_iota(jnp.int32, spread.shape, 0)
    lane = lax.broadcasted_iota(jnp.int32, spread.shape, 1)
    spread = jnp.sum(jnp.where(lane // heads == row, spread, 0.0), axis=0, keepdims=True)
    to_weight[...] = spread[:, : to_weight.shape[1]]


def tail(shares, tokens, small, ada_weight, pair_table, pair_weight, windows, class_share):
    width = tokens.shape[1]
    devices = lax.axis_size("win") * lax.axis_size("seq")
    features = pair_table.shape[1]
    span = class_share if class_share % 16 == 0 else -(-(class_share + 15) // 16) * 16
    sizes = [share.size for share in shares[:4]] + [shares[4].size + shares[5].size]
    table_size = pair_table.size // devices
    ada_size = ada_weight.size // devices
    every = windows * small.shape[0]
    vmem = pl.BlockSpec(memory_space=pltpu.VMEM)

    def flat(size):
        return jax.ShapeDtypeStruct((size // 128, 128), f32)

    return pl.pallas_call(
        functools.partial(tail_kernel, windows),
        in_specs=[vmem] * 8 + [pl.BlockSpec(memory_space=pl.ANY)] + [vmem] * 2,
        out_specs=[vmem] * 10,
        out_shape=[flat(size) for size in sizes]
        + [
            jax.ShapeDtypeStruct(tokens.shape, bf16),
            jax.ShapeDtypeStruct((1, class_share), f32),
            flat(ada_size),
            flat(table_size),
            jax.ShapeDtypeStruct((1, pair_weight.size // devices), f32),
        ],
        scratch_shapes=[pltpu.VMEM((every, 8 * width), f32)]
        + [pltpu.VMEM((width, every), f32)] * 3
        + [
            pltpu.VMEM((pair_table.size // 128, 128), f32),
            pltpu.VMEM((features, 16), f32),
            pltpu.VMEM((features, 16), f32),
            pltpu.VMEM((span, ada_weight.shape[1]), bf16),
            pltpu.VMEM((span, every), f32),
            pltpu.SemaphoreType.DMA,
        ],
        name="tail",
    )(*shares, tokens, small, ada_weight, pair_table, pair_weight)


def feed_forward_kernel(windows, *refs):
    mod, tokens, cotangent, mixed, out_weight, gate, up, down = refs[:8]
    layer_out, grad_hidden_out, grad_mixed, grad_out, sums, grad_gate, grad_up, grad_down = refs[8:16]
    attn_out, hidden_state, ffn_in, ffn_in_t, grad_ffn, ffn_out, grad_in = refs[16:]
    total_rows, width = tokens.shape
    rows = total_rows // windows

    def part(which):
        cols = slice(which * width, (which + 1) * width)
        return jnp.concatenate(
            [jnp.broadcast_to(mod[w : w + 1, cols], (rows, width)) for w in range(windows)], axis=0
        )

    @pl.when(pl.program_id(0) == 0)
    def _():
        projected = dot(mixed[...], out_weight[...])
        attn_out[...] = projected
        state = tokens[...].astype(f32) + jax.nn.sigmoid(part(2)) * projected
        hidden_state[...] = state
        normed, _ = norm_rows(state)
        block = (normed * (1.0 + part(4)) + part(3)).astype(bf16)
        ffn_in[...] = block
        ffn_in_t[...] = block.T
        grad_ffn[...] = (jax.nn.sigmoid(part(5)) * cotangent[...].astype(f32)).astype(bf16)
        ffn_out[...] = jnp.zeros_like(ffn_out)
        grad_in[...] = jnp.zeros_like(grad_in)

    gate_val = dot(ffn_in[...], gate[...])
    up_val = dot(ffn_in[...], up[...])
    gate_sig = jax.nn.sigmoid(gate_val)
    silu_gate = gate_val * gate_sig
    ffn_hidden = (silu_gate * up_val).astype(bf16)
    ffn_out[...] += dot(ffn_hidden, down[...])
    grad_down[...] = dot(ffn_hidden.T, grad_ffn[...]).astype(bf16)
    grad_hidden_ffn = dot_nt(grad_ffn[...], down[...])
    grad_up_val = (grad_hidden_ffn * silu_gate).astype(bf16)
    grad_gate_val = (
        grad_hidden_ffn * up_val * gate_sig * (1.0 + gate_val * (1.0 - gate_sig))
    ).astype(bf16)
    grad_gate[...] = dot(ffn_in_t[...], grad_gate_val).astype(bf16)
    grad_up[...] = dot(ffn_in_t[...], grad_up_val).astype(bf16)
    grad_in[...] += dot_nt(grad_gate_val, gate[...]) + dot_nt(grad_up_val, up[...])

    @pl.when(pl.program_id(0) == pl.num_programs(0) - 1)
    def _():
        def window_sums(at, values):
            for w in range(windows):
                total = jnp.sum(values[w * rows : (w + 1) * rows], axis=0, keepdims=True)
                sums[pl.ds(at * windows + w, 1), :] = total

        state = hidden_state[...]
        sig_f = jax.nn.sigmoid(part(5))
        grad_layer = cotangent[...].astype(f32)
        layer_out[...] = (state + sig_f * ffn_out[...]).astype(bf16)
        window_sums(3, grad_layer * ffn_out[...] * sig_f * (1.0 - sig_f))
        normed, inv_std = norm_rows(state)
        window_sums(1, grad_in[...])
        window_sums(2, grad_in[...] * normed)
        back = norm_back(grad_in[...] * (1.0 + part(4)), normed, inv_std)
        grad_hidden = grad_layer + back
        grad_hidden_out[...] = grad_hidden
        sig_a = jax.nn.sigmoid(part(2))
        window_sums(0, grad_hidden * attn_out[...] * sig_a * (1.0 - sig_a))
        grad_attn_out = (sig_a * grad_hidden).astype(bf16)
        grad_out[...] = dot(mixed[...].T, grad_attn_out).astype(bf16)
        grad_mixed[...] = dot_nt(grad_attn_out, out_weight[...]).astype(bf16)


def feed_forward(modulation, tokens, cotangent, mixed, out_weight, gate, up, down, windows):
    total_rows, width = tokens.shape
    hidden = gate.shape[1]
    blocks = 6
    size = hidden // blocks

    def whole(shape):
        return pl.BlockSpec(shape, lambda j: (0, 0))

    columns = pl.BlockSpec((width, size), lambda j: (0, j))
    lines = pl.BlockSpec((size, width), lambda j: (j, 0))
    row = (total_rows, width)
    return pl.pallas_call(
        functools.partial(feed_forward_kernel, windows),
        grid=(blocks,),
        in_specs=[whole(modulation.shape)]
        + [whole(row)] * 3
        + [whole(out_weight.shape), columns, columns, lines],
        out_specs=[whole(row)] * 3
        + [whole(out_weight.shape), whole((4 * windows, width)), columns, columns, lines],
        out_shape=[
            jax.ShapeDtypeStruct(row, bf16),
            jax.ShapeDtypeStruct(row, f32),
            jax.ShapeDtypeStruct(row, bf16),
            jax.ShapeDtypeStruct(out_weight.shape, bf16),
            jax.ShapeDtypeStruct((4 * windows, width), f32),
            jax.ShapeDtypeStruct(gate.shape, bf16),
            jax.ShapeDtypeStruct(up.shape, bf16),
            jax.ShapeDtypeStruct(down.shape, bf16),
        ],
        scratch_shapes=[
            pltpu.VMEM(row, f32),
            pltpu.VMEM(row, f32),
            pltpu.VMEM(row, bf16),
            pltpu.VMEM((width, total_rows), bf16),
            pltpu.VMEM(row, bf16),
            pltpu.VMEM(row, f32),
            pltpu.VMEM(row, f32),
        ],
        compiler_params=pltpu.CompilerParams(vmem_limit_bytes=63 * 2**20),
        cost_estimate=pl.CostEstimate(
            flops=18 * total_rows * width * hidden, bytes_accessed=40 * 2**20, transcendentals=0
        ),
        name="ffn",
    )(modulation, tokens, cotangent, mixed, out_weight, gate, up, down)


def three_parts(values):
    parts = []
    for _ in range(3):
        part = lax.reduce_precision(values, 8, 7)
        parts.append(part.astype(bf16))
        values = values - part
    return parts


def per_device(
    tokens,
    cotangent,
    noise_times,
    cath_ids,
    chain_start,
    distance_bins,
    class_table,
    ada_weight,
    qkv_weight,
    out_weight,
    pair_table,
    pair_weight,
    gate_weight,
    up_weight,
    down_weight,
):
    windows, row_count, width = tokens.shape
    length = distance_bins.shape[2]
    head_count = pair_weight.shape[1]
    head_size = width // head_count
    table_rows = pair_table.shape[0]
    bin_count = table_rows // 2
    classes = class_table.shape[0]
    total_rows = windows * row_count
    win_count = lax.axis_size("win")
    seq_count = lax.axis_size("seq")
    devices = win_count * seq_count
    class_onehot = (cath_ids[:, None] == jnp.arange(classes, dtype=jnp.int32)[None, :]).astype(f32)
    pre_cond = jnp.dot(
        class_onehot, class_table.astype(f32), precision=highest
    ) + time_embed(noise_times, width)
    cond_sig = jax.nn.sigmoid(pre_cond)
    condition = pre_cond * cond_sig
    cond_parts = jnp.concatenate(
        [jnp.pad(part, ((0, 8 - windows), (0, 0))) for part in three_parts(condition)], axis=0
    )
    table_bias = dot(pair_table, pair_weight).astype(bf16)
    modulation, queries, keys_values, attn_in_all, attn_mixed, probs, pair_index = forward(
        chain_start,
        tokens,
        cond_parts,
        table_bias.astype(f32).T,
        ada_weight,
        qkv_weight,
        distance_bins,
        head_size,
    )
    flat_tokens = tokens.reshape(total_rows, width)
    layer_out, grad_hidden, grad_mixed, grad_out, sums, grad_gate, grad_up, grad_down = feed_forward(
        modulation,
        flat_tokens,
        cotangent.reshape(total_rows, width),
        attn_mixed,
        out_weight,
        gate_weight,
        up_weight,
        down_weight,
        windows,
    )
    scale_attn = modulation[:windows, width : 2 * width]
    early = [
        sums,
        pre_cond / seq_count,
        jnp.pad(class_onehot, ((0, 0), (0, width - classes))) / seq_count,
    ]
    owned_gate, owned_up, owned_down, owned_out, owned_q, owned_kv, grad_tokens, small = backward(
        [grad_gate, grad_up, grad_down, grad_out],
        [
            queries,
            keys_values,
            probs,
            grad_mixed,
            attn_in_all,
            qkv_weight,
            pair_index,
            flat_tokens,
            grad_hidden,
        ],
        1.0 + scale_attn,
        early,
        (windows, row_count, length, head_size),
        6,
        [False, True, False, True, True, True],
    )
    class_share = classes * width // devices
    flat_gate, flat_up, flat_down, flat_out, flat_qkv, grad_tokens, of_class, flat_ada, of_table, of_weight = tail(
        [owned_gate, owned_up, owned_down, owned_out, owned_q, owned_kv],
        grad_tokens,
        small,
        ada_weight,
        pair_table,
        pair_weight,
        windows,
        class_share,
    )
    return (
        layer_out.reshape(windows, row_count, width),
        grad_tokens.reshape(windows, row_count, width),
        of_class.reshape(-1),
        flat_ada.reshape(-1),
        flat_qkv.reshape(-1),
        flat_out.reshape(-1),
        of_table.reshape(-1),
        of_weight.reshape(-1),
        flat_gate.reshape(-1),
        flat_up.reshape(-1),
        flat_down.reshape(-1),
    )


def solution(mesh):
    rows = P("win", "seq", None)
    flat = P(("win", "seq"))
    placed = (rows, rows, P("win"), P("win"), P("win"), rows) + (P(),) * 9
    return jax.shard_map(
        per_device, mesh=mesh, in_specs=placed, out_specs=(rows, rows) + (flat,) * 9, check_vma=False
    )
```

```python
import functools
import math

import jax
import jax.numpy as jnp
from jax import lax
from jax.experimental import pallas as pl
from jax.experimental.pallas import tpu as pltpu
from jax.sharding import PartitionSpec as P

highest = lax.Precision.HIGHEST
norm_eps = 1e-06
f32 = jnp.float32
bf16 = jnp.bfloat16


def norm_back(grad_normed, normed, inv_std):
    first_mean = jnp.mean(grad_normed, axis=-1, keepdims=True)
    second_mean = jnp.mean(grad_normed * normed, axis=-1, keepdims=True)
    return (grad_normed - first_mean - normed * second_mean) * inv_std


def time_embed(noise_times, model_width):
    half_width = model_width // 2
    frequency = jnp.exp(
        -math.log(10000.0) * jnp.arange(half_width).astype(f32) / half_width
    )
    angles = 1000.0 * noise_times[:, None] * frequency[None, :]
    return jnp.concatenate([jnp.sin(angles), jnp.cos(angles)], axis=-1)


def dot(a, b):
    return jnp.dot(a, b, preferred_element_type=f32)


def dot_nt(a, b):
    return lax.dot_general(a, b, (((1,), (1,)), ((), ())), preferred_element_type=f32)


def dot_tn(a, b):
    return lax.dot_general(a, b, (((0,), (0,)), ((), ())), preferred_element_type=f32)


def pair_halves(values, head_size):
    lane = lax.broadcasted_iota(jnp.int32, values.shape, 1)
    zero = jnp.zeros_like(values)
    return jnp.concatenate(
        [jnp.where(lane < head_size, values, zero), jnp.where(lane >= head_size, values, zero)], axis=0
    )


def pair_diagonal(values, head_size, rows):
    return jnp.concatenate([values[:head_size, :rows], values[head_size:, rows:]], axis=0).T


def forward_kernel(
    sizes,
    facts_ref,
    tokens_hbm,
    cond_ref,
    pair_table,
    pair_weight,
    ada_hbm,
    weight_hbm,
    bins_hbm,
    mod_ref,
    q_ref,
    kv_ref,
    in_ref,
    mixed_ref,
    probs_ref,
    index_ref,
    ada_ref,
    weight_ref,
    bins_ref,
    tokens_ref,
    table_ref,
    load_sem,
    gathered,
    send_sem,
    recv_sem,
):
    windows, rows, length, head_size = sizes
    width = q_ref.shape[1]
    count = gathered.shape[0]
    here = lax.axis_index("seq")
    head_scale = 1.0 / math.sqrt(head_size)
    loads = [
        Load(source, target, load_sem.at[at])
        for at, (source, target) in enumerate(
            [(ada_hbm, ada_ref), (weight_hbm, weight_ref), (bins_hbm, bins_ref), (tokens_hbm, tokens_ref)]
        )
    ]
    for load in loads:
        load.copy.start()
    barrier = pltpu.get_barrier_semaphore()
    for sign in (1, -1):

        @pl.when((here + sign >= 0) & (here + sign < count))
        def _(sign=sign):
            pl.semaphore_signal(
                barrier, inc=1, device_id={"seq": here + sign}, device_id_type=pl.DeviceIdType.MESH
            )

    pl.semaphore_wait(barrier, jnp.where((here == 0) | (here == count - 1), 1, 2))

    def copy(way, hop, window, shard, source=None):
        slot = gathered.at[shard, window]
        return pltpu.make_async_remote_copy(
            src_ref=slot if source is None else source,
            dst_ref=slot,
            send_sem=send_sem.at[way, hop, window],
            recv_sem=recv_sem.at[way, hop, window],
            device_id={"seq": here + 1 - 2 * way},
            device_id_type=pl.DeviceIdType.MESH,
        )

    def for_sends(body):
        for window in range(windows):
            for way in range(2):

                @pl.when((here + 1 - 2 * way >= 0) & (here + 1 - 2 * way < count))
                def _(way=way, window=window):
                    body(copy(way, 0, window, here, tokens_hbm.at[window]))

    for_sends(lambda each: each.start())
    table_ref[...] = dot_nt(pair_weight[...], pair_table[...]).astype(bf16).astype(f32)
    loads[0].copy.wait()
    for part in range(mod_ref.shape[1] // width):
        cols = slice(part * width, (part + 1) * width)
        mod = dot(cond_ref[...], ada_ref[:, cols])
        mod_ref[:, cols] = mod[:8] + mod[8:16] + mod[16:24]
    loads[1].copy.wait()
    loads[2].copy.wait()
    loads[3].copy.wait()

    def project(window, shard, values):
        normed, _ = norm_rows(values.astype(f32))
        scale = 1.0 + mod_ref[pl.ds(window, 1), width : 2 * width]
        block = (normed * scale + mod_ref[pl.ds(window, 1), :width]).astype(bf16)
        at = pl.ds(pl.multiple_of(window * length + shard * rows, rows), rows)
        in_ref[at, :] = block
        kv_ref[at, :] = dot(block, weight_ref[:, width:]).astype(bf16)
        return block

    def own(window, carry):
        block = project(window, here, tokens_ref[window])
        at = pl.ds(pl.multiple_of(window * rows, rows), rows)
        q_ref[at, :] = dot(block, weight_ref[:, :width]).astype(bf16)
        return carry

    lax.fori_loop(0, windows, own, 0)

    def arrive(way, hop, window):
        sign = 1 - 2 * way
        shard = here - sign * (hop + 1)

        @pl.when((shard >= 0) & (shard < count))
        def _():
            copy(way, hop, window, shard).wait_recv()

            @pl.when((here + sign >= 0) & (here + sign < count))
            def _():
                copy(way, hop + 1, window, shard).start()

            project(window, shard, gathered[shard, window])

    def relay(at, carry):
        arrive(lax.rem(at, 2), at // (2 * windows), lax.rem(at // 2, windows))
        return carry

    lax.fori_loop(0, (count - 2) * windows * 2, relay, 0)

    def finish(window, carry):
        def last(way, inner):
            arrive(way, count - 2, window)
            return inner

        lax.fori_loop(0, 2, last, 0)
        rows_at = pl.ds(pl.multiple_of(window * rows, rows), rows)
        keys_at = pl.ds(pl.multiple_of(window * length, length), length)
        start = facts_ref[window]
        bins = bins_ref[window].T
        key_first = lax.broadcasted_iota(jnp.int32, bins.shape, 0) < start
        row_first = lax.broadcasted_iota(jnp.int32, bins.shape, 1) + here * rows < start
        index_ref[window] = bins + jnp.where(key_first == row_first, table_ref.shape[1] // 2, 0)

        def one_pair(pair, inner):
            begin = pl.multiple_of(pair * 2 * head_size, 2 * head_size)
            cols = pl.ds(begin, 2 * head_size)
            v_cols = pl.ds(width + begin, 2 * head_size)
            index = index_ref[window]
            biases = []
            for head in range(2):
                entries = jnp.broadcast_to(table_ref[pl.ds(2 * pair + head, 1), :], index.shape)
                biases.append(jnp.take_along_axis(entries, index, axis=1, mode="promise_in_bounds"))
            q_pair = pair_halves(q_ref[rows_at, cols] * head_scale, head_size)
            scores = dot_nt(kv_ref[keys_at, cols], q_pair) + jnp.concatenate(biases, axis=1)
            top = jnp.max(scores, axis=0, keepdims=True)
            raised = jnp.exp(scores - top)
            total = jnp.sum(raised, axis=0, keepdims=True)
            probs = (raised * (1.0 / total)).astype(bf16)
            mixed = dot(kv_ref[keys_at, v_cols].T, probs)
            mixed_ref[rows_at, cols] = pair_diagonal(mixed, head_size, rows).astype(bf16)
            probs_ref[window, pair] = probs
            return inner

        lax.fori_loop(0, width // (2 * head_size), one_pair, 0)
        return carry

    lax.fori_loop(0, windows, finish, 0)
    for_sends(lambda each: each.wait_send())

    def sent(at, carry):
        way, hop, window = (lax.rem(at, 2), at // (2 * windows), lax.rem(at // 2, windows))
        sign = 1 - 2 * way
        shard = here - sign * (hop + 1)

        @pl.when((shard >= 0) & (shard < count) & (here + sign >= 0) & (here + sign < count))
        def _():
            copy(way, hop + 1, window, shard).wait_send()

        return carry

    lax.fori_loop(0, (count - 2) * windows * 2, sent, 0)


def forward(facts, tokens, cond_parts, pair_table, pair_weight, ada_weight, qkv_weight, bins, head_size):
    windows, rows, length = bins.shape
    width = tokens.shape[-1]
    pairs = width // (2 * head_size)
    count = lax.axis_size("seq")
    vmem = pl.BlockSpec(memory_space=pltpu.VMEM)
    hbm = pl.BlockSpec(memory_space=pltpu.HBM)
    return pl.pallas_call(
        functools.partial(forward_kernel, (windows, rows, length, head_size)),
        in_specs=[pl.BlockSpec(memory_space=pltpu.SMEM), hbm, vmem, vmem, vmem, hbm, hbm, hbm],
        out_specs=[vmem] * 7,
        out_shape=[
            jax.ShapeDtypeStruct((8, ada_weight.shape[1]), f32),
            jax.ShapeDtypeStruct((windows * rows, width), bf16),
            jax.ShapeDtypeStruct((windows * length, 2 * width), bf16),
            jax.ShapeDtypeStruct((windows * length, width), bf16),
            jax.ShapeDtypeStruct((windows * rows, width), bf16),
            jax.ShapeDtypeStruct((windows, pairs, length, 2 * rows), bf16),
            jax.ShapeDtypeStruct((windows, length, rows), jnp.int32),
        ],
        scratch_shapes=[
            pltpu.VMEM(ada_weight.shape, bf16),
            pltpu.VMEM(qkv_weight.shape, bf16),
            pltpu.VMEM(bins.shape, jnp.int32),
            pltpu.VMEM(tokens.shape, bf16),
            pltpu.VMEM((pair_weight.shape[0], pair_table.shape[0]), f32),
            pltpu.SemaphoreType.DMA((4,)),
            pltpu.VMEM((count, windows, rows, width), bf16),
            pltpu.SemaphoreType.DMA((2, count - 1, windows)),
            pltpu.SemaphoreType.DMA((2, count - 1, windows)),
        ],
        compiler_params=pltpu.CompilerParams(
            collective_id=0, has_side_effects=True, vmem_limit_bytes=63 * 2**20
        ),
        cost_estimate=pl.CostEstimate(flops=10**10, bytes_accessed=40 * 2**20, transcendentals=0),
        name="forward",
    )(facts, tokens, cond_parts, pair_table, pair_weight, ada_weight, qkv_weight, bins)


def bit_steps():
    win_bits = int(math.log2(lax.axis_size("win")))
    seq_bits = int(math.log2(lax.axis_size("seq")))
    return [("win", bit) for bit in range(win_bits)[::-1]] + [
        ("seq", bit) for bit in range(seq_bits)[::-1]
    ]


CORE = ("win", 0)


def my_bit(step):
    return lax.rem(lax.axis_index(step[0]) // (1 << step[1]), 2)


def partner(step):
    return {step[0]: lax.axis_index(step[0]) + (1 - 2 * my_bit(step)) * (1 << step[1])}


def greet():
    barrier = pltpu.get_barrier_semaphore()
    for step in bit_steps():
        pl.semaphore_signal(barrier, inc=1, device_id=partner(step), device_id_type=pl.DeviceIdType.MESH)
    pl.semaphore_wait(barrier, len(bit_steps()))


def remote(source, target, send_sem, recv_sem, step):
    return pltpu.make_async_remote_copy(
        src_ref=source,
        dst_ref=target,
        send_sem=send_sem,
        recv_sem=recv_sem,
        device_id=partner(step),
        device_id_type=pl.DeviceIdType.MESH,
    )


def each_block(shape, body):
    lead = shape[:-2]
    count = math.prod(lead)

    def one(flat, carry):
        index = []
        for size in lead[::-1]:
            index.append(lax.rem(flat, size))
            flat = flat // size
        body(tuple(index[::-1]))
        return carry

    if count == 1:
        body((0,) * len(lead))
    else:
        lax.fori_loop(0, count, one, 0)


class Flow:
    def __init__(self, rows, columns, chunks, flip, offset):
        steps = bit_steps()
        win_steps = [step for step in steps if step[0] == "win" and step != CORE]
        self.seq_steps = [step for step in steps if step[0] == "seq"]
        self.far = win_steps if flip else win_steps[::-1]
        self.names = win_steps
        self.near = self.seq_steps[::-1]
        self.chunks = chunks
        self.offset = offset
        self.width = columns // chunks
        self.share = rows // 2 ** len(steps)
        self.block = self.share * 2 ** len(self.seq_steps)
        self.columns = columns

    def view(self, grad):
        return grad.reshape((2,) * (len(self.far) + 1) + (self.block, self.columns))

    def scratch(self):
        chunks, width = (self.chunks, self.width)
        far, near = (len(self.far), len(self.near))
        shapes = [(2,) * far + (self.block, width)] * 2
        shapes += [(2,) * (far - 1 - i) + (self.block, width) for i in range(far)]
        shapes += [(2,) * near + (self.share, width)]
        shapes += [(2,) * (near - 1 - i) + (self.share, width) for i in range(near)]
        buffers = [pltpu.VMEM((chunks if at else 2,) + shape, bf16) for at, shape in enumerate(shapes)]
        count = 1 + far + near
        return buffers + [
            pltpu.SemaphoreType.DMA((chunks,)),
            pltpu.SemaphoreType.DMA((count, chunks)),
            pltpu.SemaphoreType.DMA((count, chunks)),
        ]

    def bind(self, grad, out, scratch):
        self.grad, self.out = grad, out
        far, near = (len(self.far), len(self.near))
        self.mine = scratch[0]
        self.first = scratch[1]
        self.far_bufs = list(scratch[2 : 2 + far])
        self.turn = scratch[2 + far]
        self.near_bufs = list(scratch[3 + far : 3 + far + near])
        self.local_sem, self.send_sem, self.recv_sem = scratch[3 + far + near :]

    def piece(self, bit, chunk):
        index = (slice(None),) * len(self.far) + (bit, slice(None))
        return self.grad.at[index + (pl.ds(pl.multiple_of(chunk * self.width, 128), self.width),)]

    def local_copy(self, chunk):
        return pltpu.make_async_copy(
            self.piece(my_bit(CORE), chunk), self.mine.at[lax.rem(chunk, 2)], self.local_sem.at[chunk]
        )

    def copy(self, stage, chunk):
        send, recv = (self.send_sem.at[stage, chunk], self.recv_sem.at[stage, chunk])
        far = len(self.far)
        if stage == 0:
            return remote(
                self.piece(1 - my_bit(CORE), chunk), self.first.at[chunk], send, recv, CORE
            )
        if stage <= far:
            step = self.far[stage - 1]
            source = ([self.first] + self.far_bufs)[stage - 1]
            target = self.far_bufs[stage - 1]
            axis = self.axis_of(step, self.far[: stage - 1], self.names)
        else:
            at = stage - 1 - far
            step = self.near[at]
            source = ([self.turn] + self.near_bufs)[at]
            target = self.near_bufs[at]
            axis = self.axis_of(step, self.near[:at], self.seq_steps)
        index = (chunk,) + (slice(None),) * axis + (1 - my_bit(step),)
        return remote(source.at[index], target.at[chunk], send, recv, step)

    def axis_of(self, step, gone, names):
        return [name for name in names if name not in gone].index(step)

    def stages(self):
        return 2 + len(self.far) + len(self.near)

    def run(self, stage, chunk):
        far, near = (len(self.far), len(self.near))
        if stage == 0:
            self.local_copy(chunk).start()
            self.copy(0, chunk).start()
            return
        self.copy(stage - 1, chunk).wait_recv()
        if stage == 1:
            self.local_copy(chunk).wait()
            shape = self.first.shape[1:]

            def add_first(index):
                at = (chunk,) + index
                kept = self.mine[(lax.rem(chunk, 2),) + index].astype(f32)
                self.first[at] = (self.first[at].astype(f32) + kept).astype(bf16)

            each_block(shape, add_first)
        elif stage < 1 + far:
            target = self.far_bufs[stage - 2]
            source = ([self.first] + self.far_bufs)[stage - 2]
            self.add_half(target, source, self.far, self.names, stage - 2, chunk)
        elif stage == 1 + far:
            step = self.far[-1]
            source = ([self.first] + self.far_bufs)[far - 1]
            target = self.far_bufs[far - 1]
            total = target[chunk].astype(f32) + source[chunk, my_bit(step)].astype(f32)
            total = total.astype(bf16)
            count = 2**near
            for owner in range(count):
                at, rest = ((), owner)
                for _ in range(near):
                    at = (rest % 2,) + at
                    rest = rest // 2
                self.turn[(chunk,) + at] = total[owner * self.share : (owner + 1) * self.share]
        elif stage < 1 + far + near:
            at = stage - 2 - far
            source = ([self.turn] + self.near_bufs)[at]
            self.add_half(self.near_bufs[at], source, self.near, self.seq_steps, at, chunk)
        else:
            source = ([self.turn] + self.near_bufs)[near - 1]
            kept = source[chunk, my_bit(self.near[-1])]
            total = self.near_bufs[near - 1][chunk].astype(f32) + kept.astype(f32)
            self.out[:, pl.ds(pl.multiple_of(chunk * self.width, 128), self.width)] = total
        if stage < 1 + far + near:
            self.copy(stage, chunk).start()

    def add_half(self, target, source, steps, names, at, chunk):
        step = steps[at]
        axis = self.axis_of(step, steps[:at], names)
        bit = my_bit(step)

        def add(index):
            from_at = (chunk,) + index[:axis] + (bit,) + index[axis:]
            to_at = (chunk,) + index
            target[to_at] = (target[to_at].astype(f32) + source[from_at].astype(f32)).astype(bf16)

        each_block(target.shape[1:], add)

    def drain(self, chunk):
        for stage in range(self.stages() - 1):
            self.copy(stage, chunk).wait_send()


class Load:
    def __init__(self, source, target, sem):
        self.target = target
        self.copy = pltpu.make_async_copy(source, target, sem)


class SmallGather:
    def __init__(self, mine, halves, gathered, send_sem, recv_sem):
        self.mine, self.halves, self.gathered = mine, halves, gathered
        self.send_sem, self.recv_sem = send_sem, recv_sem
        self.steps = bit_steps()[::-1]
        self.seq_count = len([step for step in self.steps if step[0] == "seq"])

    def copy(self, at):
        step = self.steps[at]
        if at < self.seq_count:
            source, target = self.mine.at[at], self.halves.at[at]
        else:
            size = 1 << step[1]
            here = lax.axis_index("win")
            block = pl.ds(here - lax.rem(here, size), size)
            source = target = self.gathered.at[block]
        return remote(source, target, self.send_sem.at[at], self.recv_sem.at[at], step)

    def run(self, at):
        if at > 0:
            self.copy(at - 1).wait_recv()
            if at <= self.seq_count:
                total = self.mine[at - 1] + self.halves[at - 1]
                if at < self.seq_count:
                    self.mine[at] = total
                else:
                    self.gathered[lax.axis_index("win")] = total
        if at < len(self.steps):
            self.copy(at).start()

    def drain(self):
        for at in range(len(self.steps)):
            self.copy(at).wait_send()


def norm_rows(values):
    centered = values - jnp.mean(values, axis=-1, keepdims=True)
    inv_std = lax.rsqrt(jnp.mean(centered * centered, axis=-1, keepdims=True) + norm_eps)
    return (centered * inv_std, inv_std)


def backward_kernel(flows, sizes, *refs):
    windows, rows, length, head_size = sizes
    refs = list(refs)

    def take(count):
        taken = refs[:count]
        del refs[:count]
        return taken

    grads = take(4)
    sources = take(9)
    (scale_ref,) = take(1)
    early_refs = take(3)
    shares = take(6)
    tokens_out, small_out = take(2)
    targets = take(9)
    (load_sem,) = take(1)
    grad_q, grad_kv, grad_scores, q_weight, kv_weight, own_in = take(6)
    far_in, far_half, far_own, far_send, far_recv = take(5)
    (table_sum,) = take(1)
    small = SmallGather(*take(5))
    (small_sem,) = take(1)
    for flow, grad, share in zip(flows, grads + [q_weight, kv_weight], shares):
        flow.bind(grad, share, take(len(flow.scratch())))
    loads = [Load(s, t, load_sem.at[at]) for at, (s, t) in enumerate(zip(sources, targets))]
    q_ref, kv_ref, probs_ref, grad_ref, in_ref, weight_ref, index_ref, tokens_ref, hidden_ref = targets
    width = q_ref.shape[1]
    head_scale = 1.0 / math.sqrt(head_size)
    heads = width // head_size
    seq_steps = bit_steps()[::-1][: small.seq_count]
    for load in loads:
        load.copy.start()
    greet()

    def attend_back(window):
        rows_at = pl.ds(pl.multiple_of(window * rows, rows), rows)
        keys_at = pl.ds(pl.multiple_of(window * length, length), length)

        def one_pair(pair, carry):
            start = pl.multiple_of(pair * 2 * head_size, 2 * head_size)
            cols = pl.ds(start, 2 * head_size)
            v_cols = pl.ds(width + start, 2 * head_size)
            q_pair = pair_halves(q_ref[rows_at, cols] * head_scale, head_size)
            g_pair = pair_halves(grad_ref[rows_at, cols], head_size)
            probs = probs_ref[window, pair]
            grad_kv[keys_at, v_cols] = dot(probs, g_pair).astype(bf16)
            grad_probs = dot_nt(kv_ref[keys_at, v_cols], g_pair)
            probs = probs.astype(f32)
            delta = jnp.sum(probs * grad_probs, axis=0, keepdims=True)
            scores = (probs * (grad_probs - delta)).astype(bf16)
            grad_kv[keys_at, cols] = dot(scores, q_pair).astype(bf16)
            back = dot(kv_ref[keys_at, cols].T, scores)
            grad_q[rows_at, cols] = (pair_diagonal(back, head_size, rows) * head_scale).astype(bf16)
            grad_scores[window, 2 * pair] = scores[:, :rows]
            grad_scores[window, 2 * pair + 1] = scores[:, rows:]
            return carry

        lax.fori_loop(0, heads // 2, one_pair, 0)

    def split_rows(target, values, cols):
        lead = target.shape[:-2]
        block = target.shape[-2]
        for at in range(math.prod(lead)):
            index, rest = ((), at)
            for size in lead[::-1]:
                index = (rest % size,) + index
                rest = rest // size
            target[index + (slice(None), cols)] = values[at * block : (at + 1) * block].astype(bf16)

    def project_back():
        def one_window(window, carry):
            keys_at = pl.ds(pl.multiple_of(window * length, length), length)
            far = dot_nt(grad_kv[keys_at, :], weight_ref[:, width:]).astype(bf16)
            split_owner(far, window)
            return carry

        def split_owner(far, window):
            rows_at = pl.ds(pl.multiple_of(window * rows, rows), rows)
            for owner in range(length // rows):
                index, rest = ((), owner)
                for _ in seq_steps:
                    index = (rest % 2,) + index
                    rest = rest // 2
                far_in[index + (rows_at,)] = far[owner * rows : (owner + 1) * rows]

        lax.fori_loop(0, windows, one_window, 0)
        far_copy(0).start()
        own_in[...] = dot_nt(grad_q[...], weight_ref[:, :width])

    def weight_grads():
        here = lax.axis_index("seq") * rows
        own = [in_ref[pl.ds(pl.multiple_of(w * length + here, rows), rows), :] for w in range(windows)]
        split_rows(q_weight, dot(jnp.concatenate(own, axis=0).T, grad_q[...]), slice(None))
        turned = in_ref[...].T
        step = 512
        for at in range(2 * width // step):
            cols = slice(at * step, (at + 1) * step)
            split_rows(kv_weight, dot(turned, grad_kv[:, cols]), cols)

    far_bufs = [far_in] + [far_half, far_own][-small.seq_count :]

    def far_copy(at):
        step = seq_steps[at]
        index = (slice(None),) * (small.seq_count - 1 - at) + (1 - my_bit(step),)
        return remote(
            far_bufs[at].at[index], far_bufs[at + 1], far_send.at[at], far_recv.at[at], step
        )

    def far_add(at):
        far_copy(at).wait_recv()
        step = seq_steps[at]
        bit = my_bit(step)
        target, source = far_bufs[at + 1], far_bufs[at]
        lead = target.shape[:-2]
        for flat in range(math.prod(lead)):
            for window in range(windows):
                index = ((flat,) if lead else ()) + (pl.ds(window * rows, rows),)
                kept = source[index[:-1] + (bit,) + index[-1:]].astype(f32)
                target[index] = (target[index].astype(f32) + kept).astype(bf16)
        if at + 1 < small.seq_count:
            far_copy(at + 1).start()

    def table_back(window):
        group = 16
        entries = table_sum.shape[1]

        def one_group(at, carry):
            keys = pl.ds(pl.multiple_of(at * group, group), group)
            scores = grad_scores[window, :, keys, :].astype(f32)
            scores = jnp.concatenate([scores, jnp.zeros((16 - heads, group, rows), f32)], axis=0)
            scores = jnp.swapaxes(scores, 0, 1).astype(bf16)
            index = index_ref[window, keys, :]
            spot = lax.broadcasted_iota(jnp.int32, (entries, rows), 0)
            total = jnp.zeros((16, entries), f32)
            for key in range(0, group, 2):
                terms, hots = [], []
                for which in (key, key + 1):
                    terms.append(scores[which])
                    hot = spot == jnp.broadcast_to(index[which : which + 1], (entries, rows))
                    hots.append(jnp.where(hot, 1.0, 0.0).astype(bf16))
                total = total + dot_nt(
                    jnp.concatenate(terms, axis=1), jnp.concatenate(hots, axis=1)
                )
            table_sum[...] += total
            return carry

        lax.fori_loop(0, length // group, one_group, 0)

    def finish_tokens():
        shift_rows, scale_rows = [], []
        for window in range(windows):
            rows_at = pl.ds(window * rows, rows)
            normed, inv_std = norm_rows(tokens_ref[rows_at, :].astype(f32))
            grad_in = own_in[rows_at, :] + far_own[rows_at, :].astype(f32)
            shift_rows.append(jnp.sum(grad_in, axis=0, keepdims=True))
            scale_rows.append(jnp.sum(grad_in * normed, axis=0, keepdims=True))
            dy = grad_in * scale_ref[pl.ds(window, 1), :]
            first = jnp.mean(dy, axis=-1, keepdims=True)
            second = jnp.mean(dy * normed, axis=-1, keepdims=True)
            back = (dy - first - normed * second) * inv_std
            tokens_out[rows_at, :] = (hidden_ref[rows_at, :] + back).astype(bf16)
        facts = jnp.concatenate(shift_rows + scale_rows + [early[...] for early in early_refs], axis=0)
        small.mine[0, :, :width] = facts
        small.mine[0, :, width:] = table_sum[...]

    steps = len(small.steps)
    jobs = {}
    for window in range(windows):
        jobs.setdefault(window, []).append(functools.partial(attend_back, window))
    jobs.setdefault(windows, []).extend([project_back, weight_grads])
    jobs.setdefault(windows + 1, []).append(functools.partial(table_back, 0))
    jobs.setdefault(windows + 2, []).append(functools.partial(far_add, 0))
    for window in range(1, windows):
        jobs.setdefault(windows + 2 + window, []).append(functools.partial(table_back, window))
    last = 2 * windows + 2
    for at in range(1, small.seq_count):
        jobs.setdefault(last + 2 * (at - 1), []).append(functools.partial(far_add, at))
    last = last + 2 * (small.seq_count - 2)
    jobs[last].append(finish_tokens)
    for at in range(steps + 1):
        jobs.setdefault(last + at, []).append(functools.partial(small.run, at))
    chunks = flows[0].chunks
    stages = flows[0].stages()
    order = [1, 0] + list(range(2, stages))
    total = max(max(flow.offset for flow in flows) + chunks + stages - 1, max(jobs) + 1)
    table_sum[...] = jnp.zeros_like(table_sum)

    def step(at, carry):
        for stage in order:
            for offset in sorted({flow.offset for flow in flows}):
                chunk = at - stage - offset

                @pl.when((chunk >= 0) & (chunk < chunks))
                def _(stage=stage, chunk=chunk, offset=offset):
                    for flow in flows:
                        if flow.offset == offset:
                            flow.run(stage, chunk)

            if stage == 0:

                @pl.when(at == 0)
                def _():
                    for load in loads:
                        load.copy.wait()

                for when, work in sorted(jobs.items()):

                    @pl.when(at == when)
                    def _(work=work):
                        for job in work:
                            job()

        return carry

    lax.fori_loop(0, total, step, 0)
    store_small = pltpu.make_async_copy(small.gathered, small_out, small_sem)
    store_small.start()

    def finish(chunk, carry):
        for flow in flows:
            flow.drain(chunk)
        return carry

    lax.fori_loop(0, chunks, finish, 0)
    for at in range(small.seq_count):
        far_copy(at).wait_send()
    small.drain()
    store_small.wait()


def backward(grads, loads, scales, early, sizes, chunks, flips):
    windows, rows, length, head_size = sizes
    width = loads[0].shape[1]
    shapes = [g.shape for g in grads] + [(width, width), (width, 2 * width)]
    offsets = [0] * len(grads) + [windows + 1] * 2
    flows = [Flow(s[0], s[1], chunks, flip, offset) for s, flip, offset in zip(shapes, flips, offsets)]
    win_bits = int(math.log2(lax.axis_size("win")))
    seq_bits = int(math.log2(lax.axis_size("seq")))
    total_rows = windows * rows
    small_shape = (16, width + 128)
    heads = width // head_size
    near = (2,) * seq_bits
    scratch = [pltpu.VMEM(load.shape, load.dtype) for load in loads]
    scratch += [
        pltpu.SemaphoreType.DMA((len(loads),)),
        pltpu.VMEM((total_rows, width), bf16),
        pltpu.VMEM((windows * length, 2 * width), bf16),
        pltpu.VMEM((windows, heads, length, rows), bf16),
        pltpu.VMEM((2,) * win_bits + (flows[-2].block, width), bf16),
        pltpu.VMEM((2,) * win_bits + (flows[-1].block, 2 * width), bf16),
        pltpu.VMEM((total_rows, width), f32),
        pltpu.VMEM(near + (total_rows, width), bf16),
        pltpu.VMEM(near[1:] + (total_rows, width), bf16),
        pltpu.VMEM((total_rows, width), bf16),
        pltpu.SemaphoreType.DMA((seq_bits,)),
        pltpu.SemaphoreType.DMA((seq_bits,)),
        pltpu.VMEM((16, 128), f32),
        pltpu.VMEM((seq_bits,) + small_shape, f32),
        pltpu.VMEM((seq_bits,) + small_shape, f32),
        pltpu.VMEM((2**win_bits,) + small_shape, f32),
        pltpu.SemaphoreType.DMA((win_bits + seq_bits,)),
        pltpu.SemaphoreType.DMA((win_bits + seq_bits,)),
        pltpu.SemaphoreType.DMA,
    ]
    for flow in flows:
        scratch += flow.scratch()
    vmem = pl.BlockSpec(memory_space=pltpu.VMEM)
    out_shape = [jax.ShapeDtypeStruct((flow.share, flow.columns), f32) for flow in flows]
    out_shape += [
        jax.ShapeDtypeStruct((total_rows, width), bf16),
        jax.ShapeDtypeStruct((2**win_bits,) + small_shape, f32),
    ]
    return pl.pallas_call(
        functools.partial(backward_kernel, flows, sizes),
        in_specs=[pl.BlockSpec(memory_space=pl.ANY)] * (len(grads) + len(loads)) + [vmem] * (1 + len(early)),
        out_specs=[vmem] * (len(out_shape) - 1) + [pl.BlockSpec(memory_space=pl.ANY)],
        out_shape=out_shape,
        scratch_shapes=scratch,
        compiler_params=pltpu.CompilerParams(
            collective_id=1, has_side_effects=True, vmem_limit_bytes=62 * 2**20
        ),
        cost_estimate=pl.CostEstimate(flops=10**10, bytes_accessed=200 * 2**20, transcendentals=0),
        name="backward",
    )(*[flow.view(grad) for flow, grad in zip(flows, grads)], *loads, scales, *early)


def tail_kernel(windows, *refs):
    gate, up, down, out, q, kv, tokens, small, ada_hbm, pair_table, pair_weight = refs[:11]
    to_gate, to_up, to_down, to_out, to_qkv, to_tokens, to_class, to_ada, to_table, to_weight = refs[11:21]
    by_row, cond_t, pre_t, onehot_t, table_flat, weight_rows, padded, ada_rows, cond_grad, ada_sem = refs[21:]
    width = tokens.shape[1]
    owner = lax.axis_index("win") * lax.axis_size("seq") + lax.axis_index("seq")
    share = to_class.shape[1]
    per_class = width // share
    column_at = lax.rem(owner, per_class) * share
    window_at = pl.multiple_of(jnp.minimum(column_at // 16 * 16, width - ada_rows.shape[0]), 16)
    load_ada = pltpu.make_async_copy(ada_hbm.at[pl.ds(window_at, ada_rows.shape[0]), :], ada_rows, ada_sem)
    load_ada.start()

    def flatten(target, values, columns, first):
        rows = values.shape[0]
        for at in range(values.shape[1] // 128):
            spot = pl.ds(first // 128 + at, rows, stride=columns // 128)
            target[spot, :] = values[:, at * 128 : (at + 1) * 128]

    for target, source in ((to_gate, gate), (to_up, up), (to_down, down), (to_out, out)):
        flatten(target, source, source.shape[1], 0)
    flatten(to_qkv, q, 3 * width, 0)
    flatten(to_qkv, kv, 3 * width, width)
    to_tokens[...] = tokens[...]

    groups = small.shape[0]

    def sort_rows(group, carry):
        for which in range(8):
            for window in range(windows):
                row = small[group, pl.ds(which * windows + window, 1), :width]
                by_row[pl.ds(window * groups + group, 1), which * width : (which + 1) * width] = row
        return carry

    lax.fori_loop(0, groups, sort_rows, 0)

    def rows_of(which):
        return by_row[:, which * width : (which + 1) * width]

    mods = [rows_of(part) for part in range(6)]
    pre = rows_of(6)
    cond_t[...] = (pre * jax.nn.sigmoid(pre)).T
    pre_t[...] = pre.T
    onehot_t[...] = rows_of(7).T
    ada_share = width // (lax.axis_size("win") * lax.axis_size("seq"))
    cond_rows = cond_t[pl.ds(owner * ada_share, ada_share), :]
    grad_cond = jnp.zeros((ada_rows.shape[0], pre.shape[0]), f32)
    load_ada.wait()
    for part, mod in enumerate(mods):
        product = jnp.dot(cond_rows, mod, precision=highest, preferred_element_type=f32)
        flatten(to_ada, product, 6 * width, part * width)
        grad_cond = grad_cond + lax.dot_general(
            ada_rows[:, part * width : (part + 1) * width].astype(f32),
            mod,
            (((1,), (1,)), ((), ())),
            precision=highest,
            preferred_element_type=f32,
        )
    cond_grad[...] = grad_cond
    grad_cond = cond_grad[pl.ds(column_at - window_at, share), :]
    pre_cols = pre_t[pl.ds(column_at, share), :]
    sig_cols = jax.nn.sigmoid(pre_cols)
    grad_pre = grad_cond * sig_cols * (1.0 + pre_cols * (1.0 - sig_cols))
    mine = jnp.broadcast_to(onehot_t[pl.ds(owner // per_class, 1), :], (8, pre.shape[0]))
    of_class = lax.dot_general(
        mine, grad_pre, (((1,), (1,)), ((), ())), precision=highest, preferred_element_type=f32
    )
    to_class[...] = of_class[:1]

    table = jnp.sum(small[:, :, width:], axis=0)
    heads = pair_weight.shape[0]
    padded[...] = jnp.zeros_like(padded)
    padded[:heads, :] = pair_weight[...].astype(f32)
    grad_table = jnp.dot(table.T, padded[...], precision=highest, preferred_element_type=f32)
    flatten(table_flat, grad_table, grad_table.shape[1], 0)
    count = to_table.shape[0]
    to_table[...] = table_flat[pl.ds(owner * count, count), :]
    grad_weight = jnp.dot(
        table, pair_table[...].astype(f32), precision=highest, preferred_element_type=f32
    )
    weight_rows[...] = grad_weight.T
    count = to_weight.shape[1] // heads
    mine = weight_rows[pl.ds(owner * count, count), :]
    head = lax.broadcasted_iota(jnp.int32, (16, 128), 0)
    lane = lax.broadcasted_iota(jnp.int32, (16, 128), 1)
    spread = jnp.dot(
        mine,
        jnp.where(lax.rem(lane, heads) == head, 1.0, 0.0),
        precision=highest,
        preferred_element_type=f32,
    )
    row = lax.broadcasted_iota(jnp.int32, spread.shape, 0)
    lane = lax.broadcasted_iota(jnp.int32, spread.shape, 1)
    spread = jnp.sum(jnp.where(lane // heads == row, spread, 0.0), axis=0, keepdims=True)
    to_weight[...] = spread[:, : to_weight.shape[1]]


def tail(shares, tokens, small, ada_weight, pair_table, pair_weight, windows, class_share):
    width = tokens.shape[1]
    devices = lax.axis_size("win") * lax.axis_size("seq")
    features = pair_table.shape[1]
    span = class_share if class_share % 16 == 0 else -(-(class_share + 15) // 16) * 16
    sizes = [share.size for share in shares[:4]] + [shares[4].size + shares[5].size]
    table_size = pair_table.size // devices
    ada_size = ada_weight.size // devices
    every = windows * small.shape[0]
    vmem = pl.BlockSpec(memory_space=pltpu.VMEM)

    def flat(size):
        return jax.ShapeDtypeStruct((size // 128, 128), f32)

    return pl.pallas_call(
        functools.partial(tail_kernel, windows),
        in_specs=[vmem] * 8 + [pl.BlockSpec(memory_space=pl.ANY)] + [vmem] * 2,
        out_specs=[vmem] * 10,
        out_shape=[flat(size) for size in sizes]
        + [
            jax.ShapeDtypeStruct(tokens.shape, bf16),
            jax.ShapeDtypeStruct((1, class_share), f32),
            flat(ada_size),
            flat(table_size),
            jax.ShapeDtypeStruct((1, pair_weight.size // devices), f32),
        ],
        scratch_shapes=[pltpu.VMEM((every, 8 * width), f32)]
        + [pltpu.VMEM((width, every), f32)] * 3
        + [
            pltpu.VMEM((pair_table.size // 128, 128), f32),
            pltpu.VMEM((features, 16), f32),
            pltpu.VMEM((16, features), f32),
            pltpu.VMEM((span, ada_weight.shape[1]), bf16),
            pltpu.VMEM((span, every), f32),
            pltpu.SemaphoreType.DMA,
        ],
        name="tail",
    )(*shares, tokens, small, ada_weight, pair_table, pair_weight)


def feed_forward_kernel(windows, *refs):
    mod, tokens, cotangent, mixed, out_weight, gate, up, down = refs[:8]
    layer_out, grad_hidden_out, grad_mixed, grad_out, sums, grad_gate, grad_up, grad_down = refs[8:16]
    attn_out, hidden_state, ffn_in, ffn_in_t, grad_ffn, ffn_out, grad_in = refs[16:]
    total_rows, width = tokens.shape
    rows = total_rows // windows

    def part(which):
        cols = slice(which * width, (which + 1) * width)
        return jnp.concatenate(
            [jnp.broadcast_to(mod[w : w + 1, cols], (rows, width)) for w in range(windows)], axis=0
        )

    @pl.when(pl.program_id(0) == 0)
    def _():
        projected = dot(mixed[...], out_weight[...])
        attn_out[...] = projected
        state = tokens[...].astype(f32) + jax.nn.sigmoid(part(2)) * projected
        hidden_state[...] = state
        normed, _ = norm_rows(state)
        block = (normed * (1.0 + part(4)) + part(3)).astype(bf16)
        ffn_in[...] = block
        ffn_in_t[...] = block.T
        grad_ffn[...] = (jax.nn.sigmoid(part(5)) * cotangent[...].astype(f32)).astype(bf16)
        ffn_out[...] = jnp.zeros_like(ffn_out)
        grad_in[...] = jnp.zeros_like(grad_in)

    gate_val = dot(ffn_in[...], gate[...])
    up_val = dot(ffn_in[...], up[...])
    gate_sig = jax.nn.sigmoid(gate_val)
    silu_gate = gate_val * gate_sig
    ffn_hidden = (silu_gate * up_val).astype(bf16)
    ffn_out[...] += dot(ffn_hidden, down[...])
    grad_down[...] = dot(ffn_hidden.T, grad_ffn[...]).astype(bf16)
    grad_hidden_ffn = dot_nt(grad_ffn[...], down[...])
    grad_up_val = (grad_hidden_ffn * silu_gate).astype(bf16)
    grad_gate_val = (
        grad_hidden_ffn * up_val * gate_sig * (1.0 + gate_val * (1.0 - gate_sig))
    ).astype(bf16)
    grad_gate[...] = dot(ffn_in_t[...], grad_gate_val).astype(bf16)
    grad_up[...] = dot(ffn_in_t[...], grad_up_val).astype(bf16)
    grad_in[...] += dot_nt(grad_gate_val, gate[...]) + dot_nt(grad_up_val, up[...])

    @pl.when(pl.program_id(0) == pl.num_programs(0) - 1)
    def _():
        def window_sums(at, values):
            for w in range(windows):
                total = jnp.sum(values[w * rows : (w + 1) * rows], axis=0, keepdims=True)
                sums[pl.ds(at * windows + w, 1), :] = total

        state = hidden_state[...]
        sig_f = jax.nn.sigmoid(part(5))
        grad_layer = cotangent[...].astype(f32)
        layer_out[...] = (state + sig_f * ffn_out[...]).astype(bf16)
        window_sums(3, grad_layer * ffn_out[...] * sig_f * (1.0 - sig_f))
        normed, inv_std = norm_rows(state)
        window_sums(1, grad_in[...])
        window_sums(2, grad_in[...] * normed)
        back = norm_back(grad_in[...] * (1.0 + part(4)), normed, inv_std)
        grad_hidden = grad_layer + back
        grad_hidden_out[...] = grad_hidden
        sig_a = jax.nn.sigmoid(part(2))
        window_sums(0, grad_hidden * attn_out[...] * sig_a * (1.0 - sig_a))
        grad_attn_out = (sig_a * grad_hidden).astype(bf16)
        grad_out[...] = dot(mixed[...].T, grad_attn_out).astype(bf16)
        grad_mixed[...] = dot_nt(grad_attn_out, out_weight[...]).astype(bf16)


def feed_forward(modulation, tokens, cotangent, mixed, out_weight, gate, up, down, windows):
    total_rows, width = tokens.shape
    hidden = gate.shape[1]
    blocks = 3
    size = hidden // blocks

    def whole(shape):
        return pl.BlockSpec(shape, lambda j: (0, 0))

    columns = pl.BlockSpec((width, size), lambda j: (0, j))
    lines = pl.BlockSpec((size, width), lambda j: (j, 0))
    row = (total_rows, width)
    return pl.pallas_call(
        functools.partial(feed_forward_kernel, windows),
        grid=(blocks,),
        in_specs=[whole(modulation.shape)]
        + [whole(row)] * 3
        + [whole(out_weight.shape), columns, columns, lines],
        out_specs=[whole(row)] * 3
        + [whole(out_weight.shape), whole((4 * windows, width)), columns, columns, lines],
        out_shape=[
            jax.ShapeDtypeStruct(row, bf16),
            jax.ShapeDtypeStruct(row, f32),
            jax.ShapeDtypeStruct(row, bf16),
            jax.ShapeDtypeStruct(out_weight.shape, bf16),
            jax.ShapeDtypeStruct((4 * windows, width), f32),
            jax.ShapeDtypeStruct(gate.shape, bf16),
            jax.ShapeDtypeStruct(up.shape, bf16),
            jax.ShapeDtypeStruct(down.shape, bf16),
        ],
        scratch_shapes=[
            pltpu.VMEM(row, f32),
            pltpu.VMEM(row, f32),
            pltpu.VMEM(row, bf16),
            pltpu.VMEM((width, total_rows), bf16),
            pltpu.VMEM(row, bf16),
            pltpu.VMEM(row, f32),
            pltpu.VMEM(row, f32),
        ],
        compiler_params=pltpu.CompilerParams(vmem_limit_bytes=63 * 2**20),
        cost_estimate=pl.CostEstimate(
            flops=18 * total_rows * width * hidden, bytes_accessed=40 * 2**20, transcendentals=0
        ),
        name="ffn",
    )(modulation, tokens, cotangent, mixed, out_weight, gate, up, down)


def three_parts(values):
    parts = []
    for _ in range(3):
        part = lax.reduce_precision(values, 8, 7)
        parts.append(part.astype(bf16))
        values = values - part
    return parts


def per_device(
    tokens,
    cotangent,
    noise_times,
    cath_ids,
    chain_start,
    distance_bins,
    class_table,
    ada_weight,
    qkv_weight,
    out_weight,
    pair_table,
    pair_weight,
    gate_weight,
    up_weight,
    down_weight,
):
    windows, row_count, width = tokens.shape
    length = distance_bins.shape[2]
    head_count = pair_weight.shape[1]
    head_size = width // head_count
    table_rows = pair_table.shape[0]
    bin_count = table_rows // 2
    classes = class_table.shape[0]
    total_rows = windows * row_count
    win_count = lax.axis_size("win")
    seq_count = lax.axis_size("seq")
    devices = win_count * seq_count
    class_onehot = (cath_ids[:, None] == jnp.arange(classes, dtype=jnp.int32)[None, :]).astype(f32)
    pre_cond = jnp.dot(
        class_onehot, class_table.astype(f32), precision=highest
    ) + time_embed(noise_times, width)
    cond_sig = jax.nn.sigmoid(pre_cond)
    condition = pre_cond * cond_sig
    cond_parts = jnp.concatenate(
        [jnp.pad(part, ((0, 8 - windows), (0, 0))) for part in three_parts(condition)], axis=0
    )
    modulation, queries, keys_values, attn_in_all, attn_mixed, probs, pair_index = forward(
        chain_start,
        tokens,
        cond_parts,
        pair_table,
        pair_weight.T,
        ada_weight,
        qkv_weight,
        distance_bins,
        head_size,
    )
    flat_tokens = tokens.reshape(total_rows, width)
    layer_out, grad_hidden, grad_mixed, grad_out, sums, grad_gate, grad_up, grad_down = feed_forward(
        modulation,
        flat_tokens,
        cotangent.reshape(total_rows, width),
        attn_mixed,
        out_weight,
        gate_weight,
        up_weight,
        down_weight,
        windows,
    )
    scale_attn = modulation[:windows, width : 2 * width]
    early = [
        sums,
        pre_cond / seq_count,
        jnp.pad(class_onehot, ((0, 0), (0, width - classes))) / seq_count,
    ]
    owned_gate, owned_up, owned_down, owned_out, owned_q, owned_kv, grad_tokens, small = backward(
        [grad_gate, grad_up, grad_down, grad_out],
        [
            queries,
            keys_values,
            probs,
            grad_mixed,
            attn_in_all,
            qkv_weight,
            pair_index,
            flat_tokens,
            grad_hidden,
        ],
        1.0 + scale_attn,
        early,
        (windows, row_count, length, head_size),
        6,
        [False, True, False, True, True, True],
    )
    class_share = classes * width // devices
    flat_gate, flat_up, flat_down, flat_out, flat_qkv, grad_tokens, of_class, flat_ada, of_table, of_weight = tail(
        [owned_gate, owned_up, owned_down, owned_out, owned_q, owned_kv],
        grad_tokens,
        small,
        ada_weight,
        pair_table,
        pair_weight.T,
        windows,
        class_share,
    )
    return (
        layer_out.reshape(windows, row_count, width),
        grad_tokens.reshape(windows, row_count, width),
        of_class.reshape(-1),
        flat_ada.reshape(-1),
        flat_qkv.reshape(-1),
        flat_out.reshape(-1),
        of_table.reshape(-1),
        of_weight.reshape(-1),
        flat_gate.reshape(-1),
        flat_up.reshape(-1),
        flat_down.reshape(-1),
    )


def solution(mesh):
    rows = P("win", "seq", None)
    flat = P(("win", "seq"))
    placed = (rows, rows, P("win"), P("win"), P("win"), rows) + (P(),) * 9
    return jax.shard_map(
        per_device, mesh=mesh, in_specs=placed, out_specs=(rows, rows) + (flat,) * 9, check_vma=False
    )
```

```python
import functools
import math

import jax
import jax.numpy as jnp
from jax import lax
from jax.experimental import pallas as pl
from jax.experimental.pallas import tpu as pltpu
from jax.sharding import PartitionSpec as P

highest = lax.Precision.HIGHEST
norm_eps = 1e-06
f32 = jnp.float32
bf16 = jnp.bfloat16


def norm_back(grad_normed, normed, inv_std):
    first_mean = jnp.mean(grad_normed, axis=-1, keepdims=True)
    second_mean = jnp.mean(grad_normed * normed, axis=-1, keepdims=True)
    return (grad_normed - first_mean - normed * second_mean) * inv_std


def time_embed(noise_times, model_width):
    half_width = model_width // 2
    frequency = jnp.exp(
        -math.log(10000.0) * jnp.arange(half_width).astype(f32) / half_width
    )
    angles = 1000.0 * noise_times[:, None] * frequency[None, :]
    return jnp.concatenate([jnp.sin(angles), jnp.cos(angles)], axis=-1)


def dot(a, b):
    return jnp.dot(a, b, preferred_element_type=f32)


def dot_nt(a, b):
    return lax.dot_general(a, b, (((1,), (1,)), ((), ())), preferred_element_type=f32)


def dot_tn(a, b):
    return lax.dot_general(a, b, (((0,), (0,)), ((), ())), preferred_element_type=f32)


def pair_halves(values, head_size):
    lane = lax.broadcasted_iota(jnp.int32, values.shape, 1)
    zero = jnp.zeros_like(values)
    return jnp.concatenate(
        [jnp.where(lane < head_size, values, zero), jnp.where(lane >= head_size, values, zero)], axis=0
    )


def pair_diagonal(values, head_size, rows):
    return jnp.concatenate([values[:head_size, :rows], values[head_size:, rows:]], axis=0).T


def forward_kernel(
    sizes,
    facts_ref,
    tokens_hbm,
    cond_ref,
    pair_table,
    pair_weight,
    ada_hbm,
    weight_hbm,
    bins_hbm,
    mod_ref,
    q_ref,
    kv_ref,
    in_ref,
    mixed_ref,
    probs_ref,
    index_ref,
    ada_ref,
    weight_ref,
    bins_ref,
    tokens_ref,
    table_ref,
    load_sem,
    gathered,
    send_sem,
    recv_sem,
):
    windows, rows, length, head_size = sizes
    width = q_ref.shape[1]
    count = gathered.shape[0]
    here = lax.axis_index("seq")
    head_scale = 1.0 / math.sqrt(head_size)
    loads = [
        Load(source, target, load_sem.at[at])
        for at, (source, target) in enumerate(
            [(ada_hbm, ada_ref), (weight_hbm, weight_ref), (bins_hbm, bins_ref), (tokens_hbm, tokens_ref)]
        )
    ]
    for load in loads:
        load.copy.start()
    barrier = pltpu.get_barrier_semaphore()
    for sign in (1, -1):

        @pl.when((here + sign >= 0) & (here + sign < count))
        def _(sign=sign):
            pl.semaphore_signal(
                barrier, inc=1, device_id={"seq": here + sign}, device_id_type=pl.DeviceIdType.MESH
            )

    pl.semaphore_wait(barrier, jnp.where((here == 0) | (here == count - 1), 1, 2))

    def copy(way, hop, window, shard, source=None):
        slot = gathered.at[shard, window]
        return pltpu.make_async_remote_copy(
            src_ref=slot if source is None else source,
            dst_ref=slot,
            send_sem=send_sem.at[way, hop, window],
            recv_sem=recv_sem.at[way, hop, window],
            device_id={"seq": here + 1 - 2 * way},
            device_id_type=pl.DeviceIdType.MESH,
        )

    def for_sends(body):
        for window in range(windows):
            for way in range(2):

                @pl.when((here + 1 - 2 * way >= 0) & (here + 1 - 2 * way < count))
                def _(way=way, window=window):
                    body(copy(way, 0, window, here, tokens_hbm.at[window]))

    for_sends(lambda each: each.start())
    table_ref[...] = dot_nt(pair_weight[...], pair_table[...]).astype(bf16).astype(f32)
    loads[0].copy.wait()
    for part in range(mod_ref.shape[1] // width):
        cols = slice(part * width, (part + 1) * width)
        mod = dot(cond_ref[...], ada_ref[:, cols])
        mod_ref[:, cols] = mod[:8] + mod[8:16] + mod[16:24]
    loads[1].copy.wait()
    loads[2].copy.wait()
    loads[3].copy.wait()

    def project(window, shard, values):
        normed, _ = norm_rows(values.astype(f32))
        scale = 1.0 + mod_ref[pl.ds(window, 1), width : 2 * width]
        block = (normed * scale + mod_ref[pl.ds(window, 1), :width]).astype(bf16)
        at = pl.ds(pl.multiple_of(window * length + shard * rows, rows), rows)
        in_ref[at, :] = block
        kv_ref[at, :] = dot(block, weight_ref[:, width:]).astype(bf16)
        return block

    def own(window, carry):
        block = project(window, here, tokens_ref[window])
        at = pl.ds(pl.multiple_of(window * rows, rows), rows)
        q_ref[at, :] = dot(block, weight_ref[:, :width]).astype(bf16)
        return carry

    lax.fori_loop(0, windows, own, 0)

    def arrive(way, hop, window):
        sign = 1 - 2 * way
        shard = here - sign * (hop + 1)

        @pl.when((shard >= 0) & (shard < count))
        def _():
            copy(way, hop, window, shard).wait_recv()

            @pl.when((here + sign >= 0) & (here + sign < count))
            def _():
                copy(way, hop + 1, window, shard).start()

            project(window, shard, gathered[shard, window])

    def relay(at, carry):
        arrive(lax.rem(at, 2), at // (2 * windows), lax.rem(at // 2, windows))
        return carry

    lax.fori_loop(0, (count - 2) * windows * 2, relay, 0)

    def finish(window, carry):
        def last(way, inner):
            arrive(way, count - 2, window)
            return inner

        lax.fori_loop(0, 2, last, 0)
        rows_at = pl.ds(pl.multiple_of(window * rows, rows), rows)
        keys_at = pl.ds(pl.multiple_of(window * length, length), length)
        start = facts_ref[window]
        bins = bins_ref[window].T
        key_first = lax.broadcasted_iota(jnp.int32, bins.shape, 0) < start
        row_first = lax.broadcasted_iota(jnp.int32, bins.shape, 1) + here * rows < start
        index_ref[window] = bins + jnp.where(key_first == row_first, table_ref.shape[1] // 2, 0)

        def one_pair(pair, inner):
            begin = pl.multiple_of(pair * 2 * head_size, 2 * head_size)
            cols = pl.ds(begin, 2 * head_size)
            v_cols = pl.ds(width + begin, 2 * head_size)
            index = index_ref[window]
            biases = []
            for head in range(2):
                entries = jnp.broadcast_to(table_ref[pl.ds(2 * pair + head, 1), :], index.shape)
                biases.append(jnp.take_along_axis(entries, index, axis=1, mode="promise_in_bounds"))
            q_pair = pair_halves(q_ref[rows_at, cols] * head_scale, head_size)
            scores = dot_nt(kv_ref[keys_at, cols], q_pair) + jnp.concatenate(biases, axis=1)
            top = jnp.max(scores, axis=0, keepdims=True)
            raised = jnp.exp(scores - top)
            total = jnp.sum(raised, axis=0, keepdims=True)
            probs = (raised * (1.0 / total)).astype(bf16)
            mixed = dot(kv_ref[keys_at, v_cols].T, probs)
            mixed_ref[rows_at, cols] = pair_diagonal(mixed, head_size, rows).astype(bf16)
            probs_ref[window, pair] = probs
            return inner

        lax.fori_loop(0, width // (2 * head_size), one_pair, 0)
        return carry

    lax.fori_loop(0, windows, finish, 0)
    for_sends(lambda each: each.wait_send())

    def sent(at, carry):
        way, hop, window = (lax.rem(at, 2), at // (2 * windows), lax.rem(at // 2, windows))
        sign = 1 - 2 * way
        shard = here - sign * (hop + 1)

        @pl.when((shard >= 0) & (shard < count) & (here + sign >= 0) & (here + sign < count))
        def _():
            copy(way, hop + 1, window, shard).wait_send()

        return carry

    lax.fori_loop(0, (count - 2) * windows * 2, sent, 0)


def forward(facts, tokens, cond_parts, pair_table, pair_weight, ada_weight, qkv_weight, bins, head_size):
    windows, rows, length = bins.shape
    width = tokens.shape[-1]
    pairs = width // (2 * head_size)
    count = lax.axis_size("seq")
    vmem = pl.BlockSpec(memory_space=pltpu.VMEM)
    hbm = pl.BlockSpec(memory_space=pltpu.HBM)
    return pl.pallas_call(
        functools.partial(forward_kernel, (windows, rows, length, head_size)),
        in_specs=[pl.BlockSpec(memory_space=pltpu.SMEM), hbm, vmem, vmem, vmem, hbm, hbm, hbm],
        out_specs=[vmem] * 7,
        out_shape=[
            jax.ShapeDtypeStruct((8, ada_weight.shape[1]), f32),
            jax.ShapeDtypeStruct((windows * rows, width), bf16),
            jax.ShapeDtypeStruct((windows * length, 2 * width), bf16),
            jax.ShapeDtypeStruct((windows * length, width), bf16),
            jax.ShapeDtypeStruct((windows * rows, width), bf16),
            jax.ShapeDtypeStruct((windows, pairs, length, 2 * rows), bf16),
            jax.ShapeDtypeStruct((windows, length, rows), jnp.int32),
        ],
        scratch_shapes=[
            pltpu.VMEM(ada_weight.shape, bf16),
            pltpu.VMEM(qkv_weight.shape, bf16),
            pltpu.VMEM(bins.shape, jnp.int32),
            pltpu.VMEM(tokens.shape, bf16),
            pltpu.VMEM((pair_weight.shape[0], pair_table.shape[0]), f32),
            pltpu.SemaphoreType.DMA((4,)),
            pltpu.VMEM((count, windows, rows, width), bf16),
            pltpu.SemaphoreType.DMA((2, count - 1, windows)),
            pltpu.SemaphoreType.DMA((2, count - 1, windows)),
        ],
        compiler_params=pltpu.CompilerParams(
            collective_id=0, has_side_effects=True, vmem_limit_bytes=63 * 2**20
        ),
        cost_estimate=pl.CostEstimate(flops=10**10, bytes_accessed=40 * 2**20, transcendentals=0),
        name="forward",
    )(facts, tokens, cond_parts, pair_table, pair_weight, ada_weight, qkv_weight, bins)


def bit_steps():
    win_bits = int(math.log2(lax.axis_size("win")))
    seq_bits = int(math.log2(lax.axis_size("seq")))
    return [("win", bit) for bit in range(win_bits)[::-1]] + [
        ("seq", bit) for bit in range(seq_bits)[::-1]
    ]


CORE = ("win", 0)


def my_bit(step):
    return lax.rem(lax.axis_index(step[0]) // (1 << step[1]), 2)


def partner(step):
    return {step[0]: lax.axis_index(step[0]) + (1 - 2 * my_bit(step)) * (1 << step[1])}


def greet():
    barrier = pltpu.get_barrier_semaphore()
    for step in bit_steps():
        pl.semaphore_signal(barrier, inc=1, device_id=partner(step), device_id_type=pl.DeviceIdType.MESH)
    pl.semaphore_wait(barrier, len(bit_steps()))


def remote(source, target, send_sem, recv_sem, step):
    return pltpu.make_async_remote_copy(
        src_ref=source,
        dst_ref=target,
        send_sem=send_sem,
        recv_sem=recv_sem,
        device_id=partner(step),
        device_id_type=pl.DeviceIdType.MESH,
    )


def each_block(shape, body):
    lead = shape[:-2]
    count = math.prod(lead)

    def one(flat, carry):
        index = []
        for size in lead[::-1]:
            index.append(lax.rem(flat, size))
            flat = flat // size
        body(tuple(index[::-1]))
        return carry

    if count == 1:
        body((0,) * len(lead))
    else:
        lax.fori_loop(0, count, one, 0)


class Flow:
    def __init__(self, rows, columns, chunks, flip, offset):
        steps = bit_steps()
        win_steps = [step for step in steps if step[0] == "win" and step != CORE]
        self.seq_steps = [step for step in steps if step[0] == "seq"]
        self.far = win_steps if flip else win_steps[::-1]
        self.names = win_steps
        self.near = self.seq_steps[::-1]
        self.chunks = chunks
        self.offset = offset
        self.width = columns // chunks
        self.share = rows // 2 ** len(steps)
        self.block = self.share * 2 ** len(self.seq_steps)
        self.columns = columns

    def view(self, grad):
        return grad.reshape((2,) * (len(self.far) + 1) + (self.block, self.columns))

    def scratch(self):
        chunks, width = (self.chunks, self.width)
        far, near = (len(self.far), len(self.near))
        shapes = [(2,) * far + (self.block, width)] * 2
        shapes += [(2,) * (far - 1 - i) + (self.block, width) for i in range(far)]
        shapes += [(2,) * near + (self.share, width)]
        shapes += [(2,) * (near - 1 - i) + (self.share, width) for i in range(near)]
        buffers = [pltpu.VMEM((chunks if at else 2,) + shape, bf16) for at, shape in enumerate(shapes)]
        count = 1 + far + near
        return buffers + [
            pltpu.SemaphoreType.DMA((chunks,)),
            pltpu.SemaphoreType.DMA((count, chunks)),
            pltpu.SemaphoreType.DMA((count, chunks)),
        ]

    def bind(self, grad, out, scratch):
        self.grad, self.out = grad, out
        far, near = (len(self.far), len(self.near))
        self.mine = scratch[0]
        self.first = scratch[1]
        self.far_bufs = list(scratch[2 : 2 + far])
        self.turn = scratch[2 + far]
        self.near_bufs = list(scratch[3 + far : 3 + far + near])
        self.local_sem, self.send_sem, self.recv_sem = scratch[3 + far + near :]

    def piece(self, bit, chunk):
        index = (slice(None),) * len(self.far) + (bit, slice(None))
        return self.grad.at[index + (pl.ds(pl.multiple_of(chunk * self.width, 128), self.width),)]

    def local_copy(self, chunk):
        return pltpu.make_async_copy(
            self.piece(my_bit(CORE), chunk), self.mine.at[lax.rem(chunk, 2)], self.local_sem.at[chunk]
        )

    def copy(self, stage, chunk):
        send, recv = (self.send_sem.at[stage, chunk], self.recv_sem.at[stage, chunk])
        far = len(self.far)
        if stage == 0:
            return remote(
                self.piece(1 - my_bit(CORE), chunk), self.first.at[chunk], send, recv, CORE
            )
        if stage <= far:
            step = self.far[stage - 1]
            source = ([self.first] + self.far_bufs)[stage - 1]
            target = self.far_bufs[stage - 1]
            axis = self.axis_of(step, self.far[: stage - 1], self.names)
        else:
            at = stage - 1 - far
            step = self.near[at]
            source = ([self.turn] + self.near_bufs)[at]
            target = self.near_bufs[at]
            axis = self.axis_of(step, self.near[:at], self.seq_steps)
        index = (chunk,) + (slice(None),) * axis + (1 - my_bit(step),)
        return remote(source.at[index], target.at[chunk], send, recv, step)

    def axis_of(self, step, gone, names):
        return [name for name in names if name not in gone].index(step)

    def stages(self):
        return 2 + len(self.far) + len(self.near)

    def run(self, stage, chunk):
        far, near = (len(self.far), len(self.near))
        if stage == 0:
            self.local_copy(chunk).start()
            self.copy(0, chunk).start()
            return
        self.copy(stage - 1, chunk).wait_recv()
        if stage == 1:
            self.local_copy(chunk).wait()
            shape = self.first.shape[1:]

            def add_first(index):
                at = (chunk,) + index
                kept = self.mine[(lax.rem(chunk, 2),) + index].astype(f32)
                self.first[at] = (self.first[at].astype(f32) + kept).astype(bf16)

            each_block(shape, add_first)
        elif stage < 1 + far:
            target = self.far_bufs[stage - 2]
            source = ([self.first] + self.far_bufs)[stage - 2]
            self.add_half(target, source, self.far, self.names, stage - 2, chunk)
        elif stage == 1 + far:
            step = self.far[-1]
            source = ([self.first] + self.far_bufs)[far - 1]
            target = self.far_bufs[far - 1]
            total = target[chunk].astype(f32) + source[chunk, my_bit(step)].astype(f32)
            total = total.astype(bf16)
            count = 2**near
            for owner in range(count):
                at, rest = ((), owner)
                for _ in range(near):
                    at = (rest % 2,) + at
                    rest = rest // 2
                self.turn[(chunk,) + at] = total[owner * self.share : (owner + 1) * self.share]
        elif stage < 1 + far + near:
            at = stage - 2 - far
            source = ([self.turn] + self.near_bufs)[at]
            self.add_half(self.near_bufs[at], source, self.near, self.seq_steps, at, chunk)
        else:
            source = ([self.turn] + self.near_bufs)[near - 1]
            kept = source[chunk, my_bit(self.near[-1])]
            total = self.near_bufs[near - 1][chunk].astype(f32) + kept.astype(f32)
            self.out[:, pl.ds(pl.multiple_of(chunk * self.width, 128), self.width)] = total
        if stage < 1 + far + near:
            self.copy(stage, chunk).start()

    def add_half(self, target, source, steps, names, at, chunk):
        step = steps[at]
        axis = self.axis_of(step, steps[:at], names)
        bit = my_bit(step)

        def add(index):
            from_at = (chunk,) + index[:axis] + (bit,) + index[axis:]
            to_at = (chunk,) + index
            target[to_at] = (target[to_at].astype(f32) + source[from_at].astype(f32)).astype(bf16)

        each_block(target.shape[1:], add)

    def drain(self, chunk):
        for stage in range(self.stages() - 1):
            self.copy(stage, chunk).wait_send()


class Load:
    def __init__(self, source, target, sem):
        self.target = target
        self.copy = pltpu.make_async_copy(source, target, sem)


class SmallGather:
    def __init__(self, mine, halves, gathered, send_sem, recv_sem):
        self.mine, self.halves, self.gathered = mine, halves, gathered
        self.send_sem, self.recv_sem = send_sem, recv_sem
        self.steps = bit_steps()[::-1]
        self.seq_count = len([step for step in self.steps if step[0] == "seq"])

    def copy(self, at):
        step = self.steps[at]
        if at < self.seq_count:
            source, target = self.mine.at[at], self.halves.at[at]
        else:
            size = 1 << step[1]
            here = lax.axis_index("win")
            block = pl.ds(here - lax.rem(here, size), size)
            source = target = self.gathered.at[block]
        return remote(source, target, self.send_sem.at[at], self.recv_sem.at[at], step)

    def run(self, at):
        if at > 0:
            self.copy(at - 1).wait_recv()
            if at <= self.seq_count:
                total = self.mine[at - 1] + self.halves[at - 1]
                if at < self.seq_count:
                    self.mine[at] = total
                else:
                    self.gathered[lax.axis_index("win")] = total
        if at < len(self.steps):
            self.copy(at).start()

    def drain(self):
        for at in range(len(self.steps)):
            self.copy(at).wait_send()


def norm_rows(values):
    centered = values - jnp.mean(values, axis=-1, keepdims=True)
    inv_std = lax.rsqrt(jnp.mean(centered * centered, axis=-1, keepdims=True) + norm_eps)
    return (centered * inv_std, inv_std)


def backward_kernel(flows, sizes, *refs):
    windows, rows, length, head_size = sizes
    refs = list(refs)

    def take(count):
        taken = refs[:count]
        del refs[:count]
        return taken

    grads = take(4)
    sources = take(9)
    (scale_ref,) = take(1)
    early_refs = take(3)
    shares = take(6)
    tokens_out, small_out = take(2)
    targets = take(9)
    (load_sem,) = take(1)
    grad_q, grad_kv, grad_scores, q_weight, kv_weight, own_in = take(6)
    far_in, far_half, far_own, far_send, far_recv = take(5)
    (table_sum,) = take(1)
    small = SmallGather(*take(5))
    (small_sem,) = take(1)
    for flow, grad, share in zip(flows, grads + [q_weight, kv_weight], shares):
        flow.bind(grad, share, take(len(flow.scratch())))
    loads = [Load(s, t, load_sem.at[at]) for at, (s, t) in enumerate(zip(sources, targets))]
    q_ref, kv_ref, probs_ref, grad_ref, in_ref, weight_ref, index_ref, tokens_ref, hidden_ref = targets
    width = q_ref.shape[1]
    head_scale = 1.0 / math.sqrt(head_size)
    heads = width // head_size
    seq_steps = bit_steps()[::-1][: small.seq_count]
    for load in loads:
        load.copy.start()
    greet()

    def attend_back(window):
        rows_at = pl.ds(pl.multiple_of(window * rows, rows), rows)
        keys_at = pl.ds(pl.multiple_of(window * length, length), length)

        def one_pair(pair, carry):
            start = pl.multiple_of(pair * 2 * head_size, 2 * head_size)
            cols = pl.ds(start, 2 * head_size)
            v_cols = pl.ds(width + start, 2 * head_size)
            q_pair = pair_halves(q_ref[rows_at, cols] * head_scale, head_size)
            g_pair = pair_halves(grad_ref[rows_at, cols], head_size)
            probs = probs_ref[window, pair]
            grad_kv[keys_at, v_cols] = dot(probs, g_pair).astype(bf16)
            grad_probs = dot_nt(kv_ref[keys_at, v_cols], g_pair)
            probs = probs.astype(f32)
            delta = jnp.sum(probs * grad_probs, axis=0, keepdims=True)
            scores = (probs * (grad_probs - delta)).astype(bf16)
            grad_kv[keys_at, cols] = dot(scores, q_pair).astype(bf16)
            back = dot(kv_ref[keys_at, cols].T, scores)
            grad_q[rows_at, cols] = (pair_diagonal(back, head_size, rows) * head_scale).astype(bf16)
            grad_scores[window, 2 * pair] = scores[:, :rows]
            grad_scores[window, 2 * pair + 1] = scores[:, rows:]
            return carry

        lax.fori_loop(0, heads // 2, one_pair, 0)

    def split_rows(target, values, cols):
        lead = target.shape[:-2]
        block = target.shape[-2]
        for at in range(math.prod(lead)):
            index, rest = ((), at)
            for size in lead[::-1]:
                index = (rest % size,) + index
                rest = rest // size
            target[index + (slice(None), cols)] = values[at * block : (at + 1) * block].astype(bf16)

    def project_back():
        def one_window(window, carry):
            keys_at = pl.ds(pl.multiple_of(window * length, length), length)
            far = dot_nt(grad_kv[keys_at, :], weight_ref[:, width:]).astype(bf16)
            split_owner(far, window)
            return carry

        def split_owner(far, window):
            rows_at = pl.ds(pl.multiple_of(window * rows, rows), rows)
            for owner in range(length // rows):
                index, rest = ((), owner)
                for _ in seq_steps:
                    index = (rest % 2,) + index
                    rest = rest // 2
                far_in[index + (rows_at,)] = far[owner * rows : (owner + 1) * rows]

        lax.fori_loop(0, windows, one_window, 0)
        far_copy(0).start()
        own_in[...] = dot_nt(grad_q[...], weight_ref[:, :width])

    def weight_grads():
        here = lax.axis_index("seq") * rows
        own = [in_ref[pl.ds(pl.multiple_of(w * length + here, rows), rows), :] for w in range(windows)]
        split_rows(q_weight, dot(jnp.concatenate(own, axis=0).T, grad_q[...]), slice(None))
        turned = in_ref[...].T
        step = 512
        for at in range(2 * width // step):
            cols = slice(at * step, (at + 1) * step)
            split_rows(kv_weight, dot(turned, grad_kv[:, cols]), cols)

    far_bufs = [far_in] + [far_half, far_own][-small.seq_count :]

    def far_copy(at):
        step = seq_steps[at]
        index = (slice(None),) * (small.seq_count - 1 - at) + (1 - my_bit(step),)
        return remote(
            far_bufs[at].at[index], far_bufs[at + 1], far_send.at[at], far_recv.at[at], step
        )

    def far_add(at):
        far_copy(at).wait_recv()
        step = seq_steps[at]
        bit = my_bit(step)
        target, source = far_bufs[at + 1], far_bufs[at]
        lead = target.shape[:-2]
        for flat in range(math.prod(lead)):
            for window in range(windows):
                index = ((flat,) if lead else ()) + (pl.ds(window * rows, rows),)
                kept = source[index[:-1] + (bit,) + index[-1:]].astype(f32)
                target[index] = (target[index].astype(f32) + kept).astype(bf16)
        if at + 1 < small.seq_count:
            far_copy(at + 1).start()

    def table_back(window):
        group = 16
        entries = table_sum.shape[1]

        def one_group(at, carry):
            keys = pl.ds(pl.multiple_of(at * group, group), group)
            scores = grad_scores[window, :, keys, :].astype(f32)
            scores = jnp.concatenate([scores, jnp.zeros((16 - heads, group, rows), f32)], axis=0)
            scores = jnp.swapaxes(scores, 0, 1).astype(bf16)
            index = index_ref[window, keys, :]
            spot = lax.broadcasted_iota(jnp.int32, (entries, rows), 0)
            total = jnp.zeros((16, entries), f32)
            for key in range(0, group, 2):
                terms, hots = [], []
                for which in (key, key + 1):
                    terms.append(scores[which])
                    hot = spot == jnp.broadcast_to(index[which : which + 1], (entries, rows))
                    hots.append(jnp.where(hot, 1.0, 0.0).astype(bf16))
                total = total + dot_nt(
                    jnp.concatenate(terms, axis=1), jnp.concatenate(hots, axis=1)
                )
            table_sum[...] += total
            return carry

        lax.fori_loop(0, length // group, one_group, 0)

    def finish_tokens():
        shift_rows, scale_rows = [], []
        for window in range(windows):
            rows_at = pl.ds(window * rows, rows)
            normed, inv_std = norm_rows(tokens_ref[rows_at, :].astype(f32))
            grad_in = own_in[rows_at, :] + far_own[rows_at, :].astype(f32)
            shift_rows.append(jnp.sum(grad_in, axis=0, keepdims=True))
            scale_rows.append(jnp.sum(grad_in * normed, axis=0, keepdims=True))
            dy = grad_in * scale_ref[pl.ds(window, 1), :]
            first = jnp.mean(dy, axis=-1, keepdims=True)
            second = jnp.mean(dy * normed, axis=-1, keepdims=True)
            back = (dy - first - normed * second) * inv_std
            tokens_out[rows_at, :] = (hidden_ref[rows_at, :] + back).astype(bf16)
        facts = jnp.concatenate(shift_rows + scale_rows + [early[...] for early in early_refs], axis=0)
        small.mine[0, :, :width] = facts
        small.mine[0, :, width:] = table_sum[...]

    steps = len(small.steps)
    jobs = {}
    for window in range(windows):
        jobs.setdefault(window, []).append(functools.partial(attend_back, window))
    jobs.setdefault(windows, []).extend([project_back, weight_grads])
    jobs.setdefault(windows + 1, []).append(functools.partial(table_back, 0))
    jobs.setdefault(windows + 2, []).append(functools.partial(far_add, 0))
    for window in range(1, windows):
        jobs.setdefault(windows + 2 + window, []).append(functools.partial(table_back, window))
    last = 2 * windows + 2
    for at in range(1, small.seq_count):
        jobs.setdefault(last + 2 * (at - 1), []).append(functools.partial(far_add, at))
    last = last + 2 * (small.seq_count - 2)
    jobs[last].append(finish_tokens)
    for at in range(steps + 1):
        jobs.setdefault(last + at, []).append(functools.partial(small.run, at))
    chunks = flows[0].chunks
    stages = flows[0].stages()
    order = [1, 0] + list(range(2, stages))
    near = len(flows[0].near)
    lags = list(range(stages - near)) + [stages - near + 1 + 2 * at for at in range(near)]
    total = max(max(flow.offset for flow in flows) + chunks + lags[-1], max(jobs) + 1)
    table_sum[...] = jnp.zeros_like(table_sum)

    def step(at, carry):
        for stage in order:
            for offset in sorted({flow.offset for flow in flows}):
                chunk = at - lags[stage] - offset

                @pl.when((chunk >= 0) & (chunk < chunks))
                def _(stage=stage, chunk=chunk, offset=offset):
                    for flow in flows:
                        if flow.offset == offset:
                            flow.run(stage, chunk)

            if stage == 0:

                @pl.when(at == 0)
                def _():
                    for load in loads:
                        load.copy.wait()

                for when, work in sorted(jobs.items()):

                    @pl.when(at == when)
                    def _(work=work):
                        for job in work:
                            job()

        return carry

    lax.fori_loop(0, total, step, 0)
    store_small = pltpu.make_async_copy(small.gathered, small_out, small_sem)
    store_small.start()

    def finish(chunk, carry):
        for flow in flows:
            flow.drain(chunk)
        return carry

    lax.fori_loop(0, chunks, finish, 0)
    for at in range(small.seq_count):
        far_copy(at).wait_send()
    small.drain()
    store_small.wait()


def backward(grads, loads, scales, early, sizes, chunks, flips):
    windows, rows, length, head_size = sizes
    width = loads[0].shape[1]
    shapes = [g.shape for g in grads] + [(width, width), (width, 2 * width)]
    offsets = [0] * len(grads) + [windows + 1] * 2
    flows = [Flow(s[0], s[1], chunks, flip, offset) for s, flip, offset in zip(shapes, flips, offsets)]
    win_bits = int(math.log2(lax.axis_size("win")))
    seq_bits = int(math.log2(lax.axis_size("seq")))
    total_rows = windows * rows
    small_shape = (16, width + 128)
    heads = width // head_size
    near = (2,) * seq_bits
    scratch = [pltpu.VMEM(load.shape, load.dtype) for load in loads]
    scratch += [
        pltpu.SemaphoreType.DMA((len(loads),)),
        pltpu.VMEM((total_rows, width), bf16),
        pltpu.VMEM((windows * length, 2 * width), bf16),
        pltpu.VMEM((windows, heads, length, rows), bf16),
        pltpu.VMEM((2,) * win_bits + (flows[-2].block, width), bf16),
        pltpu.VMEM((2,) * win_bits + (flows[-1].block, 2 * width), bf16),
        pltpu.VMEM((total_rows, width), f32),
        pltpu.VMEM(near + (total_rows, width), bf16),
        pltpu.VMEM(near[1:] + (total_rows, width), bf16),
        pltpu.VMEM((total_rows, width), bf16),
        pltpu.SemaphoreType.DMA((seq_bits,)),
        pltpu.SemaphoreType.DMA((seq_bits,)),
        pltpu.VMEM((16, 128), f32),
        pltpu.VMEM((seq_bits,) + small_shape, f32),
        pltpu.VMEM((seq_bits,) + small_shape, f32),
        pltpu.VMEM((2**win_bits,) + small_shape, f32),
        pltpu.SemaphoreType.DMA((win_bits + seq_bits,)),
        pltpu.SemaphoreType.DMA((win_bits + seq_bits,)),
        pltpu.SemaphoreType.DMA,
    ]
    for flow in flows:
        scratch += flow.scratch()
    vmem = pl.BlockSpec(memory_space=pltpu.VMEM)
    out_shape = [jax.ShapeDtypeStruct((flow.share, flow.columns), f32) for flow in flows]
    out_shape += [
        jax.ShapeDtypeStruct((total_rows, width), bf16),
        jax.ShapeDtypeStruct((2**win_bits,) + small_shape, f32),
    ]
    return pl.pallas_call(
        functools.partial(backward_kernel, flows, sizes),
        in_specs=[pl.BlockSpec(memory_space=pl.ANY)] * (len(grads) + len(loads)) + [vmem] * (1 + len(early)),
        out_specs=[vmem] * (len(out_shape) - 1) + [pl.BlockSpec(memory_space=pl.ANY)],
        out_shape=out_shape,
        scratch_shapes=scratch,
        compiler_params=pltpu.CompilerParams(
            collective_id=1, has_side_effects=True, vmem_limit_bytes=62 * 2**20
        ),
        cost_estimate=pl.CostEstimate(flops=10**10, bytes_accessed=200 * 2**20, transcendentals=0),
        name="backward",
    )(*[flow.view(grad) for flow, grad in zip(flows, grads)], *loads, scales, *early)


def tail_kernel(windows, *refs):
    gate, up, down, out, q, kv, tokens, small, ada_hbm, pair_table, pair_weight = refs[:11]
    to_gate, to_up, to_down, to_out, to_qkv, to_tokens, to_class, to_ada, to_table, to_weight = refs[11:21]
    by_row, cond_t, pre_t, onehot_t, table_flat, weight_rows, padded, ada_rows, cond_grad, ada_sem = refs[21:]
    width = tokens.shape[1]
    owner = lax.axis_index("win") * lax.axis_size("seq") + lax.axis_index("seq")
    share = to_class.shape[1]
    per_class = width // share
    column_at = lax.rem(owner, per_class) * share
    window_at = pl.multiple_of(jnp.minimum(column_at // 16 * 16, width - ada_rows.shape[0]), 16)
    load_ada = pltpu.make_async_copy(ada_hbm.at[pl.ds(window_at, ada_rows.shape[0]), :], ada_rows, ada_sem)
    load_ada.start()

    def flatten(target, values, columns, first):
        rows = values.shape[0]
        for at in range(values.shape[1] // 128):
            spot = pl.ds(first // 128 + at, rows, stride=columns // 128)
            target[spot, :] = values[:, at * 128 : (at + 1) * 128]

    for target, source in ((to_gate, gate), (to_up, up), (to_down, down), (to_out, out)):
        flatten(target, source, source.shape[1], 0)
    flatten(to_qkv, q, 3 * width, 0)
    flatten(to_qkv, kv, 3 * width, width)
    to_tokens[...] = tokens[...]

    groups = small.shape[0]

    def sort_rows(group, carry):
        for which in range(8):
            for window in range(windows):
                row = small[group, pl.ds(which * windows + window, 1), :width]
                by_row[pl.ds(window * groups + group, 1), which * width : (which + 1) * width] = row
        return carry

    lax.fori_loop(0, groups, sort_rows, 0)

    def rows_of(which):
        return by_row[:, which * width : (which + 1) * width]

    mods = [rows_of(part) for part in range(6)]
    pre = rows_of(6)
    cond_t[...] = (pre * jax.nn.sigmoid(pre)).T
    pre_t[...] = pre.T
    onehot_t[...] = rows_of(7).T
    ada_share = width // (lax.axis_size("win") * lax.axis_size("seq"))
    cond_rows = cond_t[pl.ds(owner * ada_share, ada_share), :]
    grad_cond = jnp.zeros((ada_rows.shape[0], pre.shape[0]), f32)
    load_ada.wait()
    for part, mod in enumerate(mods):
        product = jnp.dot(cond_rows, mod, precision=highest, preferred_element_type=f32)
        flatten(to_ada, product, 6 * width, part * width)
        grad_cond = grad_cond + lax.dot_general(
            ada_rows[:, part * width : (part + 1) * width].astype(f32),
            mod,
            (((1,), (1,)), ((), ())),
            precision=highest,
            preferred_element_type=f32,
        )
    cond_grad[...] = grad_cond
    grad_cond = cond_grad[pl.ds(column_at - window_at, share), :]
    pre_cols = pre_t[pl.ds(column_at, share), :]
    sig_cols = jax.nn.sigmoid(pre_cols)
    grad_pre = grad_cond * sig_cols * (1.0 + pre_cols * (1.0 - sig_cols))
    mine = jnp.broadcast_to(onehot_t[pl.ds(owner // per_class, 1), :], (8, pre.shape[0]))
    of_class = lax.dot_general(
        mine, grad_pre, (((1,), (1,)), ((), ())), precision=highest, preferred_element_type=f32
    )
    to_class[...] = of_class[:1]

    table = jnp.sum(small[:, :, width:], axis=0)
    heads = pair_weight.shape[0]
    padded[...] = jnp.zeros_like(padded)
    padded[:heads, :] = pair_weight[...].astype(f32)
    grad_table = jnp.dot(table.T, padded[...], precision=highest, preferred_element_type=f32)
    flatten(table_flat, grad_table, grad_table.shape[1], 0)
    count = to_table.shape[0]
    to_table[...] = table_flat[pl.ds(owner * count, count), :]
    grad_weight = jnp.dot(
        table, pair_table[...].astype(f32), precision=highest, preferred_element_type=f32
    )
    weight_rows[...] = grad_weight.T
    count = to_weight.shape[1] // heads
    mine = weight_rows[pl.ds(owner * count, count), :]
    head = lax.broadcasted_iota(jnp.int32, (16, 128), 0)
    lane = lax.broadcasted_iota(jnp.int32, (16, 128), 1)
    spread = jnp.dot(
        mine,
        jnp.where(lax.rem(lane, heads) == head, 1.0, 0.0),
        precision=highest,
        preferred_element_type=f32,
    )
    row = lax.broadcasted_iota(jnp.int32, spread.shape, 0)
    lane = lax.broadcasted_iota(jnp.int32, spread.shape, 1)
    spread = jnp.sum(jnp.where(lane // heads == row, spread, 0.0), axis=0, keepdims=True)
    to_weight[...] = spread[:, : to_weight.shape[1]]


def tail(shares, tokens, small, ada_weight, pair_table, pair_weight, windows, class_share):
    width = tokens.shape[1]
    devices = lax.axis_size("win") * lax.axis_size("seq")
    features = pair_table.shape[1]
    span = class_share if class_share % 16 == 0 else -(-(class_share + 15) // 16) * 16
    sizes = [share.size for share in shares[:4]] + [shares[4].size + shares[5].size]
    table_size = pair_table.size // devices
    ada_size = ada_weight.size // devices
    every = windows * small.shape[0]
    vmem = pl.BlockSpec(memory_space=pltpu.VMEM)

    def flat(size):
        return jax.ShapeDtypeStruct((size // 128, 128), f32)

    return pl.pallas_call(
        functools.partial(tail_kernel, windows),
        in_specs=[vmem] * 8 + [pl.BlockSpec(memory_space=pl.ANY)] + [vmem] * 2,
        out_specs=[vmem] * 10,
        out_shape=[flat(size) for size in sizes]
        + [
            jax.ShapeDtypeStruct(tokens.shape, bf16),
            jax.ShapeDtypeStruct((1, class_share), f32),
            flat(ada_size),
            flat(table_size),
            jax.ShapeDtypeStruct((1, pair_weight.size // devices), f32),
        ],
        scratch_shapes=[pltpu.VMEM((every, 8 * width), f32)]
        + [pltpu.VMEM((width, every), f32)] * 3
        + [
            pltpu.VMEM((pair_table.size // 128, 128), f32),
            pltpu.VMEM((features, 16), f32),
            pltpu.VMEM((16, features), f32),
            pltpu.VMEM((span, ada_weight.shape[1]), bf16),
            pltpu.VMEM((span, every), f32),
            pltpu.SemaphoreType.DMA,
        ],
        name="tail",
    )(*shares, tokens, small, ada_weight, pair_table, pair_weight)


def feed_forward_kernel(windows, *refs):
    mod, tokens, cotangent, mixed, out_weight, gate, up, down = refs[:8]
    layer_out, grad_hidden_out, grad_mixed, grad_out, sums, grad_gate, grad_up, grad_down = refs[8:16]
    attn_out, hidden_state, ffn_in, ffn_in_t, grad_ffn, ffn_out, grad_in = refs[16:]
    total_rows, width = tokens.shape
    rows = total_rows // windows

    def part(which):
        cols = slice(which * width, (which + 1) * width)
        return jnp.concatenate(
            [jnp.broadcast_to(mod[w : w + 1, cols], (rows, width)) for w in range(windows)], axis=0
        )

    @pl.when(pl.program_id(0) == 0)
    def _():
        projected = dot(mixed[...], out_weight[...])
        attn_out[...] = projected
        state = tokens[...].astype(f32) + jax.nn.sigmoid(part(2)) * projected
        hidden_state[...] = state
        normed, _ = norm_rows(state)
        block = (normed * (1.0 + part(4)) + part(3)).astype(bf16)
        ffn_in[...] = block
        ffn_in_t[...] = block.T
        grad_ffn[...] = (jax.nn.sigmoid(part(5)) * cotangent[...].astype(f32)).astype(bf16)
        ffn_out[...] = jnp.zeros_like(ffn_out)
        grad_in[...] = jnp.zeros_like(grad_in)

    gate_val = dot(ffn_in[...], gate[...])
    up_val = dot(ffn_in[...], up[...])
    gate_sig = jax.nn.sigmoid(gate_val)
    silu_gate = gate_val * gate_sig
    ffn_hidden = (silu_gate * up_val).astype(bf16)
    ffn_out[...] += dot(ffn_hidden, down[...])
    grad_down[...] = dot(ffn_hidden.T, grad_ffn[...]).astype(bf16)
    grad_hidden_ffn = dot_nt(grad_ffn[...], down[...])
    grad_up_val = (grad_hidden_ffn * silu_gate).astype(bf16)
    grad_gate_val = (
        grad_hidden_ffn * up_val * gate_sig * (1.0 + gate_val * (1.0 - gate_sig))
    ).astype(bf16)
    grad_gate[...] = dot(ffn_in_t[...], grad_gate_val).astype(bf16)
    grad_up[...] = dot(ffn_in_t[...], grad_up_val).astype(bf16)
    grad_in[...] += dot_nt(grad_gate_val, gate[...]) + dot_nt(grad_up_val, up[...])

    @pl.when(pl.program_id(0) == pl.num_programs(0) - 1)
    def _():
        def window_sums(at, values):
            for w in range(windows):
                total = jnp.sum(values[w * rows : (w + 1) * rows], axis=0, keepdims=True)
                sums[pl.ds(at * windows + w, 1), :] = total

        state = hidden_state[...]
        sig_f = jax.nn.sigmoid(part(5))
        grad_layer = cotangent[...].astype(f32)
        layer_out[...] = (state + sig_f * ffn_out[...]).astype(bf16)
        window_sums(3, grad_layer * ffn_out[...] * sig_f * (1.0 - sig_f))
        normed, inv_std = norm_rows(state)
        window_sums(1, grad_in[...])
        window_sums(2, grad_in[...] * normed)
        back = norm_back(grad_in[...] * (1.0 + part(4)), normed, inv_std)
        grad_hidden = grad_layer + back
        grad_hidden_out[...] = grad_hidden
        sig_a = jax.nn.sigmoid(part(2))
        window_sums(0, grad_hidden * attn_out[...] * sig_a * (1.0 - sig_a))
        grad_attn_out = (sig_a * grad_hidden).astype(bf16)
        grad_out[...] = dot(mixed[...].T, grad_attn_out).astype(bf16)
        grad_mixed[...] = dot_nt(grad_attn_out, out_weight[...]).astype(bf16)


def feed_forward(modulation, tokens, cotangent, mixed, out_weight, gate, up, down, windows):
    total_rows, width = tokens.shape
    hidden = gate.shape[1]
    blocks = 3
    size = hidden // blocks

    def whole(shape):
        return pl.BlockSpec(shape, lambda j: (0, 0))

    columns = pl.BlockSpec((width, size), lambda j: (0, j))
    lines = pl.BlockSpec((size, width), lambda j: (j, 0))
    row = (total_rows, width)
    return pl.pallas_call(
        functools.partial(feed_forward_kernel, windows),
        grid=(blocks,),
        in_specs=[whole(modulation.shape)]
        + [whole(row)] * 3
        + [whole(out_weight.shape), columns, columns, lines],
        out_specs=[whole(row)] * 3
        + [whole(out_weight.shape), whole((4 * windows, width)), columns, columns, lines],
        out_shape=[
            jax.ShapeDtypeStruct(row, bf16),
            jax.ShapeDtypeStruct(row, f32),
            jax.ShapeDtypeStruct(row, bf16),
            jax.ShapeDtypeStruct(out_weight.shape, bf16),
            jax.ShapeDtypeStruct((4 * windows, width), f32),
            jax.ShapeDtypeStruct(gate.shape, bf16),
            jax.ShapeDtypeStruct(up.shape, bf16),
            jax.ShapeDtypeStruct(down.shape, bf16),
        ],
        scratch_shapes=[
            pltpu.VMEM(row, f32),
            pltpu.VMEM(row, f32),
            pltpu.VMEM(row, bf16),
            pltpu.VMEM((width, total_rows), bf16),
            pltpu.VMEM(row, bf16),
            pltpu.VMEM(row, f32),
            pltpu.VMEM(row, f32),
        ],
        compiler_params=pltpu.CompilerParams(vmem_limit_bytes=63 * 2**20),
        cost_estimate=pl.CostEstimate(
            flops=18 * total_rows * width * hidden, bytes_accessed=40 * 2**20, transcendentals=0
        ),
        name="ffn",
    )(modulation, tokens, cotangent, mixed, out_weight, gate, up, down)


def three_parts(values):
    parts = []
    for _ in range(3):
        part = lax.reduce_precision(values, 8, 7)
        parts.append(part.astype(bf16))
        values = values - part
    return parts


def per_device(
    tokens,
    cotangent,
    noise_times,
    cath_ids,
    chain_start,
    distance_bins,
    class_table,
    ada_weight,
    qkv_weight,
    out_weight,
    pair_table,
    pair_weight,
    gate_weight,
    up_weight,
    down_weight,
):
    windows, row_count, width = tokens.shape
    length = distance_bins.shape[2]
    head_count = pair_weight.shape[1]
    head_size = width // head_count
    table_rows = pair_table.shape[0]
    bin_count = table_rows // 2
    classes = class_table.shape[0]
    total_rows = windows * row_count
    win_count = lax.axis_size("win")
    seq_count = lax.axis_size("seq")
    devices = win_count * seq_count
    class_onehot = (cath_ids[:, None] == jnp.arange(classes, dtype=jnp.int32)[None, :]).astype(f32)
    pre_cond = jnp.dot(
        class_onehot, class_table.astype(f32), precision=highest
    ) + time_embed(noise_times, width)
    cond_sig = jax.nn.sigmoid(pre_cond)
    condition = pre_cond * cond_sig
    cond_parts = jnp.concatenate(
        [jnp.pad(part, ((0, 8 - windows), (0, 0))) for part in three_parts(condition)], axis=0
    )
    modulation, queries, keys_values, attn_in_all, attn_mixed, probs, pair_index = forward(
        chain_start,
        tokens,
        cond_parts,
        pair_table,
        pair_weight.T,
        ada_weight,
        qkv_weight,
        distance_bins,
        head_size,
    )
    flat_tokens = tokens.reshape(total_rows, width)
    layer_out, grad_hidden, grad_mixed, grad_out, sums, grad_gate, grad_up, grad_down = feed_forward(
        modulation,
        flat_tokens,
        cotangent.reshape(total_rows, width),
        attn_mixed,
        out_weight,
        gate_weight,
        up_weight,
        down_weight,
        windows,
    )
    scale_attn = modulation[:windows, width : 2 * width]
    early = [
        sums,
        pre_cond / seq_count,
        jnp.pad(class_onehot, ((0, 0), (0, width - classes))) / seq_count,
    ]
    owned_gate, owned_up, owned_down, owned_out, owned_q, owned_kv, grad_tokens, small = backward(
        [grad_gate, grad_up, grad_down, grad_out],
        [
            queries,
            keys_values,
            probs,
            grad_mixed,
            attn_in_all,
            qkv_weight,
            pair_index,
            flat_tokens,
            grad_hidden,
        ],
        1.0 + scale_attn,
        early,
        (windows, row_count, length, head_size),
        6,
        [False, True, False, True, True, True],
    )
    class_share = classes * width // devices
    flat_gate, flat_up, flat_down, flat_out, flat_qkv, grad_tokens, of_class, flat_ada, of_table, of_weight = tail(
        [owned_gate, owned_up, owned_down, owned_out, owned_q, owned_kv],
        grad_tokens,
        small,
        ada_weight,
        pair_table,
        pair_weight.T,
        windows,
        class_share,
    )
    return (
        layer_out.reshape(windows, row_count, width),
        grad_tokens.reshape(windows, row_count, width),
        of_class.reshape(-1),
        flat_ada.reshape(-1),
        flat_qkv.reshape(-1),
        flat_out.reshape(-1),
        of_table.reshape(-1),
        of_weight.reshape(-1),
        flat_gate.reshape(-1),
        flat_up.reshape(-1),
        flat_down.reshape(-1),
    )


def solution(mesh):
    rows = P("win", "seq", None)
    flat = P(("win", "seq"))
    placed = (rows, rows, P("win"), P("win"), P("win"), rows) + (P(),) * 9
    return jax.shard_map(
        per_device, mesh=mesh, in_specs=placed, out_specs=(rows, rows) + (flat,) * 9, check_vma=False
    )
```
